32 devices in a mesh: exp: 8 (over z, x), head: 4 (over y, core).
Axes of the slice: x: 2, y: 2, z: 4, core: 2. Of those that a mesh axis runs over, the one named last changes fastest.
Arguments:
- queries: bfloat16 [1024, 4096], P('exp', 'head')
- keys: bfloat16 [1024, 1024], P('exp', 'head')
- values: bfloat16 [1024, 1024], P('exp', 'head')
- w_in: bfloat16 [8, 4096, 2, 768], P('exp', 'head'), may hold values from -0.09375 to 0.09375
- w_out: bfloat16 [8, 768, 4096], P('exp', None, 'head'), may hold values from -0.21875 to 0.21875
- routes: int32 [1024, 6], P('exp'), may hold values from 0 to 7, as said below
- route_weights: float32 [1024, 6], P('exp'), may hold values from 0.05 to 0.45
- grad_out: bfloat16 [1024, 4096], P('exp', 'head'), may hold values from -6 to 6
Outputs:
- output: bfloat16 [1024, 4096], P('exp', 'head')
- grad_attended: bfloat16 [1024, 4096], P('exp', 'head')
The draws below stay inside these ranges and needn't reach their ends.
Inputs may be any that keep to these rules, and one draw needn't show every extreme that they name: `routes`: each row names 6 different experts. In each aligned block of 128 rows (the rows of one index of exp) no expert is named more than 112 times.
All inputs are finite; a program needn't handle non-finite values.
Results may differ from the reference program's by a relative error of at most 0.017.
Values may be sent and summed in bfloat16 or wider, within the bound.
A program may use at most 128 MiB of HBM per device.

```python
import jax
import jax.numpy as jnp
from jax import lax

D = 4096
QUERY_HEADS = 32
KEY_VALUE_HEADS = 8
HEAD_WIDTH = 128
FF = 768
TOP = 6
TOK_DEV = 128
CACHE_PER_INDEX = 128
EXPERTS = 8
WINDOW_TOKENS = 1024
CACHE_POSITIONS = 1024
MEAN_LOAD = 96
CAP = 112


def drawn_keys(key):
    return 1.5 * jax.random.truncated_normal(jax.random.fold_in(key, 11), -4.0, 4.0, (CACHE_POSITIONS, KEY_VALUE_HEADS * HEAD_WIDTH), jnp.float32)


def draw_keys(key, part):
    starting_key_rows = drawn_keys(key)
    return starting_key_rows.astype(jnp.bfloat16)


def draw_queries(key, part):
    unrouted = 1.5 * jax.random.truncated_normal(jax.random.fold_in(key, 13), -4.0, 4.0, (WINDOW_TOKENS, QUERY_HEADS * HEAD_WIDTH), jnp.float32)
    return unrouted.astype(jnp.bfloat16)


def draw_values(key, part):
    unrouted = jax.random.truncated_normal(jax.random.fold_in(key, 17), -4.0, 4.0, (CACHE_POSITIONS, KEY_VALUE_HEADS * HEAD_WIDTH), jnp.float32)
    return unrouted.astype(jnp.bfloat16)


def draw_routes(key, part):
    block_total = WINDOW_TOKENS // TOK_DEV
    spread = CAP - MEAN_LOAD
    order = jax.random.permutation(jax.random.fold_in(key, 21), EXPERTS)

    def one_block(block_key):
        offsets = jax.random.randint(jax.random.fold_in(block_key, 1), (EXPERTS // 2,), 0, spread + 1)
        offsets = offsets.at[0].set(spread)
        signed = jnp.stack([offsets, -offsets], axis=1).reshape(EXPERTS)
        counts = jnp.zeros((EXPERTS,), jnp.int32).at[order].set(MEAN_LOAD + signed)
        ends = jnp.cumsum(counts)
        positions = jnp.arange(TOK_DEV * TOP, dtype=jnp.int32)
        listing = jnp.sum((ends[None, :] <= positions[:, None]).astype(jnp.int32), axis=1)
        table = listing.reshape(TOP, TOK_DEV).T
        ranks = jax.random.randint(jax.random.fold_in(block_key, 3), (TOK_DEV, TOP), 0, 1000) * TOP
        ranks = ranks + jnp.arange(TOP, dtype=jnp.int32)[None, :]
        column_order = jnp.argsort(ranks, axis=1, stable=True)
        table = jnp.take_along_axis(table, column_order, axis=1)
        shuffle = jax.random.permutation(jax.random.fold_in(block_key, 2), TOK_DEV)
        return table[shuffle]
    block_keys = jax.random.split(jax.random.fold_in(key, 22), block_total)
    return jax.vmap(one_block)(block_keys).reshape(WINDOW_TOKENS, TOP).astype(jnp.int32)


def block_levels(own_key, dims, cuts, least, top_value):
    loudness, own = 1.0, jax.random.fold_in(own_key, 6)
    for dim, shards_of in cuts:
        draws = jnp.exp(jax.random.uniform(jax.random.fold_in(own, dim), (shards_of,), jnp.float32, least / len(cuts), top_value / len(cuts)))
        loudness = loudness * jnp.repeat(draws, dims[dim] // shards_of).reshape([-1 if axis == dim else 1 for axis in range(len(dims))])
    return loudness


def normal_values(rng, shape, width, bound, cuts=(), kind=jnp.bfloat16):
    result = jax.random.normal(rng, shape, jnp.float32) * width
    if len(cuts) > 0:
        result = block_levels(rng, shape, cuts, -0.22, 0.18) * result
    return jnp.clip(result, min=-bound, max=bound).astype(kind)


def setup_inputs(seed: int = 0) -> dict:
    key_of = jax.random.split(jax.random.key(seed), 9)
    return {
        "queries": draw_queries(jax.random.fold_in(key_of[8], 71), 0),
        "keys": draw_keys(jax.random.fold_in(key_of[8], 71), 0),
        "values": draw_values(jax.random.fold_in(key_of[8], 71), 0),
        "w_in": normal_values(key_of[3], (EXPERTS, D, 2, FF), D ** -0.5, 0.09375, ((0, 8), (1, 4))),
        "w_out": normal_values(key_of[4], (EXPERTS, FF, D), FF ** -0.5, 0.21875, ((0, 8), (2, 4))),
        "routes": draw_routes(jax.random.fold_in(key_of[8], 71), 0),
        "route_weights": jnp.clip(0.05 + 0.39999999 * jax.random.uniform(key_of[6], (WINDOW_TOKENS, TOP), jnp.float32) ** block_levels(key_of[6], (WINDOW_TOKENS, TOP), ((0, 8),), -0.2, 0.2), 0.05, 0.45),
        "grad_out": normal_values(key_of[7], (WINDOW_TOKENS, D), 1.0, 6.0, ((0, 8), (1, 4))),
    }


norm_eps = 1e-05
hidden_logits = -1e+30

def settle(tensor):
    return lax.optimization_barrier(tensor.astype(jnp.bfloat16)).astype(jnp.float32)

def attend(queries, keys, values):
    grouping_width = QUERY_HEADS // KEY_VALUE_HEADS
    count_of_blocks = CACHE_POSITIONS // CACHE_PER_INDEX
    heads_of_queries = queries.astype(jnp.float32).reshape(WINDOW_TOKENS, KEY_VALUE_HEADS, grouping_width, HEAD_WIDTH)
    blocked_keys = keys.astype(jnp.float32).reshape(count_of_blocks, CACHE_PER_INDEX, KEY_VALUE_HEADS, HEAD_WIDTH)
    blocked_values = values.astype(jnp.float32).reshape(count_of_blocks, CACHE_PER_INDEX, KEY_VALUE_HEADS, HEAD_WIDTH)
    query_pos = CACHE_POSITIONS - WINDOW_TOKENS + jnp.arange(WINDOW_TOKENS, dtype=jnp.int32)

    def one_block(running, element):
        top_now, total_now, sums_now = running
        key_block, value_block, block_index = element
        key_pos = block_index * CACHE_PER_INDEX + jnp.arange(CACHE_PER_INDEX, dtype=jnp.int32)
        visible = (key_pos[None, :] <= query_pos[:, None])[:, None, None, :]
        scores = jnp.einsum('tgid,jgd->tgij', heads_of_queries, key_block) * HEAD_WIDTH ** (-0.5)
        scores = jnp.where(visible, scores, hidden_logits)
        block_top = settle(lax.optimization_barrier(jnp.max(scores, axis=-1)))
        weights = jnp.where(visible, jnp.exp(scores - block_top[..., None]), 0.0)
        block_total = settle(lax.optimization_barrier(jnp.sum(weights, axis=-1)))
        block_sum = settle(jnp.einsum('tgij,jgd->tgid', settle(weights), value_block))
        new_top = jnp.maximum(top_now, block_top)
        old_factor = jnp.exp(top_now - new_top)
        new_factor = jnp.exp(block_top - new_top)
        total_next = total_now * old_factor + block_total * new_factor
        sums_next = sums_now * old_factor[..., None] + block_sum * new_factor[..., None]
        return ((new_top, total_next, sums_next), None)
    beginning = (jnp.full((WINDOW_TOKENS, KEY_VALUE_HEADS, grouping_width), hidden_logits, jnp.float32), jnp.zeros((WINDOW_TOKENS, KEY_VALUE_HEADS, grouping_width), jnp.float32), jnp.zeros((WINDOW_TOKENS, KEY_VALUE_HEADS, grouping_width, HEAD_WIDTH), jnp.float32))
    running, ignored = lax.scan(one_block, beginning, (blocked_keys, blocked_values, jnp.arange(count_of_blocks, dtype=jnp.int32)))
    return (running[2] / running[1][..., None]).reshape(WINDOW_TOKENS, QUERY_HEADS * HEAD_WIDTH).astype(jnp.bfloat16)

def expert_pass(element):
    row_block, grad_block, w_first, w_second = element
    row_float = row_block.astype(jnp.float32)
    squares = lax.optimization_barrier(jnp.sum(row_float * row_float, axis=1))
    norm_scale = lax.rsqrt(squares / D + norm_eps)[:, None]
    raw_sums = jnp.dot(row_block, w_first.reshape(D, 2 * FF), preferred_element_type=jnp.float32).reshape(-1, 2, FF)
    gate_value = raw_sums[:, 0] * norm_scale
    up_value = raw_sums[:, 1] * norm_scale
    gate_sigmoid = jax.nn.sigmoid(gate_value)
    gate_silu = gate_value * gate_sigmoid
    hidden_act = (gate_silu * up_value).astype(jnp.bfloat16)
    out_rows = jnp.dot(hidden_act, w_second, preferred_element_type=jnp.float32).astype(jnp.bfloat16)
    back_sums = jnp.dot(grad_block, jnp.transpose(w_second), preferred_element_type=jnp.float32)
    grad_gate = back_sums * up_value * gate_sigmoid * (1.0 + gate_value * (1.0 - gate_sigmoid))
    grad_up = back_sums * gate_silu
    grad_hidden = jnp.stack([grad_gate, grad_up], axis=1).astype(jnp.bfloat16)
    grad_normed = jnp.dot(grad_hidden.reshape(-1, 2 * FF), jnp.transpose(w_first.reshape(D, 2 * FF)), preferred_element_type=jnp.float32)
    inner_sum = lax.optimization_barrier(jnp.sum(grad_hidden.astype(jnp.float32) * jnp.stack([gate_value, up_value], axis=1), axis=(1, 2)))
    grad_rows = norm_scale * grad_normed - row_float * (norm_scale * norm_scale / D) * inner_sum[:, None]
    return (out_rows, grad_rows.astype(jnp.bfloat16))

def reference(queries, keys, values, w_in, w_out, routes, route_weights, grad_out):
    attended = attend(queries, keys, values)
    shard_count = WINDOW_TOKENS // TOK_DEV
    shard_routes = routes.reshape(shard_count, TOK_DEV * TOP)
    expert_hits = (shard_routes[:, :, None] == jnp.arange(EXPERTS, dtype=jnp.int32)[None, None, :]).astype(jnp.int32)
    earlier = jnp.cumsum(expert_hits, axis=1) - expert_hits
    slot_index = lax.optimization_barrier(jnp.sum(earlier * expert_hits, axis=2)).astype(jnp.int32)
    row_of = (jnp.arange(shard_count, dtype=jnp.int32)[:, None] * CAP + slot_index).reshape(-1).astype(jnp.int32)
    expert_of = shard_routes.reshape(-1).astype(jnp.int32)
    token_of = jnp.repeat(jnp.arange(WINDOW_TOKENS, dtype=jnp.int32), TOP)
    slot_rows = shard_count * CAP
    row_table = jnp.zeros((EXPERTS, slot_rows, D), jnp.bfloat16).at[expert_of, row_of].set(attended[token_of])
    grad_table = jnp.zeros((EXPERTS, slot_rows, D), jnp.bfloat16).at[expert_of, row_of].set(grad_out[token_of])
    out_table, grad_rows = lax.map(expert_pass, (row_table, grad_table, w_in, w_out))
    picked_out = out_table[expert_of, row_of].astype(jnp.float32).reshape(WINDOW_TOKENS, TOP, D)
    picked_grad = grad_rows[expert_of, row_of].astype(jnp.float32).reshape(WINDOW_TOKENS, TOP, D)
    output = (attended.astype(jnp.float32) + lax.optimization_barrier(jnp.sum(route_weights[:, :, None] * picked_out, axis=1))).astype(jnp.bfloat16)
    grad_attended = (grad_out.astype(jnp.float32) + lax.optimization_barrier(jnp.sum(route_weights[:, :, None] * picked_grad, axis=1))).astype(jnp.bfloat16)
    return (output, grad_attended)
```

```python
import jax
import jax.numpy as jnp
from jax import lax
from jax.experimental import pallas as pl
from jax.experimental.pallas import tpu as pltpu
from jax.sharding import PartitionSpec as P

D = 4096
HEAD_WIDTH = 128
TOP = 6


norm_eps = 1e-05
hidden_logits = -1e30


def block_partial(query_rows, query_pos, rows_of_keys, value_rows, key_pos):
    row_count = query_rows.shape[0]
    count_of_blocks = rows_of_keys.shape[0]
    kv_heads = rows_of_keys.shape[2] // HEAD_WIDTH
    grouping_width = query_rows.shape[1] // HEAD_WIDTH // kv_heads
    heads_of_queries = query_rows.reshape(row_count, kv_heads, grouping_width, HEAD_WIDTH)
    key_heads = rows_of_keys.reshape(count_of_blocks, -1, kv_heads, HEAD_WIDTH)
    value_heads = value_rows.reshape(count_of_blocks, -1, kv_heads, HEAD_WIDTH)
    visible = (key_pos[:, None, :] <= query_pos[None, :, None])[:, :, None, None, :]
    scores = jnp.einsum(
        "tgid,bjgd->btgij", heads_of_queries, key_heads, preferred_element_type=jnp.float32
    ) * HEAD_WIDTH ** (-0.5)
    scores = jnp.where(visible, scores, hidden_logits)
    best_score = jnp.max(scores, axis=-1).astype(jnp.bfloat16)
    weights = jnp.where(visible, jnp.exp(scores - best_score.astype(jnp.float32)[..., None]), 0.0)
    weight_total = jnp.sum(weights, axis=-1).astype(jnp.bfloat16)
    weighted_sum = jnp.einsum(
        "btgij,bjgd->btgid",
        weights.astype(jnp.bfloat16),
        value_heads,
        preferred_element_type=jnp.float32,
    ).astype(jnp.bfloat16)
    head_count = kv_heads * grouping_width
    return (
        best_score.reshape(count_of_blocks, row_count, head_count),
        weight_total.reshape(count_of_blocks, row_count, head_count),
        weighted_sum.reshape(count_of_blocks, row_count, head_count * HEAD_WIDTH),
    )


def fold_partials(running, best_score, weight_total, weighted_sum):
    top_now, total_now, sums_now = running
    best_value = best_score.astype(jnp.float32)
    new_top = jnp.maximum(top_now, jnp.max(best_value, axis=0))
    old_factor = jnp.exp(top_now - new_top)
    block_factor = jnp.exp(best_value - new_top[None])
    total_next = total_now * old_factor + jnp.sum(
        weight_total.astype(jnp.float32) * block_factor, axis=0
    )
    spread_sums = weighted_sum.reshape(
        weighted_sum.shape[0], sums_now.shape[0], sums_now.shape[1], HEAD_WIDTH
    )
    sums_next = sums_now * old_factor[..., None] + jnp.sum(
        spread_sums.astype(jnp.float32) * block_factor[..., None], axis=0
    )
    return (new_top, total_next, sums_next)


def per_device(queries, keys, values, w_in, w_out, routes, route_weights, grad_out):
    exp_count = lax.axis_size("exp")
    exp_index = lax.axis_index("exp")
    head_devices = lax.axis_size("head")
    token_count = queries.shape[0]
    query_width = queries.shape[1]
    head_count = query_width // HEAD_WIDTH
    cache_rows = keys.shape[0]
    window = token_count * exp_count
    offset = cache_rows * exp_count - window
    beginning = (
        jnp.full((token_count, head_count), hidden_logits, jnp.float32),
        jnp.zeros((token_count, head_count), jnp.float32),
        jnp.zeros((token_count, head_count, HEAD_WIDTH), jnp.float32),
    )
    own_pos = offset + exp_index * token_count + jnp.arange(token_count, dtype=jnp.int32)
    key_piece = lax.all_gather(keys, "exp", axis=0, tiled=True)
    value_piece = lax.all_gather(values, "exp", axis=0, tiled=True)
    piece_blocks = key_piece.shape[0] // cache_rows
    key_split = key_piece.reshape(piece_blocks, cache_rows, -1)
    value_split = value_piece.reshape(piece_blocks, cache_rows, -1)
    pos_split = jnp.arange(key_piece.shape[0], dtype=jnp.int32).reshape(piece_blocks, cache_rows)

    def one_block(state, element):
        key_block, value_block, pos_block = element
        block_parts = block_partial(
            queries, own_pos, key_block[None], value_block[None], pos_block[None]
        )
        return (fold_partials(state, block_parts[0], block_parts[1], block_parts[2]), None)

    state, ignored = lax.scan(one_block, beginning, (key_split, value_split, pos_split))
    attended = (
        (state[2] / state[1][..., None]).reshape(token_count, query_width).astype(jnp.bfloat16)
    )
    row_width = attended.shape[1]
    experts_all = w_in.shape[0] * exp_count
    mean_load = TOP * token_count // experts_all
    capacity = mean_load + mean_load // 6
    places = experts_all * capacity
    flat_routes = routes.reshape(-1)
    expert_hits = (
        flat_routes[:, None] == jnp.arange(experts_all, dtype=jnp.int32)[None, :]
    ).astype(jnp.bfloat16)
    before = jnp.tri(flat_routes.shape[0], k=-1, dtype=jnp.bfloat16)
    earlier = jnp.dot(before, expert_hits, preferred_element_type=jnp.float32)
    slot_index = jnp.sum(earlier * expert_hits.astype(jnp.float32), axis=1).astype(jnp.int32)
    place_index = flat_routes * capacity + slot_index
    chosen = (place_index[:, None] == jnp.arange(places, dtype=jnp.int32)[None, :]).astype(
        jnp.bfloat16
    )
    picker = jnp.sum(chosen.reshape(token_count, TOP, places), axis=1)
    contract_rows = (((0,), (0,)), ((), ()))
    send_rows = lax.dot_general(picker, attended, contract_rows, preferred_element_type=jnp.float32)
    send_rows = send_rows.astype(jnp.bfloat16).reshape(experts_all, capacity, row_width)
    send_grads = lax.dot_general(
        picker, grad_out, contract_rows, preferred_element_type=jnp.float32
    )
    send_grads = send_grads.astype(jnp.bfloat16).reshape(experts_all, capacity, row_width)
    w_first = w_in[0]
    w_second = w_out[0]
    rows_in = lax.all_to_all(send_rows, "exp", split_axis=0, concat_axis=0, tiled=True)
    grads_in = lax.all_to_all(send_grads, "exp", split_axis=0, concat_axis=0, tiled=True)
    lead_count, item_count, width_in = rows_in.shape
    row_total = lead_count * item_count
    row_block = rows_in.reshape(row_total, width_in)
    grad_block = grads_in.reshape(row_total, width_in)
    row_float = row_block.astype(jnp.float32)
    raw_sums = jnp.einsum("rd,dkf->rkf", row_block, w_first, preferred_element_type=jnp.float32)
    back_sums = lax.dot_general(
        grad_block, w_second, (((1,), (1,)), ((), ())), preferred_element_type=jnp.float32
    )
    squares = jnp.sum(row_float * row_float, axis=1)
    square_tile = jnp.broadcast_to(squares[:, None, None], (row_total, 1, head_devices))
    raw_part = lax.psum_scatter(raw_sums, "head", scatter_dimension=2, tiled=True)
    back_part = lax.psum_scatter(back_sums[:, None, :], "head", scatter_dimension=2, tiled=True)
    square_part = lax.psum_scatter(square_tile, "head", scatter_dimension=2, tiled=True)
    norm_scale = lax.rsqrt(square_part[:, 0] / D + norm_eps)
    gate_value = raw_part[:, 0] * norm_scale
    up_value = raw_part[:, 1] * norm_scale
    back_value = back_part[:, 0]
    gate_sigmoid = jax.nn.sigmoid(gate_value)
    gate_silu = gate_value * gate_sigmoid
    act_part = (gate_silu * up_value).astype(jnp.bfloat16)
    grad_gate = back_value * up_value * gate_sigmoid * (1.0 + gate_value * (1.0 - gate_sigmoid))
    grad_up = back_value * gate_silu
    grad_part = jnp.stack([grad_gate, grad_up], axis=1).astype(jnp.bfloat16)
    inner_part = jnp.sum(
        grad_part.astype(jnp.float32) * jnp.stack([gate_value, up_value], axis=1), axis=(1, 2)
    )
    act_whole = lax.all_gather(act_part[:, None, :], "head", axis=2, tiled=True)
    grad_hidden = lax.all_gather(grad_part, "head", axis=2, tiled=True)
    hidden_act = act_whole[:, 0]
    inner_sum = lax.psum(inner_part, "head")
    out_rows = jnp.dot(hidden_act, w_second, preferred_element_type=jnp.float32).astype(
        jnp.bfloat16
    )
    grad_normed = jnp.einsum(
        "rkf,dkf->rd", grad_hidden, w_first, preferred_element_type=jnp.float32
    )
    grad_rows = (
        norm_scale * grad_normed - row_float * (norm_scale * norm_scale / D) * inner_sum[:, None]
    )
    expert_out = out_rows.reshape(lead_count, item_count, width_in)
    expert_grad = grad_rows.astype(jnp.bfloat16).reshape(lead_count, item_count, width_in)
    came_out, came_grad = (
        lax.all_to_all(expert_out, "exp", split_axis=0, concat_axis=0, tiled=True),
        lax.all_to_all(expert_grad, "exp", split_axis=0, concat_axis=0, tiled=True),
    )
    picked_out = came_out.reshape(places, row_width)[place_index].reshape(
        token_count, TOP, row_width
    )
    picked_grad = came_grad.reshape(places, row_width)[place_index].reshape(
        token_count, TOP, row_width
    )
    output = attended.astype(jnp.float32) + jnp.sum(
        route_weights[:, :, None] * picked_out.astype(jnp.float32), axis=1
    )
    grad_attended = grad_out.astype(jnp.float32) + jnp.sum(
        route_weights[:, :, None] * picked_grad.astype(jnp.float32), axis=1
    )
    return (output.astype(jnp.bfloat16), grad_attended.astype(jnp.bfloat16))


LANES = 128
EXACT = (((1,), (1,)), ((), ()))


def three_parts(value):
    high = value.astype(jnp.bfloat16)
    rest = value - high.astype(jnp.float32)
    middle = rest.astype(jnp.bfloat16)
    low = (rest - middle.astype(jnp.float32)).astype(jnp.bfloat16)
    return high, middle, low


def ring_place(index, count):
    outer, inner = index // 2, index % 2
    return outer + inner * (count - 1 - 2 * outer)


def ring_index(place, count):
    inner = place // (count // 2)
    return 2 * (place + inner * (count - 1 - 2 * place)) + inner


def ring_lanes(count):
    reach = count // 2
    return ((0, 0, reach), (1, 1, reach), (0, 1, reach - 1), (1, 0, reach - 1))


def slot_of(distance, count):
    if distance == 0:
        return 0
    if abs(distance) == count // 2:
        return count - 1
    return 2 * distance - 1 if distance > 0 else -2 * distance


def wide(value, width):
    return jnp.concatenate([value] * (width // value.shape[1]), axis=1)


def fused_kernel(
    count,
    q_ref,
    k_ref,
    v_ref,
    w_in_ref,
    w_out_ref,
    routes_ref,
    share_ref,
    grad_ref,
    output_ref,
    grad_out_ref,
    w_pairs,
    w_up,
    w_down,
    k_all,
    v_all,
    grads,
    rows,
    tables,
    squares,
    head_squares,
    gains,
    scales,
    sum_raw,
    sum_back,
    near_raw,
    near_back,
    near_raw_in,
    near_back_in,
    far_raw,
    far_back,
    far_raw_in,
    far_back_in,
    act,
    act_in,
    parts,
    held,
    load_sem,
    gather_send,
    gather_recv,
    scatter_send,
    scatter_recv,
    meta_send,
    meta_recv,
    head_send,
    head_recv,
    pair_send,
    pair_recv,
):
    reach = count // 2
    tokens, width = q_ref.shape
    cached, kv_width = k_ref.shape
    half_hidden = w_down.shape[1]
    experts = tables.shape[1]
    me = lax.axis_index("exp")
    place = ring_place(me, count)
    head = lax.axis_index("head")
    core = head % 2
    mate = head + 1 - 2 * core
    across = (head + 2) % 4
    corner = 3 - head
    others = (ring_index((place + 1) % count, count), ring_index((place + count - 1) % count, count))
    distances = [0] + [d for s in range(1, reach) for d in (s, -s)] + [reach]
    groups = [(0, 1)] + [(2 * s - 1, 2) for s in range(1, reach)] + [(count - 1, 1)]
    started = []

    def begin(copy):
        copy.start()
        started.append(copy)
        return copy

    def remote(source, target, send_sem, recv_sem, where):
        return pltpu.make_async_remote_copy(
            src_ref=source,
            dst_ref=target,
            send_sem=send_sem,
            recv_sem=recv_sem,
            device_id=where,
            device_id_type=pl.DeviceIdType.MESH,
        )

    load_in = pltpu.make_async_copy(w_in_ref.at[0], w_pairs, load_sem.at[0])
    load_out = pltpu.make_async_copy(w_out_ref, w_down, load_sem.at[1])
    load_in.start()
    load_out.start()

    barrier = pltpu.get_barrier_semaphore()
    for other in (mate, across, corner):
        pl.semaphore_signal(
            barrier, inc=1, device_id={"head": other}, device_id_type=pl.DeviceIdType.MESH
        )
    for distance in distances[1:]:
        other = ring_index((place + distance + count) % count, count)
        pl.semaphore_signal(
            barrier, inc=1, device_id={"exp": other}, device_id_type=pl.DeviceIdType.MESH
        )
    pl.semaphore_wait(barrier, 3 + count - 1)

    half = tokens // 2
    gathers = {}

    def gather_ref(kind, slot, part):
        if kind == 0:
            store = v_all if part else k_all
            if slot == 0:
                return v_ref if part else k_ref
            return store.at[pl.ds(slot * cached, cached)]
        if kind == 1 and slot == 0:
            return grad_ref.at[pl.ds(part * half, half)]
        store = grads if kind == 1 else rows
        return store.at[pl.ds(slot * tokens + part * half, half)]

    def advance(kind, step):
        for way, part, steps in ring_lanes(count):
            if 1 <= step <= steps:
                gathers[kind, way, part, step - 1].wait_recv()
            if step < steps:
                sign = -1 if way == 0 else 1
                gathers[kind, way, part, step] = begin(
                    remote(
                        gather_ref(kind, slot_of(sign * step, count), part),
                        gather_ref(kind, slot_of(sign * (step + 1), count), part),
                        gather_send.at[kind, way, part, step],
                        gather_recv.at[kind, way, part, step],
                        {"exp": others[way]},
                    )
                )

    def broadcast(kind, store):
        copies = []
        for distance in distances[1:]:
            there = slot_of(-distance, count)
            other = ring_index((place + distance + count) % count, count)
            copies.append(
                begin(
                    remote(
                        store.at[0],
                        store.at[there],
                        meta_send.at[kind, there],
                        meta_recv.at[kind, there],
                        {"exp": other},
                    )
                )
            )
        return copies

    advance(0, 0)
    advance(1, 0)
    expert_row = lax.broadcasted_iota(jnp.int32, (experts, tokens), 0)
    table = jnp.zeros((experts, tokens), jnp.float32)
    for k in range(routes_ref.shape[0]):
        table = table + jnp.where(expert_row == routes_ref[k : k + 1, :], share_ref[k : k + 1, :], 0.0)
    tables[0] = table
    table_copies = broadcast(0, tables)

    k_all[0:cached, :] = k_ref[...]
    v_all[0:cached, :] = v_ref[...]

    load_in.wait()
    chunk = LANES
    to = lax.broadcasted_iota(jnp.int32, (2 * chunk, 2 * chunk), 0)
    source = lax.broadcasted_iota(jnp.int32, (2 * chunk, 2 * chunk), 1)
    picks = (source == jnp.where(to < chunk, 2 * to, 2 * to - 2 * chunk + 1)).astype(jnp.bfloat16)

    def split_chunk(index, carry):
        span = pl.ds(pl.multiple_of(index * chunk, chunk), chunk)
        pairs = w_pairs[span].reshape(2 * chunk, 2 * half_hidden)
        apart = jnp.dot(picks, pairs, preferred_element_type=jnp.float32).astype(jnp.bfloat16)
        for side in range(2):
            cols = slice(side * half_hidden, (side + 1) * half_hidden)
            w_up[side, span, :half_hidden] = apart[:chunk, cols]
            w_up[side, span, half_hidden:] = apart[chunk:, cols]
        return carry

    lax.fori_loop(0, width // chunk, split_chunk, 0)
    load_out.wait()

    def span_of(group):
        slot, blocks = groups[group]
        return slice(slot * tokens, (slot + blocks) * tokens)

    pairs = {}

    def pair_begin(kind, group, source, target, other):
        span = span_of(group)
        pairs[kind, group] = begin(
            remote(
                source.at[span],
                target.at[span],
                pair_send.at[kind, group],
                pair_recv.at[kind, group],
                {"head": other},
            )
        )

    def back(group):
        span = span_of(group)
        block = grad_ref[...] if group == 0 else grads[span, :]
        near_back[span, :] = lax.dot_general(
            block, w_down[1 - core], EXACT, preferred_element_type=jnp.float32
        ).astype(jnp.bfloat16)
        pair_begin(0, group, near_back, near_back_in, mate)
        sum_back[span, :] = lax.dot_general(
            block, w_down[core], EXACT, preferred_element_type=jnp.float32
        )

    def raw(group):
        span = span_of(group)
        block = rows[span, :]
        near_raw[span, :] = jnp.dot(
            block, w_up[1 - core], preferred_element_type=jnp.float32
        ).astype(jnp.bfloat16)
        pair_begin(1, group, near_raw, near_raw_in, mate)
        sum_raw[span, :] = jnp.dot(block, w_up[core], preferred_element_type=jnp.float32)

    def far(kind, group):
        span = span_of(group)
        total, near_in = ((sum_back, near_back_in), (sum_raw, near_raw_in))[kind]
        out, target = ((far_back, far_back_in), (far_raw, far_raw_in))[kind]
        pairs[kind, group].wait_recv()
        both = total[span, :] + near_in[span, :].astype(jnp.float32)
        total[span, :] = both
        out[span, :] = both.astype(jnp.bfloat16)
        pair_begin(2 + kind, group, out, target, across)

    def attention():
        heads = width // HEAD_WIDTH
        together = heads // (kv_width // HEAD_WIDTH)
        every = count * cached
        column = lax.broadcasted_iota(jnp.int32, (1, every), 1)
        first = jnp.zeros((1, every), jnp.int32)
        for slot, distance in enumerate(distances):
            owner = ring_index((place + distance + count) % count, count)
            first = jnp.where(column // cached == slot, (owner - slot) * cached, first)
        row_pos = (
            count * (cached - tokens)
            + me * tokens
            + lax.broadcasted_iota(jnp.int32, (tokens, every), 0)
        )
        visible = jnp.broadcast_to(first + column, (tokens, every)) <= row_pos
        total = jnp.zeros((tokens, LANES), jnp.float32)
        for one in range(heads):
            cols = slice(one * HEAD_WIDTH, (one + 1) * HEAD_WIDTH)
            kv_cols = slice(one // together * HEAD_WIDTH, (one // together + 1) * HEAD_WIDTH)
            scores = lax.dot_general(
                q_ref[:, cols], k_all[:, kv_cols], EXACT, preferred_element_type=jnp.float32
            ) * HEAD_WIDTH ** (-0.5)
            scores = jnp.where(visible, scores, hidden_logits)
            best = jnp.max(scores, axis=1, keepdims=True)
            weights = jnp.exp(scores - best)
            weight_total = jnp.sum(weights, axis=1, keepdims=True)
            sums = jnp.dot(
                weights.astype(jnp.bfloat16), v_all[:, kv_cols], preferred_element_type=jnp.float32
            )
            mixed = (sums / weight_total).astype(jnp.bfloat16)
            rows[0:tokens, cols] = mixed
            mixed = mixed.astype(jnp.float32)
            total = total + mixed * mixed
        return total

    back(0)
    for step in range(1, reach):
        advance(0, step)
        advance(1, step)
        far(0, step - 1)
        back(step)
    advance(0, reach)
    square_cols = attention()
    advance(2, 0)
    square_cols = jnp.broadcast_to(
        jnp.sum(square_cols, axis=1, keepdims=True), (tokens, LANES)
    )
    head_squares[0] = jnp.transpose(square_cols)[: head_squares.shape[1]]
    square_copies = []
    for index, other in enumerate((mate, across, corner)):
        square_copies.append(
            begin(
                remote(
                    head_squares.at[0],
                    head_squares.at[index + 1],
                    head_send.at[index],
                    head_recv.at[index],
                    {"head": other},
                )
            )
        )
    advance(1, reach)
    far(0, reach - 1)
    back(reach)
    raw(0)
    for each in square_copies:
        each.wait_recv()
    squares[0] = (head_squares[0] + head_squares[1]) + (head_squares[2] + head_squares[3])
    square_copies = broadcast(1, squares)
    far(0, reach)
    far(1, 0)

    def columns_of(row):
        return jnp.transpose(jnp.broadcast_to(row, (LANES, tokens)))

    def fill_gains():
        for each in table_copies:
            each.wait_recv()
        for slot in range(count):
            row = jnp.sum(jnp.where(expert_row == me, tables[slot], 0.0), axis=0, keepdims=True)
            gains[slot * tokens : (slot + 1) * tokens, :] = columns_of(row)

    def fill_scales():
        for each in square_copies:
            each.wait_recv()
        for slot in range(count):
            row = lax.rsqrt(squares[slot][0:1, :] / D + norm_eps)
            scales[slot * tokens : (slot + 1) * tokens, :] = columns_of(row)

    def activate(group):
        slot, blocks = groups[group]
        pairs[2, group].wait_recv()
        pairs[3, group].wait_recv()
        step = 32
        lane = lax.broadcasted_iota(jnp.int32, (step, LANES), 1)

        def some_rows(index, carry):
            span = pl.ds(pl.multiple_of(slot * tokens + index * step, step), step)
            scale = scales[span, :]
            inner = jnp.zeros((step, LANES), jnp.float32)
            for start in range(0, half_hidden, LANES):
                cols = slice(start, start + LANES)
                up_cols = slice(half_hidden + start, half_hidden + start + LANES)
                down_cols = slice(2 * half_hidden + start, 2 * half_hidden + start + LANES)
                gate = (sum_raw[span, cols] + far_raw_in[span, cols].astype(jnp.float32)) * scale
                up = (sum_raw[span, up_cols] + far_raw_in[span, up_cols].astype(jnp.float32)) * scale
                back_value = sum_back[span, cols] + far_back_in[span, cols].astype(jnp.float32)
                sigmoid = jax.nn.sigmoid(gate)
                silu = gate * sigmoid
                grad_gate = back_value * up * sigmoid * (1.0 + gate * (1.0 - sigmoid))
                grad_gate = grad_gate.astype(jnp.bfloat16)
                grad_up = (back_value * silu).astype(jnp.bfloat16)
                act[span, cols] = (silu * up).astype(jnp.bfloat16)
                act[span, up_cols] = grad_gate
                act[span, down_cols] = grad_up
                inner = inner + (
                    grad_gate.astype(jnp.float32) * gate + grad_up.astype(jnp.float32) * up
                )
            high, middle, low = three_parts(
                jnp.broadcast_to(jnp.sum(inner, axis=1, keepdims=True), (step, LANES))
            )
            zero = jnp.zeros((step, LANES), jnp.float32)
            spread = jnp.where(lane == 0, high.astype(jnp.float32), zero)
            spread = jnp.where(lane == 1, middle.astype(jnp.float32), spread)
            spread = jnp.where(lane == 2, low.astype(jnp.float32), spread)
            act[span, 3 * half_hidden :] = spread.astype(jnp.bfloat16)
            return carry

        lax.fori_loop(0, blocks * tokens // step, some_rows, 0)
        pair_begin(4, group, act, act_in, mate)

    def finish(group):
        span = span_of(group)
        size = span.stop - span.start
        pairs[4, group].wait_recv()
        tail = slice(3 * half_hidden, 3 * half_hidden + LANES)
        inner = jnp.sum(
            act[span, tail].astype(jnp.float32) + act_in[span, tail].astype(jnp.float32),
            axis=1,
            keepdims=True,
        )
        tile = 256
        gain = gains[span, :]
        scale = scales[span, :]
        bent = wide(gain * scale * scale / D * inner, tile)
        gain = wide(gain, tile)
        scale = gain * wide(scale, tile)
        hidden = slice(0, half_hidden)
        slopes = slice(half_hidden, 3 * half_hidden)
        for start in range(0, width, tile):
            cols = slice(start, start + tile)
            out = jnp.dot(
                act[span, hidden], w_down[core, :, cols], preferred_element_type=jnp.float32
            ) + jnp.dot(
                act_in[span, hidden], w_down[1 - core, :, cols], preferred_element_type=jnp.float32
            )
            parts[span, cols] = (gain * out).astype(jnp.bfloat16)
            grad = lax.dot_general(
                act[span, slopes], w_up[core, cols, :], EXACT, preferred_element_type=jnp.float32
            ) + lax.dot_general(
                act_in[span, slopes],
                w_up[1 - core, cols, :],
                EXACT,
                preferred_element_type=jnp.float32,
            )
            grad = scale * grad - bent * rows[span, cols].astype(jnp.float32)
            parts[span, width + start : width + start + tile] = grad.astype(jnp.bfloat16)

    scatters = {}

    def scatter(step, which=(0, 1, 2, 3)):
        for number in which:
            way, part, steps = ring_lanes(count)[number]
            if step >= steps:
                continue
            sign = 1 if way == 0 else -1
            slot = slot_of(sign * (steps - step), count)
            block = parts.at[pl.ds(slot * tokens + part * half, half)]
            if step > 0:
                scatters[way, part, step - 1].wait_recv()
                arrived = held.at[way, step - 1, pl.ds(part * half, half)]
                arrived[...] = (
                    arrived[...].astype(jnp.float32) + block[...].astype(jnp.float32)
                ).astype(jnp.bfloat16)
                block = arrived
            scatters[way, part, step] = begin(
                remote(
                    block,
                    held.at[way, step, pl.ds(part * half, half)],
                    scatter_send.at[way, part, step],
                    scatter_recv.at[way, part, step],
                    {"exp": others[way]},
                )
            )

    advance(2, 1)
    raw(1)
    fill_gains()
    advance(2, 2)
    far(1, 1)
    raw(2)
    fill_scales()
    for step in range(3, reach):
        advance(2, step)
        raw(step)
        far(1, step)
    activate(0)
    advance(2, reach)
    raw(reach)
    finish(0)
    far(1, reach)
    far(1, 2)
    activate(1)
    finish(1)
    activate(reach - 1)
    activate(reach)
    finish(reach - 1)
    scatter(0, (2, 3))
    finish(reach)
    scatter(0, (0, 1))
    for group in range(reach - 2, 1, -1):
        activate(group)
        finish(group)
    for step in range(1, reach):
        scatter(step)
    last = {}
    for way, part, steps in ring_lanes(count):
        scatters[way, part, steps - 1].wait_recv()
        last[way, part] = steps - 1
    for part in range(2):
        span = slice(part * half, (part + 1) * half)
        for side, base, target in ((0, rows, output_ref), (1, grad_ref, grad_out_ref)):
            cols = slice(side * width, (side + 1) * width)
            target[span, :] = (
                base[span, :].astype(jnp.float32)
                + (
                    parts[span, cols].astype(jnp.float32)
                    + held[0, last[0, part], span, cols].astype(jnp.float32)
                    + held[1, last[1, part], span, cols].astype(jnp.float32)
                )
            ).astype(jnp.bfloat16)
    for each in started:
        each.wait_send()


def fused_device(queries, keys, values, w_in, w_out, routes, route_weights, grad_out):
    count = lax.axis_size("exp")
    tokens, width = queries.shape
    cached, kv_width = keys.shape
    hidden = w_in.shape[3]
    side = hidden // 2
    reach = count // 2
    every = count * tokens
    experts = w_in.shape[0] * count

    def body(*refs):
        fused_kernel(count, *refs)

    def half(*shape):
        return pltpu.VMEM(shape, jnp.bfloat16)

    def whole(*shape):
        return pltpu.VMEM(shape, jnp.float32)

    dma = pltpu.SemaphoreType.DMA
    vmem = pl.BlockSpec(memory_space=pltpu.VMEM)
    anywhere = pl.BlockSpec(memory_space=pl.ANY)
    return pl.pallas_call(
        body,
        out_shape=[jax.ShapeDtypeStruct((tokens, width), jnp.bfloat16)] * 2,
        in_specs=[vmem, vmem, vmem, anywhere, anywhere, vmem, vmem, vmem],
        out_specs=[vmem, vmem],
        scratch_shapes=[
            half(width, 2, hidden),
            half(2, width, hidden),
            half(2, side, width),
            half(count * cached, kv_width),
            half(count * cached, kv_width),
            half(every, width),
            half(every, width),
            whole(count, experts, tokens),
            whole(count, 8, tokens),
            whole(4, 8, tokens),
            whole(every, LANES),
            whole(every, LANES),
            whole(every, hidden),
            whole(every, side),
            half(every, hidden),
            half(every, side),
            half(every, hidden),
            half(every, side),
            half(every, hidden),
            half(every, side),
            half(every, hidden),
            half(every, side),
            half(every, 3 * side + LANES),
            half(every, 3 * side + LANES),
            half(every, 2 * width),
            half(2, reach, tokens, 2 * width),
            dma((2,)),
            dma((3, 2, 2, reach)),
            dma((3, 2, 2, reach)),
            dma((2, 2, reach)),
            dma((2, 2, reach)),
            dma((2, count)),
            dma((2, count)),
            dma((3,)),
            dma((3,)),
            dma((5, reach + 1)),
            dma((5, reach + 1)),
        ],
        compiler_params=pltpu.CompilerParams(
            collective_id=1, has_side_effects=True, vmem_limit_bytes=60 * 1024 * 1024
        ),
        name="fused",
    )(
        queries,
        keys,
        values,
        w_in,
        w_out[0].reshape(2, side, width),
        routes.T,
        route_weights.T,
        grad_out,
    )


def solution(mesh):
    fused = 2 * TOP >= mesh.shape["exp"] and mesh.shape["exp"] == 8 and mesh.shape["head"] == 4
    in_specs = (
        P("exp", "head"),
        P("exp", "head"),
        P("exp", "head"),
        P("exp", "head", None, None),
        P("exp", None, "head"),
        P("exp", None),
        P("exp", None),
        P("exp", "head"),
    )
    out_specs = (P("exp", "head"), P("exp", "head"))
    return jax.shard_map(
        fused_device if fused else per_device, mesh=mesh, in_specs=in_specs, out_specs=out_specs, check_vma=False
    )
```

```python
import jax
import jax.numpy as jnp
from jax import lax
from jax.experimental import pallas as pl
from jax.experimental.pallas import tpu as pltpu
from jax.sharding import PartitionSpec as P

D = 4096
HEAD_WIDTH = 128
TOP = 6


norm_eps = 1e-05
hidden_logits = -1e30


def block_partial(query_rows, query_pos, rows_of_keys, value_rows, key_pos):
    row_count = query_rows.shape[0]
    count_of_blocks = rows_of_keys.shape[0]
    kv_heads = rows_of_keys.shape[2] // HEAD_WIDTH
    grouping_width = query_rows.shape[1] // HEAD_WIDTH // kv_heads
    heads_of_queries = query_rows.reshape(row_count, kv_heads, grouping_width, HEAD_WIDTH)
    key_heads = rows_of_keys.reshape(count_of_blocks, -1, kv_heads, HEAD_WIDTH)
    value_heads = value_rows.reshape(count_of_blocks, -1, kv_heads, HEAD_WIDTH)
    visible = (key_pos[:, None, :] <= query_pos[None, :, None])[:, :, None, None, :]
    scores = jnp.einsum(
        "tgid,bjgd->btgij", heads_of_queries, key_heads, preferred_element_type=jnp.float32
    ) * HEAD_WIDTH ** (-0.5)
    scores = jnp.where(visible, scores, hidden_logits)
    best_score = jnp.max(scores, axis=-1).astype(jnp.bfloat16)
    weights = jnp.where(visible, jnp.exp(scores - best_score.astype(jnp.float32)[..., None]), 0.0)
    weight_total = jnp.sum(weights, axis=-1).astype(jnp.bfloat16)
    weighted_sum = jnp.einsum(
        "btgij,bjgd->btgid",
        weights.astype(jnp.bfloat16),
        value_heads,
        preferred_element_type=jnp.float32,
    ).astype(jnp.bfloat16)
    head_count = kv_heads * grouping_width
    return (
        best_score.reshape(count_of_blocks, row_count, head_count),
        weight_total.reshape(count_of_blocks, row_count, head_count),
        weighted_sum.reshape(count_of_blocks, row_count, head_count * HEAD_WIDTH),
    )


def fold_partials(running, best_score, weight_total, weighted_sum):
    top_now, total_now, sums_now = running
    best_value = best_score.astype(jnp.float32)
    new_top = jnp.maximum(top_now, jnp.max(best_value, axis=0))
    old_factor = jnp.exp(top_now - new_top)
    block_factor = jnp.exp(best_value - new_top[None])
    total_next = total_now * old_factor + jnp.sum(
        weight_total.astype(jnp.float32) * block_factor, axis=0
    )
    spread_sums = weighted_sum.reshape(
        weighted_sum.shape[0], sums_now.shape[0], sums_now.shape[1], HEAD_WIDTH
    )
    sums_next = sums_now * old_factor[..., None] + jnp.sum(
        spread_sums.astype(jnp.float32) * block_factor[..., None], axis=0
    )
    return (new_top, total_next, sums_next)


def per_device(queries, keys, values, w_in, w_out, routes, route_weights, grad_out):
    exp_count = lax.axis_size("exp")
    exp_index = lax.axis_index("exp")
    head_devices = lax.axis_size("head")
    token_count = queries.shape[0]
    query_width = queries.shape[1]
    head_count = query_width // HEAD_WIDTH
    cache_rows = keys.shape[0]
    window = token_count * exp_count
    offset = cache_rows * exp_count - window
    beginning = (
        jnp.full((token_count, head_count), hidden_logits, jnp.float32),
        jnp.zeros((token_count, head_count), jnp.float32),
        jnp.zeros((token_count, head_count, HEAD_WIDTH), jnp.float32),
    )
    own_pos = offset + exp_index * token_count + jnp.arange(token_count, dtype=jnp.int32)
    key_piece = lax.all_gather(keys, "exp", axis=0, tiled=True)
    value_piece = lax.all_gather(values, "exp", axis=0, tiled=True)
    piece_blocks = key_piece.shape[0] // cache_rows
    key_split = key_piece.reshape(piece_blocks, cache_rows, -1)
    value_split = value_piece.reshape(piece_blocks, cache_rows, -1)
    pos_split = jnp.arange(key_piece.shape[0], dtype=jnp.int32).reshape(piece_blocks, cache_rows)

    def one_block(state, element):
        key_block, value_block, pos_block = element
        block_parts = block_partial(
            queries, own_pos, key_block[None], value_block[None], pos_block[None]
        )
        return (fold_partials(state, block_parts[0], block_parts[1], block_parts[2]), None)

    state, ignored = lax.scan(one_block, beginning, (key_split, value_split, pos_split))
    attended = (
        (state[2] / state[1][..., None]).reshape(token_count, query_width).astype(jnp.bfloat16)
    )
    row_width = attended.shape[1]
    experts_all = w_in.shape[0] * exp_count
    mean_load = TOP * token_count // experts_all
    capacity = mean_load + mean_load // 6
    places = experts_all * capacity
    flat_routes = routes.reshape(-1)
    expert_hits = (
        flat_routes[:, None] == jnp.arange(experts_all, dtype=jnp.int32)[None, :]
    ).astype(jnp.bfloat16)
    before = jnp.tri(flat_routes.shape[0], k=-1, dtype=jnp.bfloat16)
    earlier = jnp.dot(before, expert_hits, preferred_element_type=jnp.float32)
    slot_index = jnp.sum(earlier * expert_hits.astype(jnp.float32), axis=1).astype(jnp.int32)
    place_index = flat_routes * capacity + slot_index
    chosen = (place_index[:, None] == jnp.arange(places, dtype=jnp.int32)[None, :]).astype(
        jnp.bfloat16
    )
    picker = jnp.sum(chosen.reshape(token_count, TOP, places), axis=1)
    contract_rows = (((0,), (0,)), ((), ()))
    send_rows = lax.dot_general(picker, attended, contract_rows, preferred_element_type=jnp.float32)
    send_rows = send_rows.astype(jnp.bfloat16).reshape(experts_all, capacity, row_width)
    send_grads = lax.dot_general(
        picker, grad_out, contract_rows, preferred_element_type=jnp.float32
    )
    send_grads = send_grads.astype(jnp.bfloat16).reshape(experts_all, capacity, row_width)
    w_first = w_in[0]
    w_second = w_out[0]
    rows_in = lax.all_to_all(send_rows, "exp", split_axis=0, concat_axis=0, tiled=True)
    grads_in = lax.all_to_all(send_grads, "exp", split_axis=0, concat_axis=0, tiled=True)
    lead_count, item_count, width_in = rows_in.shape
    row_total = lead_count * item_count
    row_block = rows_in.reshape(row_total, width_in)
    grad_block = grads_in.reshape(row_total, width_in)
    row_float = row_block.astype(jnp.float32)
    raw_sums = jnp.einsum("rd,dkf->rkf", row_block, w_first, preferred_element_type=jnp.float32)
    back_sums = lax.dot_general(
        grad_block, w_second, (((1,), (1,)), ((), ())), preferred_element_type=jnp.float32
    )
    squares = jnp.sum(row_float * row_float, axis=1)
    square_tile = jnp.broadcast_to(squares[:, None, None], (row_total, 1, head_devices))
    raw_part = lax.psum_scatter(raw_sums, "head", scatter_dimension=2, tiled=True)
    back_part = lax.psum_scatter(back_sums[:, None, :], "head", scatter_dimension=2, tiled=True)
    square_part = lax.psum_scatter(square_tile, "head", scatter_dimension=2, tiled=True)
    norm_scale = lax.rsqrt(square_part[:, 0] / D + norm_eps)
    gate_value = raw_part[:, 0] * norm_scale
    up_value = raw_part[:, 1] * norm_scale
    back_value = back_part[:, 0]
    gate_sigmoid = jax.nn.sigmoid(gate_value)
    gate_silu = gate_value * gate_sigmoid
    act_part = (gate_silu * up_value).astype(jnp.bfloat16)
    grad_gate = back_value * up_value * gate_sigmoid * (1.0 + gate_value * (1.0 - gate_sigmoid))
    grad_up = back_value * gate_silu
    grad_part = jnp.stack([grad_gate, grad_up], axis=1).astype(jnp.bfloat16)
    inner_part = jnp.sum(
        grad_part.astype(jnp.float32) * jnp.stack([gate_value, up_value], axis=1), axis=(1, 2)
    )
    act_whole = lax.all_gather(act_part[:, None, :], "head", axis=2, tiled=True)
    grad_hidden = lax.all_gather(grad_part, "head", axis=2, tiled=True)
    hidden_act = act_whole[:, 0]
    inner_sum = lax.psum(inner_part, "head")
    out_rows = jnp.dot(hidden_act, w_second, preferred_element_type=jnp.float32).astype(
        jnp.bfloat16
    )
    grad_normed = jnp.einsum(
        "rkf,dkf->rd", grad_hidden, w_first, preferred_element_type=jnp.float32
    )
    grad_rows = (
        norm_scale * grad_normed - row_float * (norm_scale * norm_scale / D) * inner_sum[:, None]
    )
    expert_out = out_rows.reshape(lead_count, item_count, width_in)
    expert_grad = grad_rows.astype(jnp.bfloat16).reshape(lead_count, item_count, width_in)
    came_out, came_grad = (
        lax.all_to_all(expert_out, "exp", split_axis=0, concat_axis=0, tiled=True),
        lax.all_to_all(expert_grad, "exp", split_axis=0, concat_axis=0, tiled=True),
    )
    picked_out = came_out.reshape(places, row_width)[place_index].reshape(
        token_count, TOP, row_width
    )
    picked_grad = came_grad.reshape(places, row_width)[place_index].reshape(
        token_count, TOP, row_width
    )
    output = attended.astype(jnp.float32) + jnp.sum(
        route_weights[:, :, None] * picked_out.astype(jnp.float32), axis=1
    )
    grad_attended = grad_out.astype(jnp.float32) + jnp.sum(
        route_weights[:, :, None] * picked_grad.astype(jnp.float32), axis=1
    )
    return (output.astype(jnp.bfloat16), grad_attended.astype(jnp.bfloat16))


LANES = 128
EXACT = (((1,), (1,)), ((), ()))


def three_parts(value):
    high = value.astype(jnp.bfloat16)
    rest = value - high.astype(jnp.float32)
    middle = rest.astype(jnp.bfloat16)
    low = (rest - middle.astype(jnp.float32)).astype(jnp.bfloat16)
    return high, middle, low


def ring_place(index, count):
    outer, inner = index // 2, index % 2
    return outer + inner * (count - 1 - 2 * outer)


def ring_index(place, count):
    inner = place // (count // 2)
    return 2 * (place + inner * (count - 1 - 2 * place)) + inner


def ring_lanes(count):
    reach = count // 2
    return ((0, 0, reach), (1, 1, reach), (0, 1, reach - 1), (1, 0, reach - 1))


def slot_of(distance, count):
    if distance == 0:
        return 0
    if abs(distance) == count // 2:
        return count - 1
    return 2 * distance - 1 if distance > 0 else -2 * distance


def wide(value, width):
    return jnp.concatenate([value] * (width // value.shape[1]), axis=1)


def fused_kernel(
    count,
    q_ref,
    k_ref,
    v_ref,
    w_in_ref,
    w_out_ref,
    routes_ref,
    share_ref,
    grad_ref,
    output_ref,
    grad_out_ref,
    w_pairs,
    w_up,
    w_down,
    kv_all,
    grads,
    rows,
    tables,
    squares,
    head_squares,
    gains,
    scales,
    sum_raw,
    sum_back,
    near_raw,
    near_back,
    near_raw_in,
    near_back_in,
    far_raw,
    far_back,
    far_raw_in,
    far_back_in,
    act,
    act_in,
    parts,
    held,
    load_sem,
    send_sem,
    early_recv,
    rows_recv,
    scatter_recv,
    meta_recv,
    head_recv,
    pair_recv,
):
    reach = count // 2
    tokens, width = q_ref.shape
    cached, kv_width = k_ref.shape
    side = w_down.shape[1]
    experts = tables.shape[1]
    half = tokens // 2
    quarter = half // 2
    me = lax.axis_index("exp")
    place = ring_place(me, count)
    head = lax.axis_index("head")
    core = head % 2
    mate = head + 1 - 2 * core
    across = (head + 2) % 4
    corner = 3 - head
    others = (ring_index((place + 1) % count, count), ring_index((place + count - 1) % count, count))
    distances = [0] + [d for s in range(1, reach) for d in (s, -s)] + [reach]
    lanes = []
    for way, sub, steps in ring_lanes(count):
        lanes.append((way, sub, steps, sum(lane[2] for lane in lanes)))

    def remote(source, target, kind, recv_sem, where):
        return pltpu.make_async_remote_copy(
            src_ref=source,
            dst_ref=target,
            send_sem=send_sem.at[kind],
            recv_sem=recv_sem,
            device_id=where,
            device_id_type=pl.DeviceIdType.MESH,
        )

    def begin(*what):
        copy = remote(*what)
        copy.start()
        return copy

    load_in = pltpu.make_async_copy(w_in_ref.at[0], w_pairs, load_sem.at[0])
    load_out = pltpu.make_async_copy(w_out_ref, w_down, load_sem.at[1])
    load_in.start()
    load_out.start()

    barrier = pltpu.get_barrier_semaphore()
    for other in (mate, across, corner):
        pl.semaphore_signal(
            barrier, inc=1, device_id={"head": other}, device_id_type=pl.DeviceIdType.MESH
        )
    for distance in distances[1:]:
        other = ring_index((place + distance + count) % count, count)
        pl.semaphore_signal(
            barrier, inc=1, device_id={"exp": other}, device_id_type=pl.DeviceIdType.MESH
        )

    kv_all[0, 0] = k_ref[...]
    kv_all[0, 1] = v_ref[...]
    grads[:, 0:half, :] = grad_ref[...]
    expert_row = lax.broadcasted_iota(jnp.int32, (experts, tokens), 0)
    table = jnp.zeros((experts, tokens), jnp.float32)
    for k in range(routes_ref.shape[0]):
        table = table + jnp.where(expert_row == routes_ref[k : k + 1, :], share_ref[k : k + 1, :], 0.0)
    tables[0] = table
    pl.semaphore_wait(barrier, 3 + count - 1)

    early = {}

    def early_ref(kind, slot, part):
        if kind == 0:
            return kv_all.at[slot] if part is None else kv_all.at[slot, part]
        span = pl.ds(slot * half, half)
        return grads.at[:, span] if part is None else grads.at[part, span]

    def advance(kind, step):
        for way in range(2):
            if step >= 1:
                early[kind, way, step - 1].wait_recv()
            if step < reach:
                sign = -1 if way == 0 else 1
                part = way if step == reach - 1 else None
                early[kind, way, step] = begin(
                    early_ref(kind, slot_of(sign * step, count), part),
                    early_ref(kind, slot_of(sign * (step + 1), count), part),
                    kind,
                    early_recv.at[kind, way, step],
                    {"exp": others[way]},
                )

    moving = {}

    def advance_rows(wave, step):
        for way, sub, steps, first in lanes:
            if 1 <= step <= steps:
                moving[wave, way, sub, step - 1].wait_recv()
            if step < steps:
                sign = -1 if way == 0 else 1
                there = slot_of(sign * (step + 1), count) * half + sub * quarter
                here = slot_of(sign * step, count) * half + sub * quarter
                moving[wave, way, sub, step] = begin(
                    rows.at[wave, pl.ds(here, quarter)],
                    rows.at[wave, pl.ds(there, quarter)],
                    2 + wave,
                    rows_recv.at[wave, first + step],
                    {"exp": others[way]},
                )

    def broadcast(kind, store):
        copies = []
        for distance in distances[1:]:
            there = slot_of(-distance, count)
            other = ring_index((place + distance + count) % count, count)
            copies.append(
                begin(
                    store.at[0],
                    store.at[there],
                    6 + kind,
                    meta_recv.at[kind, there - 1],
                    {"exp": other},
                )
            )
        return copies

    def split():
        load_in.wait()
        chunk = LANES
        to = lax.broadcasted_iota(jnp.int32, (2 * chunk, 2 * chunk), 0)
        source = lax.broadcasted_iota(jnp.int32, (2 * chunk, 2 * chunk), 1)
        picks = (source == jnp.where(to < chunk, 2 * to, 2 * to - 2 * chunk + 1)).astype(jnp.bfloat16)

        def split_chunk(index, carry):
            span = pl.ds(pl.multiple_of(index * chunk, chunk), chunk)
            pairs = w_pairs[span].reshape(2 * chunk, 2 * side)
            apart = jnp.dot(picks, pairs, preferred_element_type=jnp.float32).astype(jnp.bfloat16)
            for part in range(2):
                cols = slice(part * side, (part + 1) * side)
                w_up[part, span, :side] = apart[:chunk, cols]
                w_up[part, span, side:] = apart[chunk:, cols]
            return carry

        lax.fori_loop(0, width // chunk, split_chunk, 0)
        load_out.wait()

    pairs = {}

    def pair_begin(kind, wave, slot, blocks, source, target, other):
        span = pl.ds(slot * half, blocks * half)
        if wave is None:
            source, target = source.at[:, span], target.at[:, span]
        else:
            source, target = source.at[wave, span], target.at[wave, span]
        pairs[kind, wave, slot] = begin(
            source, target, 8 + kind, pair_recv.at[len(pairs)], {"head": other}
        )

    def back(slot, blocks):
        span = slice(slot * half, (slot + blocks) * half)
        size = blocks * half
        weights = jnp.concatenate([w_down[1 - core], w_down[core]], axis=0)
        both = lax.dot_general(
            grads[:, span, :].reshape(2 * size, width),
            weights,
            EXACT,
            preferred_element_type=jnp.float32,
        )
        near_back[:, span, :] = both[:, :side].astype(jnp.bfloat16).reshape(2, size, side)
        pair_begin(0, None, slot, blocks, near_back, near_back_in, mate)
        sum_back[:, span, :] = both[:, side:].reshape(2, size, side)

    def raw(unit, wave):
        slot, blocks = units[unit]
        span = slice(slot * half, (slot + blocks) * half)
        block = rows[wave, span, :]
        near_raw[wave, span, :] = jnp.dot(
            block, w_up[1 - core], preferred_element_type=jnp.float32
        ).astype(jnp.bfloat16)
        pair_begin(1, wave, slot, blocks, near_raw, near_raw_in, mate)
        sum_raw[wave, span, :] = jnp.dot(block, w_up[core], preferred_element_type=jnp.float32)

    def far_begin(kind, wave, slot, blocks):
        total, near_in = ((sum_back, near_back_in), (sum_raw, near_raw_in))[kind]
        out, target = ((far_back, far_back_in), (far_raw, far_raw_in))[kind]
        span = slice(slot * half, (slot + blocks) * half)
        for one in (0, 1) if wave is None else (wave,):
            both = total[one, span, :] + near_in[one, span, :].astype(jnp.float32)
            total[one, span, :] = both
            out[one, span, :] = both.astype(jnp.bfloat16)
        pair_begin(2 + kind, wave, slot, blocks, out, target, across)

    def far_back_sum(slot, blocks, wave=None):
        if wave is None or wave == 0:
            for near_slot in (slot, slot + 2):
                if near_slot < slot + blocks and (0, None, near_slot) in pairs:
                    pairs[0, None, near_slot].wait_recv()
        far_begin(0, wave, slot, blocks)

    def far_raw_sum(unit, wave):
        slot, blocks = units[unit]
        pairs[1, wave, slot].wait_recv()
        far_begin(1, wave, slot, blocks)

    def attention():
        heads = width // HEAD_WIDTH
        together = heads // (kv_width // HEAD_WIDTH)
        every = count * cached
        column = lax.broadcasted_iota(jnp.int32, (1, every), 1)
        first = jnp.zeros((1, every), jnp.int32)
        for slot, distance in enumerate(distances):
            owner = ring_index((place + distance + count) % count, count)
            first = jnp.where(column // cached == slot, (owner - slot) * cached, first)
        row_pos = (
            count * (cached - tokens)
            + me * tokens
            + lax.broadcasted_iota(jnp.int32, (tokens, every), 0)
        )
        visible = jnp.broadcast_to(first + column, (tokens, every)) <= row_pos
        total = jnp.zeros((tokens, LANES), jnp.float32)
        for one in range(heads):
            cols = slice(one * HEAD_WIDTH, (one + 1) * HEAD_WIDTH)
            kv_cols = slice(one // together * HEAD_WIDTH, (one // together + 1) * HEAD_WIDTH)
            scores = lax.dot_general(
                q_ref[:, cols],
                kv_all[:, 0, :, kv_cols].reshape(every, HEAD_WIDTH),
                EXACT,
                preferred_element_type=jnp.float32,
            ) * HEAD_WIDTH ** (-0.5)
            scores = jnp.where(visible, scores, hidden_logits)
            best = jnp.max(scores, axis=1, keepdims=True)
            weights = jnp.exp(scores - best)
            weight_total = jnp.sum(weights, axis=1, keepdims=True)
            sums = jnp.dot(
                weights.astype(jnp.bfloat16),
                kv_all[:, 1, :, kv_cols].reshape(every, HEAD_WIDTH),
                preferred_element_type=jnp.float32,
            )
            mixed = (sums / weight_total).astype(jnp.bfloat16)
            rows[0, 0:half, cols] = mixed[:half]
            rows[1, 0:half, cols] = mixed[half:]
            mixed = mixed.astype(jnp.float32)
            total = total + mixed * mixed
        return total

    def share_squares(total):
        columns = jnp.broadcast_to(jnp.sum(total, axis=1, keepdims=True), (tokens, LANES))
        head_squares[0] = jnp.transpose(columns)[: head_squares.shape[1]]
        return [
            begin(
                head_squares.at[0],
                head_squares.at[index + 1],
                13,
                head_recv.at[index],
                {"head": other},
            )
            for index, other in enumerate((mate, across, corner))
        ]

    def spread_squares(copies):
        for each in copies:
            each.wait_recv()
        squares[0] = (head_squares[0] + head_squares[1]) + (head_squares[2] + head_squares[3])
        return broadcast(1, squares)

    def fill(store, slot, row):
        columns = jnp.transpose(jnp.broadcast_to(row, (LANES, tokens)))
        for wave in range(2):
            store[wave, slot * half : (slot + 1) * half, :] = columns[wave * half : (wave + 1) * half]

    def fill_gains(copies):
        for each in copies:
            each.wait_recv()
        for slot in range(count):
            row = jnp.sum(jnp.where(expert_row == me, tables[slot], 0.0), axis=0, keepdims=True)
            fill(gains, slot, row)

    def fill_scales(copies):
        for each in copies:
            each.wait_recv()
        for slot in range(count):
            fill(scales, slot, lax.rsqrt(squares[slot][0:1, :] / D + norm_eps))

    def activate(unit, wave):
        slot, blocks = units[unit]
        if (2, None, slot) in pairs:
            if wave == 0:
                pairs[2, None, slot].wait_recv()
        else:
            pairs[2, wave, slot].wait_recv()
        pairs[3, wave, slot].wait_recv()
        step = 32
        lane = lax.broadcasted_iota(jnp.int32, (step, LANES), 1)

        def some_rows(index, carry):
            span = pl.ds(pl.multiple_of(slot * half + index * step, step), step)
            scale = scales[wave, span, :]
            gain = gains[wave, span, :]
            inner = jnp.zeros((step, LANES), jnp.float32)
            for start in range(0, side, LANES):
                cols = slice(start, start + LANES)
                up_cols = slice(side + start, side + start + LANES)
                down_cols = slice(2 * side + start, 2 * side + start + LANES)
                gate = sum_raw[wave, span, cols] + far_raw_in[wave, span, cols].astype(jnp.float32)
                up = sum_raw[wave, span, up_cols] + far_raw_in[wave, span, up_cols].astype(
                    jnp.float32
                )
                gate, up = gate * scale, up * scale
                back_value = sum_back[wave, span, cols] + far_back_in[wave, span, cols].astype(
                    jnp.float32
                )
                sigmoid = jax.nn.sigmoid(gate)
                silu = gate * sigmoid
                grad_gate = back_value * up * sigmoid * (1.0 + gate * (1.0 - sigmoid))
                grad_up = back_value * silu
                inner = inner + (grad_gate * gate + grad_up * up)
                act[wave, span, cols] = (gain * (silu * up)).astype(jnp.bfloat16)
                act[wave, span, up_cols] = (gain * scale * grad_gate).astype(jnp.bfloat16)
                act[wave, span, down_cols] = (gain * scale * grad_up).astype(jnp.bfloat16)
            high, middle, low = three_parts(
                jnp.broadcast_to(jnp.sum(inner, axis=1, keepdims=True), (step, LANES))
            )
            zero = jnp.zeros((step, LANES), jnp.float32)
            spread = jnp.where(lane == 0, high.astype(jnp.float32), zero)
            spread = jnp.where(lane == 1, middle.astype(jnp.float32), spread)
            spread = jnp.where(lane == 2, low.astype(jnp.float32), spread)
            act[wave, span, 3 * side :] = spread.astype(jnp.bfloat16)
            return carry

        lax.fori_loop(0, blocks * half // step, some_rows, 0)
        pair_begin(4, wave, slot, blocks, act, act_in, mate)

    def finish(unit, wave):
        slot, blocks = units[unit]
        span = slice(slot * half, (slot + blocks) * half)
        pairs[4, wave, slot].wait_recv()
        inner = jnp.sum(
            act[wave, span, 3 * side :].astype(jnp.float32)
            + act_in[wave, span, 3 * side :].astype(jnp.float32),
            axis=1,
            keepdims=True,
        )
        tile = 256
        scale = scales[wave, span, :]
        bent = wide(gains[wave, span, :] * (scale * scale / D) * inner, tile)
        hidden = slice(0, side)
        slopes = slice(side, 3 * side)
        act_all = jnp.concatenate([act[wave, span, hidden], act_in[wave, span, hidden]], axis=1)
        for start in range(0, width, tile):
            cols = slice(start, start + tile)
            weights = jnp.concatenate([w_down[core, :, cols], w_down[1 - core, :, cols]], axis=0)
            out = jnp.dot(act_all, weights, preferred_element_type=jnp.float32)
            parts[wave, span, cols] = out.astype(jnp.bfloat16)
            grad = lax.dot_general(
                act[wave, span, slopes],
                w_up[core, cols, :],
                EXACT,
                preferred_element_type=jnp.float32,
            ) + lax.dot_general(
                act_in[wave, span, slopes],
                w_up[1 - core, cols, :],
                EXACT,
                preferred_element_type=jnp.float32,
            )
            grad = grad - bent * rows[wave, span, cols].astype(jnp.float32)
            parts[wave, span, width + start : width + start + tile] = grad.astype(jnp.bfloat16)

    sums = {}

    def scatter(wave, step):
        for way, sub, steps, first in lanes:
            if step >= steps:
                continue
            sign = 1 if way == 0 else -1
            start = slot_of(sign * (steps - step), count) * half + sub * quarter
            block = parts.at[wave, pl.ds(start, quarter)]
            there = pl.ds(sub * quarter, quarter)
            if step > 0:
                sums[wave, way, sub, step - 1].wait_recv()
                arrived = held.at[wave, way, step - 1, there]
                arrived[...] = (
                    arrived[...].astype(jnp.float32) + block[...].astype(jnp.float32)
                ).astype(jnp.bfloat16)
                block = arrived
            sums[wave, way, sub, step] = begin(
                block,
                held.at[wave, way, step, there],
                4 + wave,
                scatter_recv.at[wave, first + step],
                {"exp": others[way]},
            )

    def settle(wave):
        for sub in range(2):
            span = slice(sub * quarter, (sub + 1) * quarter)
            target = slice(wave * half + sub * quarter, wave * half + (sub + 1) * quarter)
            value = parts[wave, span, :].astype(jnp.float32)
            for way, lane_sub, steps, first in lanes:
                if lane_sub == sub:
                    sums[wave, way, sub, steps - 1].wait_recv()
                    value = value + held[wave, way, steps - 1, span, :].astype(jnp.float32)
            output_ref[target, :] = (
                rows[wave, span, :].astype(jnp.float32) + value[:, :width]
            ).astype(jnp.bfloat16)
            grad_out_ref[target, :] = (
                grad_ref[wave, span, :].astype(jnp.float32) + value[:, width:]
            ).astype(jnp.bfloat16)

    def drain():
        others_of = pl.ds(half, (count - 1) * half)
        for kind, sent in enumerate(
            (
                kv_all.at[pl.ds(1, count - 1)],
                grads.at[:, others_of],
                rows.at[0, others_of],
                rows.at[1, others_of],
                parts.at[0, others_of],
                parts.at[1, others_of],
                tables.at[pl.ds(1, count - 1)],
                squares.at[pl.ds(1, count - 1)],
                near_back,
                near_raw,
                far_back,
                far_raw,
                act,
                head_squares.at[pl.ds(1, 3)],
            )
        ):
            remote(sent, sent, kind, load_sem.at[0], {"head": mate}).wait_send()

    last_unit = reach - 2
    units = (
        [(0, 3)] + [(2 * step - 1, 2) for step in range(2, reach - 1)] + [(2 * reach - 3, 3)]
    )
    advance(0, 0)
    advance(1, 0)
    table_copies = broadcast(0, tables)
    split()
    advance(0, 1)
    advance(1, 1)
    back(0, 3)
    advance(0, 2)
    far_back_sum(0, 3)
    advance(1, 2)
    back(3, 2)
    for step in range(3, reach):
        advance(0, step)
        far_back_sum(2 * step - 3, 2)
        advance(1, step)
        back(2 * step - 1, 2)
    advance(0, reach)
    square_total = attention()
    advance_rows(0, 0)
    square_copies = share_squares(square_total)
    advance(1, reach)
    back(count - 1, 1)
    advance_rows(0, 1)
    far_back_sum(2 * reach - 3, 3, 0)
    square_copies = spread_squares(square_copies)
    raw(0, 0)
    advance_rows(0, 2)
    far_raw_sum(0, 0)
    fill_gains(table_copies)
    advance_rows(0, 3)
    advance_rows(1, 0)
    raw(1, 0)
    for step in range(4, reach + 1):
        advance_rows(0, step)
    raw(last_unit, 0)
    advance_rows(1, 1)
    far_raw_sum(last_unit, 0)
    far_raw_sum(1, 0)
    fill_scales(square_copies)
    raw(0, 1)
    advance_rows(1, 2)
    activate(0, 0)
    finish(0, 0)
    advance_rows(1, 3)
    far_back_sum(2 * reach - 3, 3, 1)
    far_raw_sum(0, 1)
    raw(1, 1)
    for step in range(4, reach + 1):
        advance_rows(1, step)
    activate(last_unit, 0)
    finish(last_unit, 0)
    scatter(0, 0)
    raw(last_unit, 1)
    far_raw_sum(last_unit, 1)
    far_raw_sum(1, 1)
    activate(1, 0)
    finish(1, 0)
    scatter(0, 1)
    activate(0, 1)
    finish(0, 1)
    scatter(0, 2)
    activate(last_unit, 1)
    finish(last_unit, 1)
    for step in range(3, reach):
        scatter(0, step)
    scatter(1, 0)
    activate(1, 1)
    finish(1, 1)
    settle(0)
    for step in range(1, reach):
        scatter(1, step)
    settle(1)
    drain()


def fused_device(queries, keys, values, w_in, w_out, routes, route_weights, grad_out):
    count = lax.axis_size("exp")
    tokens, width = queries.shape
    cached, kv_width = keys.shape
    hidden = w_in.shape[3]
    side = hidden // 2
    reach = count // 2
    half_rows = tokens // 2
    every = count * half_rows
    experts = w_in.shape[0] * count

    def body(*refs):
        fused_kernel(count, *refs)

    def half(*shape):
        return pltpu.VMEM(shape, jnp.bfloat16)

    def whole(*shape):
        return pltpu.VMEM(shape, jnp.float32)

    dma = pltpu.SemaphoreType.DMA
    vmem = pl.BlockSpec(memory_space=pltpu.VMEM)
    anywhere = pl.BlockSpec(memory_space=pl.ANY)
    return pl.pallas_call(
        body,
        out_shape=[jax.ShapeDtypeStruct((tokens, width), jnp.bfloat16)] * 2,
        in_specs=[vmem, vmem, vmem, anywhere, anywhere, vmem, vmem, vmem],
        out_specs=[vmem, vmem],
        scratch_shapes=[
            half(width, 2, hidden),
            half(2, width, hidden),
            half(2, side, width),
            half(count, 2, cached, kv_width),
            half(2, every, width),
            half(2, every, width),
            whole(count, experts, tokens),
            whole(count, 8, tokens),
            whole(4, 8, tokens),
            whole(2, every, LANES),
            whole(2, every, LANES),
            whole(2, every, hidden),
            whole(2, every, side),
            half(2, every, hidden),
            half(2, every, side),
            half(2, every, hidden),
            half(2, every, side),
            half(2, every, hidden),
            half(2, every, side),
            half(2, every, hidden),
            half(2, every, side),
            half(2, every, 3 * side + LANES),
            half(2, every, 3 * side + LANES),
            half(2, every, 2 * width),
            half(2, 2, reach, half_rows, 2 * width),
            dma((2,)),
            dma((14,)),
            dma((2, 2, reach)),
            dma((2, 4 * reach - 2)),
            dma((2, 4 * reach - 2)),
            dma((2, count - 1)),
            dma((3,)),
            dma((reach + reach + 6 * (reach - 1),)),
        ],
        compiler_params=pltpu.CompilerParams(
            collective_id=1, has_side_effects=True, vmem_limit_bytes=60 * 1024 * 1024
        ),
        name="fused",
    )(
        queries,
        keys,
        values,
        w_in,
        w_out[0].reshape(2, side, width),
        routes.T,
        route_weights.T,
        grad_out.reshape(2, half_rows, width),
    )


def solution(mesh):
    fused = 2 * TOP >= mesh.shape["exp"] and mesh.shape["exp"] == 8 and mesh.shape["head"] == 4
    in_specs = (
        P("exp", "head"),
        P("exp", "head"),
        P("exp", "head"),
        P("exp", "head", None, None),
        P("exp", None, "head"),
        P("exp", None),
        P("exp", None),
        P("exp", "head"),
    )
    out_specs = (P("exp", "head"), P("exp", "head"))
    return jax.shard_map(
        fused_device if fused else per_device, mesh=mesh, in_specs=in_specs, out_specs=out_specs, check_vma=False
    )
```

```python
import jax
import jax.numpy as jnp
from jax import lax
from jax.experimental import pallas as pl
from jax.experimental.pallas import tpu as pltpu
from jax.sharding import PartitionSpec as P

D = 4096
HEAD_WIDTH = 128
TOP = 6


norm_eps = 1e-05
hidden_logits = -1e30


def block_partial(query_rows, query_pos, rows_of_keys, value_rows, key_pos):
    row_count = query_rows.shape[0]
    count_of_blocks = rows_of_keys.shape[0]
    kv_heads = rows_of_keys.shape[2] // HEAD_WIDTH
    grouping_width = query_rows.shape[1] // HEAD_WIDTH // kv_heads
    heads_of_queries = query_rows.reshape(row_count, kv_heads, grouping_width, HEAD_WIDTH)
    key_heads = rows_of_keys.reshape(count_of_blocks, -1, kv_heads, HEAD_WIDTH)
    value_heads = value_rows.reshape(count_of_blocks, -1, kv_heads, HEAD_WIDTH)
    visible = (key_pos[:, None, :] <= query_pos[None, :, None])[:, :, None, None, :]
    scores = jnp.einsum(
        "tgid,bjgd->btgij", heads_of_queries, key_heads, preferred_element_type=jnp.float32
    ) * HEAD_WIDTH ** (-0.5)
    scores = jnp.where(visible, scores, hidden_logits)
    best_score = jnp.max(scores, axis=-1).astype(jnp.bfloat16)
    weights = jnp.where(visible, jnp.exp(scores - best_score.astype(jnp.float32)[..., None]), 0.0)
    weight_total = jnp.sum(weights, axis=-1).astype(jnp.bfloat16)
    weighted_sum = jnp.einsum(
        "btgij,bjgd->btgid",
        weights.astype(jnp.bfloat16),
        value_heads,
        preferred_element_type=jnp.float32,
    ).astype(jnp.bfloat16)
    head_count = kv_heads * grouping_width
    return (
        best_score.reshape(count_of_blocks, row_count, head_count),
        weight_total.reshape(count_of_blocks, row_count, head_count),
        weighted_sum.reshape(count_of_blocks, row_count, head_count * HEAD_WIDTH),
    )


def fold_partials(running, best_score, weight_total, weighted_sum):
    top_now, total_now, sums_now = running
    best_value = best_score.astype(jnp.float32)
    new_top = jnp.maximum(top_now, jnp.max(best_value, axis=0))
    old_factor = jnp.exp(top_now - new_top)
    block_factor = jnp.exp(best_value - new_top[None])
    total_next = total_now * old_factor + jnp.sum(
        weight_total.astype(jnp.float32) * block_factor, axis=0
    )
    spread_sums = weighted_sum.reshape(
        weighted_sum.shape[0], sums_now.shape[0], sums_now.shape[1], HEAD_WIDTH
    )
    sums_next = sums_now * old_factor[..., None] + jnp.sum(
        spread_sums.astype(jnp.float32) * block_factor[..., None], axis=0
    )
    return (new_top, total_next, sums_next)


def per_device(queries, keys, values, w_in, w_out, routes, route_weights, grad_out):
    exp_count = lax.axis_size("exp")
    exp_index = lax.axis_index("exp")
    head_devices = lax.axis_size("head")
    token_count = queries.shape[0]
    query_width = queries.shape[1]
    head_count = query_width // HEAD_WIDTH
    cache_rows = keys.shape[0]
    window = token_count * exp_count
    offset = cache_rows * exp_count - window
    beginning = (
        jnp.full((token_count, head_count), hidden_logits, jnp.float32),
        jnp.zeros((token_count, head_count), jnp.float32),
        jnp.zeros((token_count, head_count, HEAD_WIDTH), jnp.float32),
    )
    own_pos = offset + exp_index * token_count + jnp.arange(token_count, dtype=jnp.int32)
    key_piece = lax.all_gather(keys, "exp", axis=0, tiled=True)
    value_piece = lax.all_gather(values, "exp", axis=0, tiled=True)
    piece_blocks = key_piece.shape[0] // cache_rows
    key_split = key_piece.reshape(piece_blocks, cache_rows, -1)
    value_split = value_piece.reshape(piece_blocks, cache_rows, -1)
    pos_split = jnp.arange(key_piece.shape[0], dtype=jnp.int32).reshape(piece_blocks, cache_rows)

    def one_block(state, element):
        key_block, value_block, pos_block = element
        block_parts = block_partial(
            queries, own_pos, key_block[None], value_block[None], pos_block[None]
        )
        return (fold_partials(state, block_parts[0], block_parts[1], block_parts[2]), None)

    state, ignored = lax.scan(one_block, beginning, (key_split, value_split, pos_split))
    attended = (
        (state[2] / state[1][..., None]).reshape(token_count, query_width).astype(jnp.bfloat16)
    )
    row_width = attended.shape[1]
    experts_all = w_in.shape[0] * exp_count
    mean_load = TOP * token_count // experts_all
    capacity = mean_load + mean_load // 6
    places = experts_all * capacity
    flat_routes = routes.reshape(-1)
    expert_hits = (
        flat_routes[:, None] == jnp.arange(experts_all, dtype=jnp.int32)[None, :]
    ).astype(jnp.bfloat16)
    before = jnp.tri(flat_routes.shape[0], k=-1, dtype=jnp.bfloat16)
    earlier = jnp.dot(before, expert_hits, preferred_element_type=jnp.float32)
    slot_index = jnp.sum(earlier * expert_hits.astype(jnp.float32), axis=1).astype(jnp.int32)
    place_index = flat_routes * capacity + slot_index
    chosen = (place_index[:, None] == jnp.arange(places, dtype=jnp.int32)[None, :]).astype(
        jnp.bfloat16
    )
    picker = jnp.sum(chosen.reshape(token_count, TOP, places), axis=1)
    contract_rows = (((0,), (0,)), ((), ()))
    send_rows = lax.dot_general(picker, attended, contract_rows, preferred_element_type=jnp.float32)
    send_rows = send_rows.astype(jnp.bfloat16).reshape(experts_all, capacity, row_width)
    send_grads = lax.dot_general(
        picker, grad_out, contract_rows, preferred_element_type=jnp.float32
    )
    send_grads = send_grads.astype(jnp.bfloat16).reshape(experts_all, capacity, row_width)
    w_first = w_in[0]
    w_second = w_out[0]
    rows_in = lax.all_to_all(send_rows, "exp", split_axis=0, concat_axis=0, tiled=True)
    grads_in = lax.all_to_all(send_grads, "exp", split_axis=0, concat_axis=0, tiled=True)
    lead_count, item_count, width_in = rows_in.shape
    row_total = lead_count * item_count
    row_block = rows_in.reshape(row_total, width_in)
    grad_block = grads_in.reshape(row_total, width_in)
    row_float = row_block.astype(jnp.float32)
    raw_sums = jnp.einsum("rd,dkf->rkf", row_block, w_first, preferred_element_type=jnp.float32)
    back_sums = lax.dot_general(
        grad_block, w_second, (((1,), (1,)), ((), ())), preferred_element_type=jnp.float32
    )
    squares = jnp.sum(row_float * row_float, axis=1)
    square_tile = jnp.broadcast_to(squares[:, None, None], (row_total, 1, head_devices))
    raw_part = lax.psum_scatter(raw_sums, "head", scatter_dimension=2, tiled=True)
    back_part = lax.psum_scatter(back_sums[:, None, :], "head", scatter_dimension=2, tiled=True)
    square_part = lax.psum_scatter(square_tile, "head", scatter_dimension=2, tiled=True)
    norm_scale = lax.rsqrt(square_part[:, 0] / D + norm_eps)
    gate_value = raw_part[:, 0] * norm_scale
    up_value = raw_part[:, 1] * norm_scale
    back_value = back_part[:, 0]
    gate_sigmoid = jax.nn.sigmoid(gate_value)
    gate_silu = gate_value * gate_sigmoid
    act_part = (gate_silu * up_value).astype(jnp.bfloat16)
    grad_gate = back_value * up_value * gate_sigmoid * (1.0 + gate_value * (1.0 - gate_sigmoid))
    grad_up = back_value * gate_silu
    grad_part = jnp.stack([grad_gate, grad_up], axis=1).astype(jnp.bfloat16)
    inner_part = jnp.sum(
        grad_part.astype(jnp.float32) * jnp.stack([gate_value, up_value], axis=1), axis=(1, 2)
    )
    act_whole = lax.all_gather(act_part[:, None, :], "head", axis=2, tiled=True)
    grad_hidden = lax.all_gather(grad_part, "head", axis=2, tiled=True)
    hidden_act = act_whole[:, 0]
    inner_sum = lax.psum(inner_part, "head")
    out_rows = jnp.dot(hidden_act, w_second, preferred_element_type=jnp.float32).astype(
        jnp.bfloat16
    )
    grad_normed = jnp.einsum(
        "rkf,dkf->rd", grad_hidden, w_first, preferred_element_type=jnp.float32
    )
    grad_rows = (
        norm_scale * grad_normed - row_float * (norm_scale * norm_scale / D) * inner_sum[:, None]
    )
    expert_out = out_rows.reshape(lead_count, item_count, width_in)
    expert_grad = grad_rows.astype(jnp.bfloat16).reshape(lead_count, item_count, width_in)
    came_out, came_grad = (
        lax.all_to_all(expert_out, "exp", split_axis=0, concat_axis=0, tiled=True),
        lax.all_to_all(expert_grad, "exp", split_axis=0, concat_axis=0, tiled=True),
    )
    picked_out = came_out.reshape(places, row_width)[place_index].reshape(
        token_count, TOP, row_width
    )
    picked_grad = came_grad.reshape(places, row_width)[place_index].reshape(
        token_count, TOP, row_width
    )
    output = attended.astype(jnp.float32) + jnp.sum(
        route_weights[:, :, None] * picked_out.astype(jnp.float32), axis=1
    )
    grad_attended = grad_out.astype(jnp.float32) + jnp.sum(
        route_weights[:, :, None] * picked_grad.astype(jnp.float32), axis=1
    )
    return (output.astype(jnp.bfloat16), grad_attended.astype(jnp.bfloat16))


LANES = 128
EXACT = (((1,), (1,)), ((), ()))


def three_parts(value):
    high = value.astype(jnp.bfloat16)
    rest = value - high.astype(jnp.float32)
    middle = rest.astype(jnp.bfloat16)
    low = (rest - middle.astype(jnp.float32)).astype(jnp.bfloat16)
    return high, middle, low


def ring_place(index, count):
    outer, inner = index // 2, index % 2
    return outer + inner * (count - 1 - 2 * outer)


def ring_index(place, count):
    inner = place // (count // 2)
    return 2 * (place + inner * (count - 1 - 2 * place)) + inner


def ring_lanes(count):
    reach = count // 2
    return ((0, 0, reach), (1, 1, reach), (0, 1, reach - 1), (1, 0, reach - 1))


def slot_of(distance, count):
    if distance == 0:
        return 0
    if abs(distance) == count // 2:
        return count - 1
    return 2 * distance - 1 if distance > 0 else -2 * distance


def wide(value, width):
    return jnp.concatenate([value] * (width // value.shape[1]), axis=1)


def fused_kernel(
    count,
    q_ref,
    k_ref,
    v_ref,
    w_in_ref,
    w_out_ref,
    routes_ref,
    share_ref,
    grad_ref,
    results_ref,
    w_pairs,
    w_up,
    w_down,
    kv_all,
    grads,
    rows,
    tables,
    squares,
    head_squares,
    gains,
    scales,
    sum_raw,
    sum_back,
    near_raw,
    near_back,
    near_raw_in,
    near_back_in,
    far_raw,
    far_back,
    far_raw_in,
    far_back_in,
    act,
    act_in,
    parts,
    held,
    load_sem,
    send_sem,
    early_recv,
    wave_recv,
    scatter_recv,
    meta_recv,
    head_recv,
    pair_recv,
):
    reach = count // 2
    tokens, width = q_ref.shape
    cached, kv_width = k_ref.shape
    side = w_down.shape[1]
    experts = tables.shape[1]
    half = tokens // 2
    quarter = half // 2
    me = lax.axis_index("exp")
    place = ring_place(me, count)
    head = lax.axis_index("head")
    core = head % 2
    mate = head + 1 - 2 * core
    across = (head + 2) % 4
    corner = 3 - head
    others = (ring_index((place + 1) % count, count), ring_index((place + count - 1) % count, count))
    distances = [0] + [d for s in range(1, reach) for d in (s, -s)] + [reach]
    lanes = []
    for way, sub, steps in ring_lanes(count):
        lanes.append((way, sub, steps, sum(lane[2] for lane in lanes)))

    def remote(source, target, kind, recv_sem, where):
        return pltpu.make_async_remote_copy(
            src_ref=source,
            dst_ref=target,
            send_sem=send_sem.at[kind],
            recv_sem=recv_sem,
            device_id=where,
            device_id_type=pl.DeviceIdType.MESH,
        )

    def begin(*what):
        copy = remote(*what)
        copy.start()
        return copy

    load_in = pltpu.make_async_copy(w_in_ref.at[0], w_pairs, load_sem.at[0])
    load_out = pltpu.make_async_copy(w_out_ref, w_down, load_sem.at[1])
    load_in.start()
    load_out.start()

    barrier = pltpu.get_barrier_semaphore()
    for other in (mate, across, corner):
        pl.semaphore_signal(
            barrier, inc=1, device_id={"head": other}, device_id_type=pl.DeviceIdType.MESH
        )
    for distance in distances[1:]:
        other = ring_index((place + distance + count) % count, count)
        pl.semaphore_signal(
            barrier, inc=1, device_id={"exp": other}, device_id_type=pl.DeviceIdType.MESH
        )

    kv_all[0, 0] = k_ref[...]
    kv_all[0, 1] = v_ref[...]
    grads[:, 0:half, :] = grad_ref[...]
    expert_row = lax.broadcasted_iota(jnp.int32, (experts, tokens), 0)
    table = jnp.zeros((experts, tokens), jnp.float32)
    for k in range(routes_ref.shape[0]):
        table = table + jnp.where(expert_row == routes_ref[k : k + 1, :], share_ref[k : k + 1, :], 0.0)
    tables[0] = table
    pl.semaphore_wait(barrier, 3 + count - 1)

    early = {}

    def advance(step):
        for way in range(2):
            if step >= 1:
                early[way, step - 1].wait_recv()
            if step < reach:
                sign = -1 if way == 0 else 1
                here, there = slot_of(sign * step, count), slot_of(sign * (step + 1), count)
                halved = step == reach - 1
                early[way, step] = begin(
                    kv_all.at[here, way] if halved else kv_all.at[here],
                    kv_all.at[there, way] if halved else kv_all.at[there],
                    0,
                    early_recv.at[way, step],
                    {"exp": others[way]},
                )

    moving = {}

    def advance_wave(kind, wave, step, subs=(0, 1)):
        store = rows if kind else grads
        for way, sub, steps, first in lanes:
            if sub not in subs:
                continue
            if 1 <= step <= steps:
                moving[kind, wave, way, sub, step - 1].wait_recv()
            if step < steps:
                sign = -1 if way == 0 else 1
                there = slot_of(sign * (step + 1), count) * half + sub * quarter
                here = slot_of(sign * step, count) * half + sub * quarter
                moving[kind, wave, way, sub, step] = begin(
                    store.at[wave, pl.ds(here, quarter)],
                    store.at[wave, pl.ds(there, quarter)],
                    1 + 2 * kind + wave,
                    wave_recv.at[kind, wave, first + step],
                    {"exp": others[way]},
                )

    def broadcast(kind, store):
        copies = []
        for distance in distances[1:]:
            there = slot_of(-distance, count)
            other = ring_index((place + distance + count) % count, count)
            copies.append(
                begin(
                    store.at[0],
                    store.at[there],
                    7 + kind,
                    meta_recv.at[kind, there - 1],
                    {"exp": other},
                )
            )
        return copies

    def split():
        load_in.wait()
        chunk = LANES
        to = lax.broadcasted_iota(jnp.int32, (2 * chunk, 2 * chunk), 0)
        source = lax.broadcasted_iota(jnp.int32, (2 * chunk, 2 * chunk), 1)
        picks = (source == jnp.where(to < chunk, 2 * to, 2 * to - 2 * chunk + 1)).astype(jnp.bfloat16)

        def split_chunk(index, carry):
            span = pl.ds(pl.multiple_of(index * chunk, chunk), chunk)
            pairs = w_pairs[span].reshape(2 * chunk, 2 * side)
            apart = jnp.dot(picks, pairs, preferred_element_type=jnp.float32).astype(jnp.bfloat16)
            for part in range(2):
                cols = slice(part * side, (part + 1) * side)
                w_up[part, span, :side] = apart[:chunk, cols]
                w_up[part, span, side:] = apart[chunk:, cols]
            return carry

        lax.fori_loop(0, width // chunk, split_chunk, 0)
        load_out.wait()

    pairs = {}

    def pair_begin(kind, wave, slot, blocks, source, target, other):
        span = pl.ds(slot * half, blocks * half)
        pairs[kind, wave, slot] = begin(
            source.at[wave, span],
            target.at[wave, span],
            9 + kind,
            pair_recv.at[len(pairs)],
            {"head": other},
        )

    def back(wave, slot, blocks):
        span = slice(slot * half, (slot + blocks) * half)
        weights = jnp.concatenate([w_down[1 - core], w_down[core]], axis=0)
        both = lax.dot_general(
            grads[wave, span, :], weights, EXACT, preferred_element_type=jnp.float32
        )
        near_back[wave, span, :] = both[:, :side].astype(jnp.bfloat16)
        pair_begin(0, wave, slot, blocks, near_back, near_back_in, mate)
        sum_back[wave, span, :] = both[:, side:]

    def raw(wave, slot, blocks):
        span = slice(slot * half, (slot + blocks) * half)
        block = rows[wave, span, :]
        near_raw[wave, span, :] = jnp.dot(
            block, w_up[1 - core], preferred_element_type=jnp.float32
        ).astype(jnp.bfloat16)
        pair_begin(1, wave, slot, blocks, near_raw, near_raw_in, mate)
        sum_raw[wave, span, :] = jnp.dot(block, w_up[core], preferred_element_type=jnp.float32)

    def far(kind, wave, slot, blocks):
        total, near_in = ((sum_back, near_back_in), (sum_raw, near_raw_in))[kind]
        out, target = ((far_back, far_back_in), (far_raw, far_raw_in))[kind]
        span = slice(slot * half, (slot + blocks) * half)
        pairs[kind, wave, slot].wait_recv()
        both = total[wave, span, :] + near_in[wave, span, :].astype(jnp.float32)
        total[wave, span, :] = both
        out[wave, span, :] = both.astype(jnp.bfloat16)
        pair_begin(2 + kind, wave, slot, blocks, out, target, across)

    def attention():
        heads = width // HEAD_WIDTH
        together = heads // (kv_width // HEAD_WIDTH)
        every = count * cached
        column = lax.broadcasted_iota(jnp.int32, (1, every), 1)
        first = jnp.zeros((1, every), jnp.int32)
        for slot, distance in enumerate(distances):
            owner = ring_index((place + distance + count) % count, count)
            first = jnp.where(column // cached == slot, (owner - slot) * cached, first)
        row_pos = (
            count * (cached - tokens)
            + me * tokens
            + lax.broadcasted_iota(jnp.int32, (tokens, every), 0)
        )
        visible = jnp.broadcast_to(first + column, (tokens, every)) <= row_pos
        total = jnp.zeros((tokens, LANES), jnp.float32)
        for one in range(heads):
            cols = slice(one * HEAD_WIDTH, (one + 1) * HEAD_WIDTH)
            kv_cols = slice(one // together * HEAD_WIDTH, (one // together + 1) * HEAD_WIDTH)
            scores = lax.dot_general(
                q_ref[:, cols],
                kv_all[:, 0, :, kv_cols].reshape(every, HEAD_WIDTH),
                EXACT,
                preferred_element_type=jnp.float32,
            ) * HEAD_WIDTH ** (-0.5)
            scores = jnp.where(visible, scores, hidden_logits)
            best = jnp.max(scores, axis=1, keepdims=True)
            weights = jnp.exp(scores - best)
            weight_total = jnp.sum(weights, axis=1, keepdims=True)
            sums = jnp.dot(
                weights.astype(jnp.bfloat16),
                kv_all[:, 1, :, kv_cols].reshape(every, HEAD_WIDTH),
                preferred_element_type=jnp.float32,
            )
            mixed = (sums / weight_total).astype(jnp.bfloat16)
            rows[0, 0:half, cols] = mixed[:half]
            rows[1, 0:half, cols] = mixed[half:]
            mixed = mixed.astype(jnp.float32)
            total = total + mixed * mixed
        return total

    def share_squares(total):
        columns = jnp.broadcast_to(jnp.sum(total, axis=1, keepdims=True), (tokens, LANES))
        head_squares[0] = jnp.transpose(columns)[: head_squares.shape[1]]
        return [
            begin(
                head_squares.at[0],
                head_squares.at[index + 1],
                14,
                head_recv.at[index],
                {"head": other},
            )
            for index, other in enumerate((mate, across, corner))
        ]

    def spread_squares(copies):
        for each in copies:
            each.wait_recv()
        squares[0] = (head_squares[0] + head_squares[1]) + (head_squares[2] + head_squares[3])
        return broadcast(1, squares)

    def fill(store, slot, row):
        columns = jnp.transpose(jnp.broadcast_to(row, (LANES, tokens)))
        for wave in range(2):
            store[wave, slot * half : (slot + 1) * half, :] = columns[wave * half : (wave + 1) * half]

    def fill_gains(copies):
        for each in copies:
            each.wait_recv()
        for slot in range(count):
            row = jnp.sum(jnp.where(expert_row == me, tables[slot], 0.0), axis=0, keepdims=True)
            fill(gains, slot, row)

    def fill_scales(copies):
        for each in copies:
            each.wait_recv()
        for slot in range(count):
            fill(scales, slot, lax.rsqrt(squares[slot][0:1, :] / D + norm_eps))

    def activate(wave, slot, blocks):
        for kind in (2, 3):
            for one in range(slot, slot + blocks):
                if (kind, wave, one) in pairs:
                    pairs[kind, wave, one].wait_recv()
        step = 32
        lane = lax.broadcasted_iota(jnp.int32, (step, LANES), 1)

        def some_rows(index, carry):
            span = pl.ds(pl.multiple_of(slot * half + index * step, step), step)
            scale = scales[wave, span, :]
            gain = gains[wave, span, :]
            inner = jnp.zeros((step, LANES), jnp.float32)
            for start in range(0, side, LANES):
                cols = slice(start, start + LANES)
                up_cols = slice(side + start, side + start + LANES)
                down_cols = slice(2 * side + start, 2 * side + start + LANES)
                gate = sum_raw[wave, span, cols] + far_raw_in[wave, span, cols].astype(jnp.float32)
                up = sum_raw[wave, span, up_cols] + far_raw_in[wave, span, up_cols].astype(
                    jnp.float32
                )
                gate, up = gate * scale, up * scale
                back_value = sum_back[wave, span, cols] + far_back_in[wave, span, cols].astype(
                    jnp.float32
                )
                sigmoid = jax.nn.sigmoid(gate)
                silu = gate * sigmoid
                grad_gate = back_value * up * sigmoid * (1.0 + gate * (1.0 - sigmoid))
                grad_up = back_value * silu
                inner = inner + (grad_gate * gate + grad_up * up)
                act[wave, span, cols] = (gain * (silu * up)).astype(jnp.bfloat16)
                act[wave, span, up_cols] = (gain * scale * grad_gate).astype(jnp.bfloat16)
                act[wave, span, down_cols] = (gain * scale * grad_up).astype(jnp.bfloat16)
            high, middle, low = three_parts(
                jnp.broadcast_to(jnp.sum(inner, axis=1, keepdims=True), (step, LANES))
            )
            zero = jnp.zeros((step, LANES), jnp.float32)
            spread = jnp.where(lane == 0, high.astype(jnp.float32), zero)
            spread = jnp.where(lane == 1, middle.astype(jnp.float32), spread)
            spread = jnp.where(lane == 2, low.astype(jnp.float32), spread)
            act[wave, span, 3 * side :] = spread.astype(jnp.bfloat16)
            return carry

        lax.fori_loop(0, blocks * half // step, some_rows, 0)
        pair_begin(4, wave, slot, blocks, act, act_in, mate)

    def finish(wave, slot, blocks):
        span = slice(slot * half, (slot + blocks) * half)
        pairs[4, wave, slot].wait_recv()
        inner = jnp.sum(
            act[wave, span, 3 * side :].astype(jnp.float32)
            + act_in[wave, span, 3 * side :].astype(jnp.float32),
            axis=1,
            keepdims=True,
        )
        tile = 256
        scale = scales[wave, span, :]
        bent = wide(gains[wave, span, :] * (scale * scale / D) * inner, tile)
        hidden = slice(0, side)
        slopes = slice(side, 3 * side)
        act_all = jnp.concatenate([act[wave, span, hidden], act_in[wave, span, hidden]], axis=1)
        for start in range(0, width, tile):
            cols = slice(start, start + tile)
            weights = jnp.concatenate([w_down[core, :, cols], w_down[1 - core, :, cols]], axis=0)
            out = jnp.dot(act_all, weights, preferred_element_type=jnp.float32)
            parts[wave, span, cols] = out.astype(jnp.bfloat16)
            grad = lax.dot_general(
                act[wave, span, slopes],
                w_up[core, cols, :],
                EXACT,
                preferred_element_type=jnp.float32,
            ) + lax.dot_general(
                act_in[wave, span, slopes],
                w_up[1 - core, cols, :],
                EXACT,
                preferred_element_type=jnp.float32,
            )
            grad = grad - bent * rows[wave, span, cols].astype(jnp.float32)
            parts[wave, span, width + start : width + start + tile] = grad.astype(jnp.bfloat16)

    sums = {}

    def scatter(wave, step):
        for way, sub, steps, first in lanes:
            if step >= steps:
                continue
            sign = 1 if way == 0 else -1
            start = slot_of(sign * (steps - step), count) * half + sub * quarter
            block = parts.at[wave, pl.ds(start, quarter)]
            there = pl.ds(sub * quarter, quarter)
            if step > 0:
                sums[wave, way, sub, step - 1].wait_recv()
                arrived = held.at[wave, way, step - 1, there]
                arrived[...] = (
                    arrived[...].astype(jnp.float32) + block[...].astype(jnp.float32)
                ).astype(jnp.bfloat16)
                block = arrived
            sums[wave, way, sub, step] = begin(
                block,
                held.at[wave, way, step, there],
                5 + wave,
                scatter_recv.at[wave, first + step],
                {"exp": others[way]},
            )

    def settle(wave):
        for sub in range(2):
            span = slice(sub * quarter, (sub + 1) * quarter)
            target = slice(wave * half + sub * quarter, wave * half + (sub + 1) * quarter)
            value = parts[wave, span, :].astype(jnp.float32)
            for way, lane_sub, steps, first in lanes:
                if lane_sub == sub:
                    sums[wave, way, sub, steps - 1].wait_recv()
                    value = value + held[wave, way, steps - 1, span, :].astype(jnp.float32)
            results_ref[target, :] = (
                rows[wave, span, :].astype(jnp.float32) + value[:, :width]
            ).astype(jnp.bfloat16)
            results_ref[slice(tokens + target.start, tokens + target.stop), :] = (
                grad_ref[wave, span, :].astype(jnp.float32) + value[:, width:]
            ).astype(jnp.bfloat16)

    def drain():
        others_of = pl.ds(half, (count - 1) * half)
        for kind, sent in enumerate(
            (
                kv_all.at[pl.ds(1, count - 1)],
                grads.at[0, others_of],
                grads.at[1, others_of],
                rows.at[0, others_of],
                rows.at[1, others_of],
                parts.at[0, others_of],
                parts.at[1, others_of],
                tables.at[pl.ds(1, count - 1)],
                squares.at[pl.ds(1, count - 1)],
                near_back,
                near_raw,
                far_back,
                far_raw,
                act,
                head_squares.at[pl.ds(1, 3)],
            )
        ):
            remote(sent, sent, kind, load_sem.at[0], {"head": mate}).wait_send()

    first = (0, 3)
    between = [(2 * step - 1, 2) for step in range(2, reach - 1)]
    last = (2 * reach - 3, 3)
    advance(0)
    advance_wave(0, 0, 0)
    table_copies = broadcast(0, tables)
    split()
    advance(1)
    advance_wave(0, 0, 1)
    back(0, *first)
    advance(2)
    far(0, 0, *first)
    advance_wave(0, 0, 2)
    for step in range(3, reach):
        back(0, *between[step - 3])
        advance(step)
        far(0, 0, *between[step - 3])
        advance_wave(0, 0, step)
    advance(reach)
    advance_wave(0, 1, 0)
    square_total = attention()
    advance_wave(1, 0, 0)
    square_copies = share_squares(square_total)
    advance_wave(0, 0, reach)
    back(0, *last)
    advance_wave(0, 1, 1, (0,))
    raw(0, 0, 1)
    far(0, 0, *last)
    square_copies = spread_squares(square_copies)
    far(1, 0, 0, 1)
    advance_wave(1, 0, 1)
    raw(0, 1, 2)
    advance_wave(0, 1, 2, (0,))
    advance_wave(1, 0, 2)
    far(1, 0, 1, 2)
    for unit in between[:1]:
        raw(0, *unit)
    advance_wave(1, 0, 3)
    for unit in between[:1]:
        far(1, 0, *unit)
    advance_wave(0, 1, 3, (0,))
    advance_wave(1, 1, 0)
    for step in range(4, reach + 1):
        advance_wave(1, 0, step)
        for unit in between[step - 3 : step - 2]:
            raw(0, *unit)
            far(1, 0, *unit)
    raw(0, *last)
    advance_wave(0, 1, 1, (1,))
    back(1, *first)
    far(1, 0, *last)
    advance_wave(1, 1, 1)
    for step in range(4, reach + 1):
        advance_wave(0, 1, step, (0,))
    fill_gains(table_copies)
    fill_scales(square_copies)
    far(0, 1, *first)
    advance_wave(0, 1, 2, (1,))
    activate(0, *first)
    advance_wave(1, 1, 2)
    raw(1, *first)
    activate(0, *last)
    for step in range(3, reach):
        advance_wave(0, 1, step, (1,))
    far(1, 1, *first)
    for unit in between:
        activate(0, *unit)
    finish(0, *last)
    for step in range(3, reach):
        advance_wave(1, 1, step)
    scatter(0, 0)
    for unit in between:
        back(1, *unit)
        finish(0, *unit)
        far(0, 1, *unit)
    advance_wave(0, 1, reach, (1,))
    back(1, *last)
    advance_wave(1, 1, reach)
    raw(1, *last)
    far(0, 1, *last)
    finish(0, *first)
    far(1, 1, *last)
    for unit in between:
        raw(1, *unit)
    scatter(0, 1)
    for unit in between:
        far(1, 1, *unit)
    activate(1, *first)
    finish(1, *first)
    scatter(0, 2)
    activate(1, *last)
    finish(1, *last)
    for step in range(3, reach):
        scatter(0, step)
    scatter(1, 0)
    for unit in between:
        activate(1, *unit)
        finish(1, *unit)
    settle(0)
    for step in range(1, reach):
        scatter(1, step)
    settle(1)
    drain()


def fused_device(queries, keys, values, w_in, w_out, routes, route_weights, grad_out):
    count = lax.axis_size("exp")
    tokens, width = queries.shape
    cached, kv_width = keys.shape
    hidden = w_in.shape[3]
    side = hidden // 2
    reach = count // 2
    half_rows = tokens // 2
    every = count * half_rows
    experts = w_in.shape[0] * count

    def body(*refs):
        fused_kernel(count, *refs)

    def half(*shape):
        return pltpu.VMEM(shape, jnp.bfloat16)

    def whole(*shape):
        return pltpu.VMEM(shape, jnp.float32)

    dma = pltpu.SemaphoreType.DMA
    vmem = pl.BlockSpec(memory_space=pltpu.VMEM)
    anywhere = pl.BlockSpec(memory_space=pl.ANY)
    both = pl.pallas_call(
        body,
        out_shape=jax.ShapeDtypeStruct((2 * tokens, width), jnp.bfloat16),
        in_specs=[vmem, vmem, vmem, anywhere, anywhere, vmem, vmem, vmem],
        out_specs=vmem,
        scratch_shapes=[
            half(width, 2, hidden),
            half(2, width, hidden),
            half(2, side, width),
            half(count, 2, cached, kv_width),
            half(2, every, width),
            half(2, every, width),
            whole(count, experts, tokens),
            whole(count, 8, tokens),
            whole(4, 8, tokens),
            whole(2, every, LANES),
            whole(2, every, LANES),
            whole(2, every, hidden),
            whole(2, every, side),
            half(2, every, hidden),
            half(2, every, side),
            half(2, every, hidden),
            half(2, every, side),
            half(2, every, hidden),
            half(2, every, side),
            half(2, every, hidden),
            half(2, every, side),
            half(2, every, 3 * side + LANES),
            half(2, every, 3 * side + LANES),
            half(2, every, 2 * width),
            half(2, 2, reach, half_rows, 2 * width),
            dma((2,)),
            dma((15,)),
            dma((2, reach)),
            dma((2, 2, 4 * reach - 2)),
            dma((2, 4 * reach - 2)),
            dma((2, count - 1)),
            dma((3,)),
            dma((5 * 2 * (reach - 1) + 2,)),
        ],
        compiler_params=pltpu.CompilerParams(
            collective_id=1, has_side_effects=True, vmem_limit_bytes=60 * 1024 * 1024
        ),
        name="fused",
    )(
        queries,
        keys,
        values,
        w_in,
        w_out[0].reshape(2, side, width),
        routes.T,
        route_weights.T,
        grad_out.reshape(2, half_rows, width),
    )
    return both[:tokens], both[tokens:]


def solution(mesh):
    fused = 2 * TOP >= mesh.shape["exp"] and mesh.shape["exp"] == 8 and mesh.shape["head"] == 4
    in_specs = (
        P("exp", "head"),
        P("exp", "head"),
        P("exp", "head"),
        P("exp", "head", None, None),
        P("exp", None, "head"),
        P("exp", None),
        P("exp", None),
        P("exp", "head"),
    )
    out_specs = (P("exp", "head"), P("exp", "head"))
    return jax.shard_map(
        fused_device if fused else per_device, mesh=mesh, in_specs=in_specs, out_specs=out_specs, check_vma=False
    )
```

```python
import jax
import jax.numpy as jnp
from jax import lax
from jax.experimental import pallas as pl
from jax.experimental.pallas import tpu as pltpu
from jax.sharding import PartitionSpec as P

D = 4096
HEAD_WIDTH = 128
TOP = 6


norm_eps = 1e-05
hidden_logits = -1e30


def block_partial(query_rows, query_pos, rows_of_keys, value_rows, key_pos):
    row_count = query_rows.shape[0]
    count_of_blocks = rows_of_keys.shape[0]
    kv_heads = rows_of_keys.shape[2] // HEAD_WIDTH
    grouping_width = query_rows.shape[1] // HEAD_WIDTH // kv_heads
    heads_of_queries = query_rows.reshape(row_count, kv_heads, grouping_width, HEAD_WIDTH)
    key_heads = rows_of_keys.reshape(count_of_blocks, -1, kv_heads, HEAD_WIDTH)
    value_heads = value_rows.reshape(count_of_blocks, -1, kv_heads, HEAD_WIDTH)
    visible = (key_pos[:, None, :] <= query_pos[None, :, None])[:, :, None, None, :]
    scores = jnp.einsum(
        "tgid,bjgd->btgij", heads_of_queries, key_heads, preferred_element_type=jnp.float32
    ) * HEAD_WIDTH ** (-0.5)
    scores = jnp.where(visible, scores, hidden_logits)
    best_score = jnp.max(scores, axis=-1).astype(jnp.bfloat16)
    weights = jnp.where(visible, jnp.exp(scores - best_score.astype(jnp.float32)[..., None]), 0.0)
    weight_total = jnp.sum(weights, axis=-1).astype(jnp.bfloat16)
    weighted_sum = jnp.einsum(
        "btgij,bjgd->btgid",
        weights.astype(jnp.bfloat16),
        value_heads,
        preferred_element_type=jnp.float32,
    ).astype(jnp.bfloat16)
    head_count = kv_heads * grouping_width
    return (
        best_score.reshape(count_of_blocks, row_count, head_count),
        weight_total.reshape(count_of_blocks, row_count, head_count),
        weighted_sum.reshape(count_of_blocks, row_count, head_count * HEAD_WIDTH),
    )


def fold_partials(running, best_score, weight_total, weighted_sum):
    top_now, total_now, sums_now = running
    best_value = best_score.astype(jnp.float32)
    new_top = jnp.maximum(top_now, jnp.max(best_value, axis=0))
    old_factor = jnp.exp(top_now - new_top)
    block_factor = jnp.exp(best_value - new_top[None])
    total_next = total_now * old_factor + jnp.sum(
        weight_total.astype(jnp.float32) * block_factor, axis=0
    )
    spread_sums = weighted_sum.reshape(
        weighted_sum.shape[0], sums_now.shape[0], sums_now.shape[1], HEAD_WIDTH
    )
    sums_next = sums_now * old_factor[..., None] + jnp.sum(
        spread_sums.astype(jnp.float32) * block_factor[..., None], axis=0
    )
    return (new_top, total_next, sums_next)


def per_device(queries, keys, values, w_in, w_out, routes, route_weights, grad_out):
    exp_count = lax.axis_size("exp")
    exp_index = lax.axis_index("exp")
    head_devices = lax.axis_size("head")
    token_count = queries.shape[0]
    query_width = queries.shape[1]
    head_count = query_width // HEAD_WIDTH
    cache_rows = keys.shape[0]
    window = token_count * exp_count
    offset = cache_rows * exp_count - window
    beginning = (
        jnp.full((token_count, head_count), hidden_logits, jnp.float32),
        jnp.zeros((token_count, head_count), jnp.float32),
        jnp.zeros((token_count, head_count, HEAD_WIDTH), jnp.float32),
    )
    own_pos = offset + exp_index * token_count + jnp.arange(token_count, dtype=jnp.int32)
    key_piece = lax.all_gather(keys, "exp", axis=0, tiled=True)
    value_piece = lax.all_gather(values, "exp", axis=0, tiled=True)
    piece_blocks = key_piece.shape[0] // cache_rows
    key_split = key_piece.reshape(piece_blocks, cache_rows, -1)
    value_split = value_piece.reshape(piece_blocks, cache_rows, -1)
    pos_split = jnp.arange(key_piece.shape[0], dtype=jnp.int32).reshape(piece_blocks, cache_rows)

    def one_block(state, element):
        key_block, value_block, pos_block = element
        block_parts = block_partial(
            queries, own_pos, key_block[None], value_block[None], pos_block[None]
        )
        return (fold_partials(state, block_parts[0], block_parts[1], block_parts[2]), None)

    state, ignored = lax.scan(one_block, beginning, (key_split, value_split, pos_split))
    attended = (
        (state[2] / state[1][..., None]).reshape(token_count, query_width).astype(jnp.bfloat16)
    )
    row_width = attended.shape[1]
    experts_all = w_in.shape[0] * exp_count
    mean_load = TOP * token_count // experts_all
    capacity = mean_load + mean_load // 6
    places = experts_all * capacity
    flat_routes = routes.reshape(-1)
    expert_hits = (
        flat_routes[:, None] == jnp.arange(experts_all, dtype=jnp.int32)[None, :]
    ).astype(jnp.bfloat16)
    before = jnp.tri(flat_routes.shape[0], k=-1, dtype=jnp.bfloat16)
    earlier = jnp.dot(before, expert_hits, preferred_element_type=jnp.float32)
    slot_index = jnp.sum(earlier * expert_hits.astype(jnp.float32), axis=1).astype(jnp.int32)
    place_index = flat_routes * capacity + slot_index
    chosen = (place_index[:, None] == jnp.arange(places, dtype=jnp.int32)[None, :]).astype(
        jnp.bfloat16
    )
    picker = jnp.sum(chosen.reshape(token_count, TOP, places), axis=1)
    contract_rows = (((0,), (0,)), ((), ()))
    send_rows = lax.dot_general(picker, attended, contract_rows, preferred_element_type=jnp.float32)
    send_rows = send_rows.astype(jnp.bfloat16).reshape(experts_all, capacity, row_width)
    send_grads = lax.dot_general(
        picker, grad_out, contract_rows, preferred_element_type=jnp.float32
    )
    send_grads = send_grads.astype(jnp.bfloat16).reshape(experts_all, capacity, row_width)
    w_first = w_in[0]
    w_second = w_out[0]
    rows_in = lax.all_to_all(send_rows, "exp", split_axis=0, concat_axis=0, tiled=True)
    grads_in = lax.all_to_all(send_grads, "exp", split_axis=0, concat_axis=0, tiled=True)
    lead_count, item_count, width_in = rows_in.shape
    row_total = lead_count * item_count
    row_block = rows_in.reshape(row_total, width_in)
    grad_block = grads_in.reshape(row_total, width_in)
    row_float = row_block.astype(jnp.float32)
    raw_sums = jnp.einsum("rd,dkf->rkf", row_block, w_first, preferred_element_type=jnp.float32)
    back_sums = lax.dot_general(
        grad_block, w_second, (((1,), (1,)), ((), ())), preferred_element_type=jnp.float32
    )
    squares = jnp.sum(row_float * row_float, axis=1)
    square_tile = jnp.broadcast_to(squares[:, None, None], (row_total, 1, head_devices))
    raw_part = lax.psum_scatter(raw_sums, "head", scatter_dimension=2, tiled=True)
    back_part = lax.psum_scatter(back_sums[:, None, :], "head", scatter_dimension=2, tiled=True)
    square_part = lax.psum_scatter(square_tile, "head", scatter_dimension=2, tiled=True)
    norm_scale = lax.rsqrt(square_part[:, 0] / D + norm_eps)
    gate_value = raw_part[:, 0] * norm_scale
    up_value = raw_part[:, 1] * norm_scale
    back_value = back_part[:, 0]
    gate_sigmoid = jax.nn.sigmoid(gate_value)
    gate_silu = gate_value * gate_sigmoid
    act_part = (gate_silu * up_value).astype(jnp.bfloat16)
    grad_gate = back_value * up_value * gate_sigmoid * (1.0 + gate_value * (1.0 - gate_sigmoid))
    grad_up = back_value * gate_silu
    grad_part = jnp.stack([grad_gate, grad_up], axis=1).astype(jnp.bfloat16)
    inner_part = jnp.sum(
        grad_part.astype(jnp.float32) * jnp.stack([gate_value, up_value], axis=1), axis=(1, 2)
    )
    act_whole = lax.all_gather(act_part[:, None, :], "head", axis=2, tiled=True)
    grad_hidden = lax.all_gather(grad_part, "head", axis=2, tiled=True)
    hidden_act = act_whole[:, 0]
    inner_sum = lax.psum(inner_part, "head")
    out_rows = jnp.dot(hidden_act, w_second, preferred_element_type=jnp.float32).astype(
        jnp.bfloat16
    )
    grad_normed = jnp.einsum(
        "rkf,dkf->rd", grad_hidden, w_first, preferred_element_type=jnp.float32
    )
    grad_rows = (
        norm_scale * grad_normed - row_float * (norm_scale * norm_scale / D) * inner_sum[:, None]
    )
    expert_out = out_rows.reshape(lead_count, item_count, width_in)
    expert_grad = grad_rows.astype(jnp.bfloat16).reshape(lead_count, item_count, width_in)
    came_out, came_grad = (
        lax.all_to_all(expert_out, "exp", split_axis=0, concat_axis=0, tiled=True),
        lax.all_to_all(expert_grad, "exp", split_axis=0, concat_axis=0, tiled=True),
    )
    picked_out = came_out.reshape(places, row_width)[place_index].reshape(
        token_count, TOP, row_width
    )
    picked_grad = came_grad.reshape(places, row_width)[place_index].reshape(
        token_count, TOP, row_width
    )
    output = attended.astype(jnp.float32) + jnp.sum(
        route_weights[:, :, None] * picked_out.astype(jnp.float32), axis=1
    )
    grad_attended = grad_out.astype(jnp.float32) + jnp.sum(
        route_weights[:, :, None] * picked_grad.astype(jnp.float32), axis=1
    )
    return (output.astype(jnp.bfloat16), grad_attended.astype(jnp.bfloat16))


LANES = 128
EXACT = (((1,), (1,)), ((), ()))


def three_parts(value):
    high = value.astype(jnp.bfloat16)
    rest = value - high.astype(jnp.float32)
    middle = rest.astype(jnp.bfloat16)
    low = (rest - middle.astype(jnp.float32)).astype(jnp.bfloat16)
    return high, middle, low


def ring_place(index, count):
    outer, inner = index // 2, index % 2
    return outer + inner * (count - 1 - 2 * outer)


def ring_index(place, count):
    inner = place // (count // 2)
    return 2 * (place + inner * (count - 1 - 2 * place)) + inner


def ring_lanes(count):
    reach = count // 2
    return ((0, 0, reach), (1, 1, reach), (0, 1, reach - 1), (1, 0, reach - 1))


def slot_of(distance, count):
    if distance == 0:
        return 0
    if abs(distance) == count // 2:
        return count - 1
    return 2 * distance - 1 if distance > 0 else -2 * distance


def wide(value, width):
    return jnp.concatenate([value] * (width // value.shape[1]), axis=1)


def fused_kernel(
    count,
    queries_ref,
    k_ref,
    v_ref,
    w_in_ref,
    w_out_ref,
    routes_in_ref,
    shares_ref,
    grad_ref,
    results_ref,
    q_ref,
    routes_ref,
    share_ref,
    w_pairs,
    w_up,
    w_down,
    kv_all,
    grads,
    rows,
    tables,
    squares,
    head_squares,
    gains,
    scales,
    sum_raw,
    sum_back,
    near_raw,
    near_back,
    near_raw_in,
    near_back_in,
    far_raw,
    far_back,
    far_raw_in,
    far_back_in,
    act,
    act_in,
    parts,
    held,
    settled,
    best_so_far,
    total_so_far,
    mix_so_far,
    load_sem,
    send_sem,
    early_recv,
    wave_recv,
    scatter_recv,
    meta_recv,
    head_recv,
    pair_recv,
):
    reach = count // 2
    tokens, width = q_ref.shape
    cached, kv_width = k_ref.shape
    side = w_down.shape[1]
    experts = tables.shape[1]
    half = tokens // 2
    quarter = half // 2
    me = lax.axis_index("exp")
    place = ring_place(me, count)
    head = lax.axis_index("head")
    core = head % 2
    mate = head + 1 - 2 * core
    across = (head + 2) % 4
    corner = 3 - head
    others = (ring_index((place + 1) % count, count), ring_index((place + count - 1) % count, count))
    distances = [0] + [d for s in range(1, reach) for d in (s, -s)] + [reach]
    lanes = ((reach, 0), (reach - 1, reach))

    def remote(source, target, kind, recv_sem, where):
        return pltpu.make_async_remote_copy(
            src_ref=source,
            dst_ref=target,
            send_sem=send_sem.at[kind],
            recv_sem=recv_sem,
            device_id=where,
            device_id_type=pl.DeviceIdType.MESH,
        )

    def begin(*what):
        copy = remote(*what)
        copy.start()
        return copy

    loads = [
        pltpu.make_async_copy(source, target, load_sem.at[index])
        for index, (source, target) in enumerate(
            (
                (k_ref, kv_all.at[0, 0]),
                (v_ref, kv_all.at[0, 1]),
                (grad_ref, grads.at[:, pl.ds(0, half)]),
                (routes_in_ref, routes_ref),
                (shares_ref, share_ref),
                (w_in_ref.at[0], w_pairs),
                (w_out_ref, w_down),
                (queries_ref, q_ref),
            )
        )
    ]
    for each in loads:
        each.start()

    barrier = pltpu.get_barrier_semaphore()
    for other in (mate, across, corner):
        pl.semaphore_signal(
            barrier, inc=1, device_id={"head": other}, device_id_type=pl.DeviceIdType.MESH
        )
    for distance in distances[1:]:
        other = ring_index((place + distance + count) % count, count)
        pl.semaphore_signal(
            barrier, inc=1, device_id={"exp": other}, device_id_type=pl.DeviceIdType.MESH
        )

    for each in loads[:5]:
        each.wait()
    expert_row = lax.broadcasted_iota(jnp.int32, (experts, tokens), 0)
    table = jnp.zeros((experts, tokens), jnp.float32)
    for k in range(routes_ref.shape[0]):
        table = table + jnp.where(expert_row == routes_ref[k : k + 1, :], share_ref[k : k + 1, :], 0.0)
    tables[0] = table
    pl.semaphore_wait(barrier, 3 + count - 1)

    def advance(step):
        if step >= 1:
            both = kv_all.at[0] if step == reach else kv_all.at[pl.ds(0, 2)]
            remote(both, both, 0, early_recv.at[step - 1], {"head": mate}).wait_recv()
        for way in range(2 if step < reach else 0):
            sign = -1 if way == 0 else 1
            here, there = slot_of(sign * step, count), slot_of(sign * (step + 1), count)
            halved = step == reach - 1
            begin(
                kv_all.at[here, way] if halved else kv_all.at[here],
                kv_all.at[there, way] if halved else kv_all.at[there],
                0,
                early_recv.at[step],
                {"exp": others[way]},
            )

    def advance_wave(kind, wave, step, pairs_of=(0, 1)):
        store = rows if kind else grads
        for pair in pairs_of:
            steps, first = lanes[pair]
            if 1 <= step <= steps:
                both = store.at[wave, pl.ds(0, half)]
                arrived = wave_recv.at[kind, wave, first + step - 1]
                remote(both, both, 0, arrived, {"head": mate}).wait_recv()
            for way in range(2 if step < steps else 0):
                sub = way if pair == 0 else 1 - way
                sign = -1 if way == 0 else 1
                there = slot_of(sign * (step + 1), count) * half + sub * quarter
                here = slot_of(sign * step, count) * half + sub * quarter
                begin(
                    store.at[wave, pl.ds(here, quarter)],
                    store.at[wave, pl.ds(there, quarter)],
                    1 + 2 * kind + wave,
                    wave_recv.at[kind, wave, first + step],
                    {"exp": others[way]},
                )

    def broadcast(kind, store):
        copies = []
        for distance in distances[1:]:
            there = slot_of(-distance, count)
            other = ring_index((place + distance + count) % count, count)
            copies.append(
                begin(
                    store.at[0],
                    store.at[there],
                    7 + kind,
                    meta_recv.at[kind, there - 1],
                    {"exp": other},
                )
            )
        return copies

    def split():
        loads[5].wait()
        chunk = LANES
        to = lax.broadcasted_iota(jnp.int32, (2 * chunk, 2 * chunk), 0)
        source = lax.broadcasted_iota(jnp.int32, (2 * chunk, 2 * chunk), 1)
        picks = (source == jnp.where(to < chunk, 2 * to, 2 * to - 2 * chunk + 1)).astype(jnp.bfloat16)

        def split_chunk(index, carry):
            span = pl.ds(pl.multiple_of(index * chunk, chunk), chunk)
            pairs = w_pairs[span].reshape(2 * chunk, 2 * side)
            apart = jnp.dot(picks, pairs, preferred_element_type=jnp.float32).astype(jnp.bfloat16)
            for part in range(2):
                cols = slice(part * side, (part + 1) * side)
                w_up[part, span, :side] = apart[:chunk, cols]
                w_up[part, span, side:] = apart[chunk:, cols]
            return carry

        lax.fori_loop(0, width // chunk, split_chunk, 0)
        loads[6].wait()
        loads[7].wait()

    pairs = {}

    def pair_begin(kind, wave, slot, blocks, source, target, other):
        span = pl.ds(slot * half, blocks * half)
        pairs[kind, wave, slot] = begin(
            source.at[wave, span],
            target.at[wave, span],
            9 + kind,
            pair_recv.at[len(pairs)],
            {"head": other},
        )

    def back(wave, slot, blocks):
        span = slice(slot * half, (slot + blocks) * half)
        weights = jnp.concatenate([w_down[1 - core], w_down[core]], axis=0)
        both = lax.dot_general(
            grads[wave, span, :], weights, EXACT, preferred_element_type=jnp.float32
        )
        near_back[wave, span, :] = both[:, :side].astype(jnp.bfloat16)
        pair_begin(0, wave, slot, blocks, near_back, near_back_in, mate)
        sum_back[wave, span, :] = both[:, side:]

    def raw(wave, slot, blocks):
        span = slice(slot * half, (slot + blocks) * half)
        block = rows[wave, span, :]
        near_raw[wave, span, :] = jnp.dot(
            block, w_up[1 - core], preferred_element_type=jnp.float32
        ).astype(jnp.bfloat16)
        pair_begin(1, wave, slot, blocks, near_raw, near_raw_in, mate)
        sum_raw[wave, span, :] = jnp.dot(block, w_up[core], preferred_element_type=jnp.float32)

    def far(kind, wave, slot, blocks):
        total, near_in = ((sum_back, near_back_in), (sum_raw, near_raw_in))[kind]
        out, target = ((far_back, far_back_in), (far_raw, far_raw_in))[kind]
        span = slice(slot * half, (slot + blocks) * half)
        pairs[kind, wave, slot].wait_recv()
        both = total[wave, span, :] + near_in[wave, span, :].astype(jnp.float32)
        total[wave, span, :] = both
        out[wave, span, :] = both.astype(jnp.bfloat16)
        pair_begin(2 + kind, wave, slot, blocks, out, target, across)

    groups = kv_width // HEAD_WIDTH
    together = width // kv_width

    def visible_in(low, high):
        size = (high - low) * cached
        column = low * cached + lax.broadcasted_iota(jnp.int32, (1, size), 1)
        shift = jnp.zeros((1, size), jnp.int32)
        for slot in range(low, high):
            owner = ring_index((place + distances[slot] + count) % count, count)
            shift = jnp.where(column // cached == slot, (owner - slot) * cached, shift)
        row_pos = (
            count * (cached - tokens)
            + me * tokens
            + lax.broadcasted_iota(jnp.int32, (tokens, size), 0)
        )
        row_pos = jnp.concatenate([row_pos] * together, axis=0)
        return jnp.broadcast_to(shift + column, row_pos.shape) <= row_pos

    def scores_in(group, low, high, visible):
        first_head = group * together
        stacked = jnp.concatenate(
            [
                q_ref[:, one * HEAD_WIDTH : (one + 1) * HEAD_WIDTH]
                for one in range(first_head, first_head + together)
            ],
            axis=0,
        )
        scores = lax.dot_general(
            stacked,
            kv_all[low:high, 0, :, group * HEAD_WIDTH : (group + 1) * HEAD_WIDTH].reshape(
                (high - low) * cached, HEAD_WIDTH
            ),
            EXACT,
            preferred_element_type=jnp.float32,
        ) * HEAD_WIDTH ** (-0.5)
        return jnp.where(visible, scores, hidden_logits)

    def values_in(group, low, high, weights):
        return jnp.dot(
            weights.astype(jnp.bfloat16),
            kv_all[low:high, 1, :, group * HEAD_WIDTH : (group + 1) * HEAD_WIDTH].reshape(
                (high - low) * cached, HEAD_WIDTH
            ),
            preferred_element_type=jnp.float32,
        )

    def attend_most():
        visible = visible_in(0, count - 1)
        for group in range(groups):
            scores = scores_in(group, 0, count - 1, visible)
            best = jnp.max(scores, axis=1, keepdims=True)
            weights = jnp.exp(scores - best)
            total = jnp.sum(weights, axis=1, keepdims=True)
            best_so_far[group] = jnp.broadcast_to(best, (together * tokens, HEAD_WIDTH))
            total_so_far[group] = jnp.broadcast_to(total, (together * tokens, HEAD_WIDTH))
            mix_so_far[group] = values_in(group, 0, count - 1, weights)

    def attention():
        visible = visible_in(count - 1, count)
        squared = jnp.zeros((tokens, LANES), jnp.float32)
        for group in range(groups):
            scores = scores_in(group, count - 1, count, visible)
            before = best_so_far[group]
            best = jnp.maximum(before, jnp.max(scores, axis=1, keepdims=True))
            weights = jnp.exp(scores - best[:, :1])
            factor = jnp.exp(before - best)
            total = total_so_far[group] * factor + jnp.sum(weights, axis=1, keepdims=True)
            mixed = mix_so_far[group] * factor + values_in(group, count - 1, count, weights)
            mixed = (mixed / total).astype(jnp.bfloat16)
            for one in range(together):
                start = (group * together + one) * HEAD_WIDTH
                cols = slice(start, start + HEAD_WIDTH)
                part = mixed[one * tokens : (one + 1) * tokens]
                rows[0, 0:half, cols] = part[:half]
                rows[1, 0:half, cols] = part[half:]
                part = part.astype(jnp.float32)
                squared = squared + part * part
        return squared

    def share_squares(total):
        columns = jnp.broadcast_to(jnp.sum(total, axis=1, keepdims=True), (tokens, LANES))
        head_squares[0] = jnp.transpose(columns)[: head_squares.shape[1]]
        return [
            begin(
                head_squares.at[0],
                head_squares.at[index + 1],
                14,
                head_recv.at[index],
                {"head": other},
            )
            for index, other in enumerate((mate, across, corner))
        ]

    def spread_squares(copies):
        for each in copies:
            each.wait_recv()
        squares[0] = (head_squares[0] + head_squares[1]) + (head_squares[2] + head_squares[3])
        return broadcast(1, squares)

    def fill(store, slot, row):
        columns = jnp.transpose(jnp.broadcast_to(row, (LANES, tokens)))
        for wave in range(2):
            store[wave, slot * half : (slot + 1) * half, :] = columns[wave * half : (wave + 1) * half]

    def fill_gains(copies):
        for each in copies:
            each.wait_recv()
        for slot in range(count):
            row = jnp.sum(jnp.where(expert_row == me, tables[slot], 0.0), axis=0, keepdims=True)
            fill(gains, slot, row)

    def fill_scales(copies):
        for each in copies:
            each.wait_recv()
        for slot in range(count):
            fill(scales, slot, lax.rsqrt(squares[slot][0:1, :] / D + norm_eps))

    def activate(wave, slot, blocks):
        for kind in (2, 3):
            for one in range(slot, slot + blocks):
                if (kind, wave, one) in pairs:
                    pairs[kind, wave, one].wait_recv()
        step = 32
        lane = lax.broadcasted_iota(jnp.int32, (step, LANES), 1)

        def some_rows(index, carry):
            span = pl.ds(pl.multiple_of(slot * half + index * step, step), step)
            scale = scales[wave, span, :]
            gain = gains[wave, span, :]
            inner = jnp.zeros((step, LANES), jnp.float32)
            for start in range(0, side, LANES):
                cols = slice(start, start + LANES)
                up_cols = slice(side + start, side + start + LANES)
                down_cols = slice(2 * side + start, 2 * side + start + LANES)
                gate = sum_raw[wave, span, cols] + far_raw_in[wave, span, cols].astype(jnp.float32)
                up = sum_raw[wave, span, up_cols] + far_raw_in[wave, span, up_cols].astype(
                    jnp.float32
                )
                gate, up = gate * scale, up * scale
                back_value = sum_back[wave, span, cols] + far_back_in[wave, span, cols].astype(
                    jnp.float32
                )
                sigmoid = jax.nn.sigmoid(gate)
                silu = gate * sigmoid
                grad_gate = back_value * up * sigmoid * (1.0 + gate * (1.0 - sigmoid))
                grad_up = back_value * silu
                inner = inner + (grad_gate * gate + grad_up * up)
                act[wave, span, cols] = (gain * (silu * up)).astype(jnp.bfloat16)
                act[wave, span, up_cols] = (gain * scale * grad_gate).astype(jnp.bfloat16)
                act[wave, span, down_cols] = (gain * scale * grad_up).astype(jnp.bfloat16)
            high, middle, low = three_parts(
                jnp.broadcast_to(jnp.sum(inner, axis=1, keepdims=True), (step, LANES))
            )
            zero = jnp.zeros((step, LANES), jnp.float32)
            spread = jnp.where(lane == 0, high.astype(jnp.float32), zero)
            spread = jnp.where(lane == 1, middle.astype(jnp.float32), spread)
            spread = jnp.where(lane == 2, low.astype(jnp.float32), spread)
            act[wave, span, 3 * side :] = spread.astype(jnp.bfloat16)
            return carry

        lax.fori_loop(0, blocks * half // step, some_rows, 0)
        pair_begin(4, wave, slot, blocks, act, act_in, mate)

    def finish(wave, slot, blocks):
        span = slice(slot * half, (slot + blocks) * half)
        pairs[4, wave, slot].wait_recv()
        inner = jnp.sum(
            act[wave, span, 3 * side :].astype(jnp.float32)
            + act_in[wave, span, 3 * side :].astype(jnp.float32),
            axis=1,
            keepdims=True,
        )
        tile = 256
        scale = scales[wave, span, :]
        bent = wide(gains[wave, span, :] * (scale * scale / D) * inner, tile)
        hidden = slice(0, side)
        slopes = slice(side, 3 * side)
        act_all = jnp.concatenate([act[wave, span, hidden], act_in[wave, span, hidden]], axis=1)
        for start in range(0, width, tile):
            cols = slice(start, start + tile)
            weights = jnp.concatenate([w_down[core, :, cols], w_down[1 - core, :, cols]], axis=0)
            out = jnp.dot(act_all, weights, preferred_element_type=jnp.float32)
            parts[wave, span, cols] = out.astype(jnp.bfloat16)
            grad = lax.dot_general(
                act[wave, span, slopes],
                w_up[core, cols, :],
                EXACT,
                preferred_element_type=jnp.float32,
            ) + lax.dot_general(
                act_in[wave, span, slopes],
                w_up[1 - core, cols, :],
                EXACT,
                preferred_element_type=jnp.float32,
            )
            grad = grad - bent * rows[wave, span, cols].astype(jnp.float32)
            parts[wave, span, width + start : width + start + tile] = grad.astype(jnp.bfloat16)

    def arrived(wave, pair, step):
        both = parts.at[wave, pl.ds(0, half)]
        where = scatter_recv.at[wave, lanes[pair][1] + step]
        remote(both, both, 0, where, {"head": mate}).wait_recv()

    def scatter(wave, step):
        for pair, (steps, first) in enumerate(lanes):
            if step >= steps:
                continue
            if step > 0:
                arrived(wave, pair, step - 1)
            for way in range(2):
                sub = way if pair == 0 else 1 - way
                sign = 1 if way == 0 else -1
                start = slot_of(sign * (steps - step), count) * half + sub * quarter
                block = parts.at[wave, pl.ds(start, quarter)]
                there = pl.ds(sub * quarter, quarter)
                if step > 0:
                    sum_ref = held.at[wave, way, step - 1, there]
                    sum_ref[...] = (
                        sum_ref[...].astype(jnp.float32) + block[...].astype(jnp.float32)
                    ).astype(jnp.bfloat16)
                    block = sum_ref
                begin(
                    block,
                    held.at[wave, way, step, there],
                    5 + wave,
                    scatter_recv.at[wave, first + step],
                    {"exp": others[way]},
                )

    def settle(wave):
        sides = ((rows, slice(0, width)), (grads, slice(width, 2 * width)))
        arrived(wave, 1, reach - 2)
        for sub in range(2):
            span = slice(sub * quarter, (sub + 1) * quarter)
            for base, cols in sides:
                settled[span, cols] = base[wave, span, :].astype(jnp.float32) + (
                    parts[wave, span, cols].astype(jnp.float32)
                    + held[wave, 1 - sub, reach - 2, span, cols].astype(jnp.float32)
                )
        arrived(wave, 0, reach - 1)
        for sub in range(2):
            span = slice(sub * quarter, (sub + 1) * quarter)
            for index, (base, cols) in enumerate(sides):
                start = index * tokens + wave * half + sub * quarter
                results_ref[start : start + quarter, :] = (
                    settled[span, cols] + held[wave, sub, reach - 1, span, cols].astype(jnp.float32)
                ).astype(jnp.bfloat16)

    def drain():
        others_of = pl.ds(half, (count - 1) * half)
        for kind, sent in enumerate(
            (
                kv_all.at[pl.ds(1, count - 1)],
                grads.at[0, others_of],
                grads.at[1, others_of],
                rows.at[0, others_of],
                rows.at[1, others_of],
                parts.at[0, others_of],
                parts.at[1, others_of],
                tables.at[pl.ds(1, count - 1)],
                squares.at[pl.ds(1, count - 1)],
                near_back,
                near_raw,
                far_back,
                far_raw,
                act,
                head_squares.at[pl.ds(1, 3)],
            )
        ):
            remote(sent, sent, kind, head_recv.at[0], {"head": mate}).wait_send()

    first = (0, 3)
    between = [(2 * step - 1, 2) for step in range(2, reach - 1)]
    last = (2 * reach - 3, 3)
    advance(0)
    advance_wave(0, 0, 0)
    table_copies = broadcast(0, tables)
    split()
    advance(1)
    advance_wave(0, 0, 1)
    back(0, *first)
    advance(2)
    far(0, 0, *first)
    advance_wave(0, 0, 2)
    for step in range(3, reach):
        back(0, *between[step - 3])
        advance(step)
        far(0, 0, *between[step - 3])
        if step == reach - 1:
            attend_most()
        advance_wave(0, 0, step)
    advance(reach)
    advance_wave(0, 1, 0)
    square_total = attention()
    advance_wave(1, 0, 0)
    square_copies = share_squares(square_total)
    advance_wave(0, 0, reach)
    back(0, *last)
    advance_wave(0, 1, 1, (0,))
    raw(0, 0, 1)
    far(0, 0, *last)
    square_copies = spread_squares(square_copies)
    far(1, 0, 0, 1)
    advance_wave(1, 0, 1)
    raw(0, 1, 2)
    advance_wave(0, 1, 2, (0,))
    advance_wave(1, 0, 2)
    far(1, 0, 1, 2)
    for unit in between[:1]:
        raw(0, *unit)
    advance_wave(0, 1, 3, (0,))
    advance_wave(1, 0, 3)
    for unit in between[:1]:
        far(1, 0, *unit)
    advance_wave(1, 1, 0)
    for step in range(4, reach + 1):
        advance_wave(1, 0, step)
        for unit in between[step - 3 : step - 2]:
            raw(0, *unit)
            far(1, 0, *unit)
    raw(0, *last)
    advance_wave(0, 1, 1, (1,))
    back(1, *first)
    far(1, 0, *last)
    advance_wave(1, 1, 1)
    for step in range(4, reach + 1):
        advance_wave(0, 1, step, (0,))
    fill_gains(table_copies)
    fill_scales(square_copies)
    far(0, 1, *first)
    advance_wave(0, 1, 2, (1,))
    activate(0, *first)
    advance_wave(1, 1, 2)
    raw(1, *first)
    for step in range(3, reach):
        advance_wave(0, 1, step, (1,))
    activate(0, *last)
    far(1, 1, *first)
    for unit in between:
        activate(0, *unit)
    for step in range(3, reach):
        advance_wave(1, 1, step)
    finish(0, *last)
    scatter(0, 0)
    for unit in between:
        finish(0, *unit)
    advance_wave(0, 1, reach, (1,))
    back(1, *last)
    for unit in between:
        back(1, *unit)
    far(0, 1, *last)
    advance_wave(1, 1, reach)
    raw(1, *last)
    finish(0, *first)
    far(1, 1, *last)
    activate(1, *first)
    scatter(0, 1)
    for unit in between:
        raw(1, *unit)
        far(0, 1, *unit)
    finish(1, *first)
    for unit in between:
        far(1, 1, *unit)
    scatter(0, 2)
    activate(1, *last)
    for step in range(3, reach):
        scatter(0, step)
    finish(1, *last)
    scatter(1, 0)
    for unit in between:
        activate(1, *unit)
        finish(1, *unit)
    settle(0)
    for step in range(1, reach):
        scatter(1, step)
    settle(1)
    drain()


def fused_device(queries, keys, values, w_in, w_out, routes, route_weights, grad_out):
    count = lax.axis_size("exp")
    tokens, width = queries.shape
    cached, kv_width = keys.shape
    hidden = w_in.shape[3]
    side = hidden // 2
    reach = count // 2
    half_rows = tokens // 2
    every = count * half_rows
    experts = w_in.shape[0] * count
    stacked = (kv_width // HEAD_WIDTH, width // kv_width * tokens, HEAD_WIDTH)

    def body(*refs):
        fused_kernel(count, *refs)

    def half(*shape):
        return pltpu.VMEM(shape, jnp.bfloat16)

    def whole(*shape):
        return pltpu.VMEM(shape, jnp.float32)

    dma = pltpu.SemaphoreType.DMA
    vmem = pl.BlockSpec(memory_space=pltpu.VMEM)
    anywhere = pl.BlockSpec(memory_space=pl.ANY)
    both = pl.pallas_call(
        body,
        out_shape=jax.ShapeDtypeStruct((2 * tokens, width), jnp.bfloat16),
        in_specs=[anywhere] * 8,
        out_specs=vmem,
        scratch_shapes=[
            half(tokens, width),
            pltpu.VMEM(routes.shape[::-1], routes.dtype),
            whole(*route_weights.shape[::-1]),
            half(width, 2, hidden),
            half(2, width, hidden),
            half(2, side, width),
            half(count, 2, cached, kv_width),
            half(2, every, width),
            half(2, every, width),
            whole(count, experts, tokens),
            whole(count, 8, tokens),
            whole(4, 8, tokens),
            whole(2, every, LANES),
            whole(2, every, LANES),
            whole(2, every, hidden),
            whole(2, every, side),
            half(2, every, hidden),
            half(2, every, side),
            half(2, every, hidden),
            half(2, every, side),
            half(2, every, hidden),
            half(2, every, side),
            half(2, every, hidden),
            half(2, every, side),
            half(2, every, 3 * side + LANES),
            half(2, every, 3 * side + LANES),
            half(2, every, 2 * width),
            half(2, 2, reach, half_rows, 2 * width),
            whole(half_rows, 2 * width),
            whole(*stacked),
            whole(*stacked),
            whole(*stacked),
            dma((8,)),
            dma((15,)),
            dma((reach,)),
            dma((2, 2, 2 * reach - 1)),
            dma((2, 2 * reach - 1)),
            dma((2, count - 1)),
            dma((3,)),
            dma((5 * 2 * (reach - 1) + 2,)),
        ],
        compiler_params=pltpu.CompilerParams(
            collective_id=1, has_side_effects=True, vmem_limit_bytes=60 * 1024 * 1024
        ),
        name="fused",
    )(
        queries,
        keys,
        values,
        w_in,
        w_out[0].reshape(2, side, width),
        routes.T,
        route_weights.T,
        grad_out.reshape(2, half_rows, width),
    )
    return both[:tokens], both[tokens:]


def solution(mesh):
    fused = 2 * TOP >= mesh.shape["exp"] and mesh.shape["exp"] == 8 and mesh.shape["head"] == 4
    in_specs = (
        P("exp", "head"),
        P("exp", "head"),
        P("exp", "head"),
        P("exp", "head", None, None),
        P("exp", None, "head"),
        P("exp", None),
        P("exp", None),
        P("exp", "head"),
    )
    out_specs = (P("exp", "head"), P("exp", "head"))
    return jax.shard_map(
        fused_device if fused else per_device, mesh=mesh, in_specs=in_specs, out_specs=out_specs, check_vma=False
    )
```

```python
import jax
import jax.numpy as jnp
from jax import lax
from jax.experimental import pallas as pl
from jax.experimental.pallas import tpu as pltpu
from jax.sharding import PartitionSpec as P

D = 4096
HEAD_WIDTH = 128
TOP = 6


norm_eps = 1e-05
hidden_logits = -1e30


def block_partial(query_rows, query_pos, rows_of_keys, value_rows, key_pos):
    row_count = query_rows.shape[0]
    count_of_blocks = rows_of_keys.shape[0]
    kv_heads = rows_of_keys.shape[2] // HEAD_WIDTH
    grouping_width = query_rows.shape[1] // HEAD_WIDTH // kv_heads
    heads_of_queries = query_rows.reshape(row_count, kv_heads, grouping_width, HEAD_WIDTH)
    key_heads = rows_of_keys.reshape(count_of_blocks, -1, kv_heads, HEAD_WIDTH)
    value_heads = value_rows.reshape(count_of_blocks, -1, kv_heads, HEAD_WIDTH)
    visible = (key_pos[:, None, :] <= query_pos[None, :, None])[:, :, None, None, :]
    scores = jnp.einsum(
        "tgid,bjgd->btgij", heads_of_queries, key_heads, preferred_element_type=jnp.float32
    ) * HEAD_WIDTH ** (-0.5)
    scores = jnp.where(visible, scores, hidden_logits)
    best_score = jnp.max(scores, axis=-1).astype(jnp.bfloat16)
    weights = jnp.where(visible, jnp.exp(scores - best_score.astype(jnp.float32)[..., None]), 0.0)
    weight_total = jnp.sum(weights, axis=-1).astype(jnp.bfloat16)
    weighted_sum = jnp.einsum(
        "btgij,bjgd->btgid",
        weights.astype(jnp.bfloat16),
        value_heads,
        preferred_element_type=jnp.float32,
    ).astype(jnp.bfloat16)
    head_count = kv_heads * grouping_width
    return (
        best_score.reshape(count_of_blocks, row_count, head_count),
        weight_total.reshape(count_of_blocks, row_count, head_count),
        weighted_sum.reshape(count_of_blocks, row_count, head_count * HEAD_WIDTH),
    )


def fold_partials(running, best_score, weight_total, weighted_sum):
    top_now, total_now, sums_now = running
    best_value = best_score.astype(jnp.float32)
    new_top = jnp.maximum(top_now, jnp.max(best_value, axis=0))
    old_factor = jnp.exp(top_now - new_top)
    block_factor = jnp.exp(best_value - new_top[None])
    total_next = total_now * old_factor + jnp.sum(
        weight_total.astype(jnp.float32) * block_factor, axis=0
    )
    spread_sums = weighted_sum.reshape(
        weighted_sum.shape[0], sums_now.shape[0], sums_now.shape[1], HEAD_WIDTH
    )
    sums_next = sums_now * old_factor[..., None] + jnp.sum(
        spread_sums.astype(jnp.float32) * block_factor[..., None], axis=0
    )
    return (new_top, total_next, sums_next)


def per_device(queries, keys, values, w_in, w_out, routes, route_weights, grad_out):
    exp_count = lax.axis_size("exp")
    exp_index = lax.axis_index("exp")
    head_devices = lax.axis_size("head")
    token_count = queries.shape[0]
    query_width = queries.shape[1]
    head_count = query_width // HEAD_WIDTH
    cache_rows = keys.shape[0]
    window = token_count * exp_count
    offset = cache_rows * exp_count - window
    beginning = (
        jnp.full((token_count, head_count), hidden_logits, jnp.float32),
        jnp.zeros((token_count, head_count), jnp.float32),
        jnp.zeros((token_count, head_count, HEAD_WIDTH), jnp.float32),
    )
    own_pos = offset + exp_index * token_count + jnp.arange(token_count, dtype=jnp.int32)
    key_piece = lax.all_gather(keys, "exp", axis=0, tiled=True)
    value_piece = lax.all_gather(values, "exp", axis=0, tiled=True)
    piece_blocks = key_piece.shape[0] // cache_rows
    key_split = key_piece.reshape(piece_blocks, cache_rows, -1)
    value_split = value_piece.reshape(piece_blocks, cache_rows, -1)
    pos_split = jnp.arange(key_piece.shape[0], dtype=jnp.int32).reshape(piece_blocks, cache_rows)

    def one_block(state, element):
        key_block, value_block, pos_block = element
        block_parts = block_partial(
            queries, own_pos, key_block[None], value_block[None], pos_block[None]
        )
        return (fold_partials(state, block_parts[0], block_parts[1], block_parts[2]), None)

    state, ignored = lax.scan(one_block, beginning, (key_split, value_split, pos_split))
    attended = (
        (state[2] / state[1][..., None]).reshape(token_count, query_width).astype(jnp.bfloat16)
    )
    row_width = attended.shape[1]
    experts_all = w_in.shape[0] * exp_count
    mean_load = TOP * token_count // experts_all
    capacity = mean_load + mean_load // 6
    places = experts_all * capacity
    flat_routes = routes.reshape(-1)
    expert_hits = (
        flat_routes[:, None] == jnp.arange(experts_all, dtype=jnp.int32)[None, :]
    ).astype(jnp.bfloat16)
    before = jnp.tri(flat_routes.shape[0], k=-1, dtype=jnp.bfloat16)
    earlier = jnp.dot(before, expert_hits, preferred_element_type=jnp.float32)
    slot_index = jnp.sum(earlier * expert_hits.astype(jnp.float32), axis=1).astype(jnp.int32)
    place_index = flat_routes * capacity + slot_index
    chosen = (place_index[:, None] == jnp.arange(places, dtype=jnp.int32)[None, :]).astype(
        jnp.bfloat16
    )
    picker = jnp.sum(chosen.reshape(token_count, TOP, places), axis=1)
    contract_rows = (((0,), (0,)), ((), ()))
    send_rows = lax.dot_general(picker, attended, contract_rows, preferred_element_type=jnp.float32)
    send_rows = send_rows.astype(jnp.bfloat16).reshape(experts_all, capacity, row_width)
    send_grads = lax.dot_general(
        picker, grad_out, contract_rows, preferred_element_type=jnp.float32
    )
    send_grads = send_grads.astype(jnp.bfloat16).reshape(experts_all, capacity, row_width)
    w_first = w_in[0]
    w_second = w_out[0]
    rows_in = lax.all_to_all(send_rows, "exp", split_axis=0, concat_axis=0, tiled=True)
    grads_in = lax.all_to_all(send_grads, "exp", split_axis=0, concat_axis=0, tiled=True)
    lead_count, item_count, width_in = rows_in.shape
    row_total = lead_count * item_count
    row_block = rows_in.reshape(row_total, width_in)
    grad_block = grads_in.reshape(row_total, width_in)
    row_float = row_block.astype(jnp.float32)
    raw_sums = jnp.einsum("rd,dkf->rkf", row_block, w_first, preferred_element_type=jnp.float32)
    back_sums = lax.dot_general(
        grad_block, w_second, (((1,), (1,)), ((), ())), preferred_element_type=jnp.float32
    )
    squares = jnp.sum(row_float * row_float, axis=1)
    square_tile = jnp.broadcast_to(squares[:, None, None], (row_total, 1, head_devices))
    raw_part = lax.psum_scatter(raw_sums, "head", scatter_dimension=2, tiled=True)
    back_part = lax.psum_scatter(back_sums[:, None, :], "head", scatter_dimension=2, tiled=True)
    square_part = lax.psum_scatter(square_tile, "head", scatter_dimension=2, tiled=True)
    norm_scale = lax.rsqrt(square_part[:, 0] / D + norm_eps)
    gate_value = raw_part[:, 0] * norm_scale
    up_value = raw_part[:, 1] * norm_scale
    back_value = back_part[:, 0]
    gate_sigmoid = jax.nn.sigmoid(gate_value)
    gate_silu = gate_value * gate_sigmoid
    act_part = (gate_silu * up_value).astype(jnp.bfloat16)
    grad_gate = back_value * up_value * gate_sigmoid * (1.0 + gate_value * (1.0 - gate_sigmoid))
    grad_up = back_value * gate_silu
    grad_part = jnp.stack([grad_gate, grad_up], axis=1).astype(jnp.bfloat16)
    inner_part = jnp.sum(
        grad_part.astype(jnp.float32) * jnp.stack([gate_value, up_value], axis=1), axis=(1, 2)
    )
    act_whole = lax.all_gather(act_part[:, None, :], "head", axis=2, tiled=True)
    grad_hidden = lax.all_gather(grad_part, "head", axis=2, tiled=True)
    hidden_act = act_whole[:, 0]
    inner_sum = lax.psum(inner_part, "head")
    out_rows = jnp.dot(hidden_act, w_second, preferred_element_type=jnp.float32).astype(
        jnp.bfloat16
    )
    grad_normed = jnp.einsum(
        "rkf,dkf->rd", grad_hidden, w_first, preferred_element_type=jnp.float32
    )
    grad_rows = (
        norm_scale * grad_normed - row_float * (norm_scale * norm_scale / D) * inner_sum[:, None]
    )
    expert_out = out_rows.reshape(lead_count, item_count, width_in)
    expert_grad = grad_rows.astype(jnp.bfloat16).reshape(lead_count, item_count, width_in)
    came_out, came_grad = (
        lax.all_to_all(expert_out, "exp", split_axis=0, concat_axis=0, tiled=True),
        lax.all_to_all(expert_grad, "exp", split_axis=0, concat_axis=0, tiled=True),
    )
    picked_out = came_out.reshape(places, row_width)[place_index].reshape(
        token_count, TOP, row_width
    )
    picked_grad = came_grad.reshape(places, row_width)[place_index].reshape(
        token_count, TOP, row_width
    )
    output = attended.astype(jnp.float32) + jnp.sum(
        route_weights[:, :, None] * picked_out.astype(jnp.float32), axis=1
    )
    grad_attended = grad_out.astype(jnp.float32) + jnp.sum(
        route_weights[:, :, None] * picked_grad.astype(jnp.float32), axis=1
    )
    return (output.astype(jnp.bfloat16), grad_attended.astype(jnp.bfloat16))


LANES = 128
EXACT = (((1,), (1,)), ((), ()))


def three_parts(value):
    high = value.astype(jnp.bfloat16)
    rest = value - high.astype(jnp.float32)
    middle = rest.astype(jnp.bfloat16)
    low = (rest - middle.astype(jnp.float32)).astype(jnp.bfloat16)
    return high, middle, low


def ring_place(index, count):
    outer, inner = index // 2, index % 2
    return outer + inner * (count - 1 - 2 * outer)


def ring_index(place, count):
    inner = place // (count // 2)
    return 2 * (place + inner * (count - 1 - 2 * place)) + inner


def ring_lanes(count):
    reach = count // 2
    return ((0, 0, reach), (1, 1, reach), (0, 1, reach - 1), (1, 0, reach - 1))


def slot_of(distance, count):
    if distance == 0:
        return 0
    if abs(distance) == count // 2:
        return count - 1
    return 2 * distance - 1 if distance > 0 else -2 * distance


def wide(value, width):
    return jnp.concatenate([value] * (width // value.shape[1]), axis=1)


def fused_kernel(
    count,
    queries_ref,
    k_ref,
    v_ref,
    w_in_ref,
    w_out_ref,
    routes_in_ref,
    shares_ref,
    grad_ref,
    results_ref,
    q_ref,
    routes_ref,
    share_ref,
    w_pairs,
    w_up,
    w_down,
    kv_all,
    grads,
    rows,
    tables,
    squares,
    head_squares,
    gains,
    scales,
    sum_raw,
    sum_back,
    near_raw,
    near_back,
    near_raw_in,
    near_back_in,
    far_raw,
    far_back,
    far_raw_in,
    far_back_in,
    act,
    act_in,
    parts,
    held,
    settled,
    best_so_far,
    total_so_far,
    mix_so_far,
    load_sem,
    send_sem,
    early_recv,
    wave_recv,
    scatter_recv,
    meta_recv,
    head_recv,
    pair_recv,
):
    reach = count // 2
    tokens, width = q_ref.shape
    cached, kv_width = k_ref.shape
    side = w_down.shape[1]
    experts = tables.shape[1]
    half = tokens // 2
    quarter = half // 2
    me = lax.axis_index("exp")
    place = ring_place(me, count)
    head = lax.axis_index("head")
    core = head % 2
    mate = head + 1 - 2 * core
    across = (head + 2) % 4
    corner = 3 - head
    others = (ring_index((place + 1) % count, count), ring_index((place + count - 1) % count, count))
    distances = [0] + [d for s in range(1, reach) for d in (s, -s)] + [reach]
    lanes = ((reach, 0), (reach - 1, reach))

    def remote(source, target, kind, recv_sem, where):
        return pltpu.make_async_remote_copy(
            src_ref=source,
            dst_ref=target,
            send_sem=send_sem.at[kind],
            recv_sem=recv_sem,
            device_id=where,
            device_id_type=pl.DeviceIdType.MESH,
        )

    def begin(*what):
        copy = remote(*what)
        copy.start()
        return copy

    loads = [
        pltpu.make_async_copy(source, target, load_sem.at[index])
        for index, (source, target) in enumerate(
            (
                (k_ref, kv_all.at[0, 0]),
                (v_ref, kv_all.at[0, 1]),
                (grad_ref, grads.at[:, pl.ds(0, half)]),
                (routes_in_ref, routes_ref),
                (shares_ref, share_ref),
                (w_in_ref.at[0], w_pairs),
                (w_out_ref, w_down),
                (queries_ref, q_ref),
            )
        )
    ]
    for each in loads:
        each.start()

    barrier = pltpu.get_barrier_semaphore()
    for other in (mate, across, corner):
        pl.semaphore_signal(
            barrier, inc=1, device_id={"head": other}, device_id_type=pl.DeviceIdType.MESH
        )
    for distance in distances[1:]:
        other = ring_index((place + distance + count) % count, count)
        pl.semaphore_signal(
            barrier, inc=1, device_id={"exp": other}, device_id_type=pl.DeviceIdType.MESH
        )

    for each in loads[:5]:
        each.wait()
    expert_row = lax.broadcasted_iota(jnp.int32, (experts, tokens), 0)
    table = jnp.zeros((experts, tokens), jnp.float32)
    for k in range(routes_ref.shape[0]):
        table = table + jnp.where(expert_row == routes_ref[k : k + 1, :], share_ref[k : k + 1, :], 0.0)
    tables[0] = table
    pl.semaphore_wait(barrier, 3 + count - 1)

    def advance(step):
        if step >= 1:
            both = kv_all.at[0] if step == reach else kv_all.at[pl.ds(0, 2)]
            remote(both, both, 0, early_recv.at[step - 1], {"head": mate}).wait_recv()
        for way in range(2 if step < reach else 0):
            sign = -1 if way == 0 else 1
            here, there = slot_of(sign * step, count), slot_of(sign * (step + 1), count)
            halved = step == reach - 1
            begin(
                kv_all.at[here, way] if halved else kv_all.at[here],
                kv_all.at[there, way] if halved else kv_all.at[there],
                0,
                early_recv.at[step],
                {"exp": others[way]},
            )

    def advance_wave(kind, wave, step, pairs_of=(0, 1)):
        store = rows if kind else grads
        for pair in pairs_of:
            steps, first = lanes[pair]
            if 1 <= step <= steps:
                both = store.at[wave, pl.ds(0, half)]
                arrived = wave_recv.at[kind, wave, first + step - 1]
                remote(both, both, 0, arrived, {"head": mate}).wait_recv()
            for way in range(2 if step < steps else 0):
                sub = way if pair == 0 else 1 - way
                sign = -1 if way == 0 else 1
                there = slot_of(sign * (step + 1), count) * half + sub * quarter
                here = slot_of(sign * step, count) * half + sub * quarter
                begin(
                    store.at[wave, pl.ds(here, quarter)],
                    store.at[wave, pl.ds(there, quarter)],
                    1 + 2 * kind + wave,
                    wave_recv.at[kind, wave, first + step],
                    {"exp": others[way]},
                )

    def broadcast(kind, store):
        for distance in distances[1:]:
            there = slot_of(-distance, count)
            other = ring_index((place + distance + count) % count, count)
            begin(store.at[0], store.at[there], 7 + kind, meta_recv.at[kind], {"exp": other})
        others_of = store.at[pl.ds(1, count - 1)]
        return remote(others_of, others_of, 7 + kind, meta_recv.at[kind], {"head": mate})

    def split():
        loads[5].wait()
        chunk = LANES
        to = lax.broadcasted_iota(jnp.int32, (2 * chunk, 2 * chunk), 0)
        source = lax.broadcasted_iota(jnp.int32, (2 * chunk, 2 * chunk), 1)
        picks = (source == jnp.where(to < chunk, 2 * to, 2 * to - 2 * chunk + 1)).astype(jnp.bfloat16)

        def split_chunk(index, carry):
            span = pl.ds(pl.multiple_of(index * chunk, chunk), chunk)
            pairs = w_pairs[span].reshape(2 * chunk, 2 * side)
            apart = jnp.dot(picks, pairs, preferred_element_type=jnp.float32).astype(jnp.bfloat16)
            for part in range(2):
                cols = slice(part * side, (part + 1) * side)
                w_up[part, span, :side] = apart[:chunk, cols]
                w_up[part, span, side:] = apart[chunk:, cols]
            return carry

        lax.fori_loop(0, width // chunk, split_chunk, 0)
        loads[6].wait()
        loads[7].wait()

    pairs = {}

    def pair_begin(kind, wave, slot, blocks, source, target, other):
        span = pl.ds(slot * half, blocks * half)
        pairs[kind, wave, slot] = begin(
            source.at[wave, span],
            target.at[wave, span],
            9 + kind,
            pair_recv.at[len(pairs)],
            {"head": other},
        )

    def back(wave, slot, blocks):
        span = slice(slot * half, (slot + blocks) * half)
        weights = jnp.concatenate([w_down[1 - core], w_down[core]], axis=0)
        both = lax.dot_general(
            grads[wave, span, :], weights, EXACT, preferred_element_type=jnp.float32
        )
        near_back[wave, span, :] = both[:, :side].astype(jnp.bfloat16)
        pair_begin(0, wave, slot, blocks, near_back, near_back_in, mate)
        sum_back[wave, span, :] = both[:, side:]

    def raw(wave, slot, blocks):
        span = slice(slot * half, (slot + blocks) * half)
        block = rows[wave, span, :]
        near_raw[wave, span, :] = jnp.dot(
            block, w_up[1 - core], preferred_element_type=jnp.float32
        ).astype(jnp.bfloat16)
        pair_begin(1, wave, slot, blocks, near_raw, near_raw_in, mate)
        sum_raw[wave, span, :] = jnp.dot(block, w_up[core], preferred_element_type=jnp.float32)

    def far(kind, wave, slot, blocks):
        total, near_in = ((sum_back, near_back_in), (sum_raw, near_raw_in))[kind]
        out, target = ((far_back, far_back_in), (far_raw, far_raw_in))[kind]
        span = slice(slot * half, (slot + blocks) * half)
        pairs[kind, wave, slot].wait_recv()
        both = total[wave, span, :] + near_in[wave, span, :].astype(jnp.float32)
        total[wave, span, :] = both
        out[wave, span, :] = both.astype(jnp.bfloat16)
        pair_begin(2 + kind, wave, slot, blocks, out, target, across)

    groups = kv_width // HEAD_WIDTH
    together = width // kv_width

    def visible_in(low, high):
        size = (high - low) * cached
        column = low * cached + lax.broadcasted_iota(jnp.int32, (1, size), 1)
        shift = jnp.zeros((1, size), jnp.int32)
        for slot in range(low, high):
            owner = ring_index((place + distances[slot] + count) % count, count)
            shift = jnp.where(column // cached == slot, (owner - slot) * cached, shift)
        row_pos = (
            count * (cached - tokens)
            + me * tokens
            + lax.broadcasted_iota(jnp.int32, (tokens, size), 0)
        )
        row_pos = jnp.concatenate([row_pos] * together, axis=0)
        return jnp.broadcast_to(shift + column, row_pos.shape) <= row_pos

    def scores_in(group, low, high, visible):
        first_head = group * together
        stacked = jnp.concatenate(
            [
                q_ref[:, one * HEAD_WIDTH : (one + 1) * HEAD_WIDTH]
                for one in range(first_head, first_head + together)
            ],
            axis=0,
        )
        scores = lax.dot_general(
            stacked,
            kv_all[low:high, 0, :, group * HEAD_WIDTH : (group + 1) * HEAD_WIDTH].reshape(
                (high - low) * cached, HEAD_WIDTH
            ),
            EXACT,
            preferred_element_type=jnp.float32,
        ) * HEAD_WIDTH ** (-0.5)
        return jnp.where(visible, scores, hidden_logits)

    def values_in(group, low, high, weights):
        return jnp.dot(
            weights.astype(jnp.bfloat16),
            kv_all[low:high, 1, :, group * HEAD_WIDTH : (group + 1) * HEAD_WIDTH].reshape(
                (high - low) * cached, HEAD_WIDTH
            ),
            preferred_element_type=jnp.float32,
        )

    def attend_most():
        visible = visible_in(0, count - 1)
        for group in range(groups):
            scores = scores_in(group, 0, count - 1, visible)
            best = jnp.max(scores, axis=1, keepdims=True)
            weights = jnp.exp(scores - best)
            total = jnp.sum(weights, axis=1, keepdims=True)
            best_so_far[group] = jnp.broadcast_to(best, (together * tokens, HEAD_WIDTH))
            total_so_far[group] = jnp.broadcast_to(total, (together * tokens, HEAD_WIDTH))
            mix_so_far[group] = values_in(group, 0, count - 1, weights)

    def attention():
        visible = visible_in(count - 1, count)
        squared = jnp.zeros((tokens, LANES), jnp.float32)
        for group in range(groups):
            scores = scores_in(group, count - 1, count, visible)
            before = best_so_far[group]
            best = jnp.maximum(before, jnp.max(scores, axis=1, keepdims=True))
            weights = jnp.exp(scores - best[:, :1])
            factor = jnp.exp(before - best)
            total = total_so_far[group] * factor + jnp.sum(weights, axis=1, keepdims=True)
            mixed = mix_so_far[group] * factor + values_in(group, count - 1, count, weights)
            mixed = (mixed / total).astype(jnp.bfloat16)
            for one in range(together):
                start = (group * together + one) * HEAD_WIDTH
                cols = slice(start, start + HEAD_WIDTH)
                part = mixed[one * tokens : (one + 1) * tokens]
                rows[0, 0:half, cols] = part[:half]
                rows[1, 0:half, cols] = part[half:]
                part = part.astype(jnp.float32)
                squared = squared + part * part
        return squared

    def share_squares(total):
        columns = jnp.broadcast_to(jnp.sum(total, axis=1, keepdims=True), (tokens, LANES))
        head_squares[0] = jnp.transpose(columns)[: head_squares.shape[1]]
        for index, other in enumerate((mate, across, corner)):
            begin(
                head_squares.at[0],
                head_squares.at[index + 1],
                14,
                head_recv.at[0],
                {"head": other},
            )

    def spread_squares():
        others_of = head_squares.at[pl.ds(1, 3)]
        remote(others_of, others_of, 14, head_recv.at[0], {"head": mate}).wait_recv()
        squares[0] = (head_squares[0] + head_squares[1]) + (head_squares[2] + head_squares[3])
        return broadcast(1, squares)

    def fill(store, slot, row):
        columns = jnp.transpose(jnp.broadcast_to(row, (LANES, tokens)))
        for wave in range(2):
            store[wave, slot * half : (slot + 1) * half, :] = columns[wave * half : (wave + 1) * half]

    def fill_gains(copies):
        copies.wait_recv()
        for slot in range(count):
            row = jnp.sum(jnp.where(expert_row == me, tables[slot], 0.0), axis=0, keepdims=True)
            fill(gains, slot, row)

    def fill_scales(copies):
        copies.wait_recv()
        for slot in range(count):
            fill(scales, slot, lax.rsqrt(squares[slot][0:1, :] / D + norm_eps))

    def activate(wave, slot, blocks):
        for kind in (2, 3):
            for one in range(slot, slot + blocks):
                if (kind, wave, one) in pairs:
                    pairs[kind, wave, one].wait_recv()
        step = 32
        lane = lax.broadcasted_iota(jnp.int32, (step, LANES), 1)

        def some_rows(index, carry):
            span = pl.ds(pl.multiple_of(slot * half + index * step, step), step)
            scale = scales[wave, span, :]
            gain = gains[wave, span, :]
            inner = jnp.zeros((step, LANES), jnp.float32)
            for start in range(0, side, LANES):
                cols = slice(start, start + LANES)
                up_cols = slice(side + start, side + start + LANES)
                down_cols = slice(2 * side + start, 2 * side + start + LANES)
                gate = sum_raw[wave, span, cols] + far_raw_in[wave, span, cols].astype(jnp.float32)
                up = sum_raw[wave, span, up_cols] + far_raw_in[wave, span, up_cols].astype(
                    jnp.float32
                )
                gate, up = gate * scale, up * scale
                back_value = sum_back[wave, span, cols] + far_back_in[wave, span, cols].astype(
                    jnp.float32
                )
                sigmoid = jax.nn.sigmoid(gate)
                silu = gate * sigmoid
                grad_gate = back_value * up * sigmoid * (1.0 + gate * (1.0 - sigmoid))
                grad_up = back_value * silu
                inner = inner + (grad_gate * gate + grad_up * up)
                act[wave, span, cols] = (gain * (silu * up)).astype(jnp.bfloat16)
                act[wave, span, up_cols] = (gain * scale * grad_gate).astype(jnp.bfloat16)
                act[wave, span, down_cols] = (gain * scale * grad_up).astype(jnp.bfloat16)
            high, middle, low = three_parts(
                jnp.broadcast_to(jnp.sum(inner, axis=1, keepdims=True), (step, LANES))
            )
            zero = jnp.zeros((step, LANES), jnp.float32)
            spread = jnp.where(lane == 0, high.astype(jnp.float32), zero)
            spread = jnp.where(lane == 1, middle.astype(jnp.float32), spread)
            spread = jnp.where(lane == 2, low.astype(jnp.float32), spread)
            act[wave, span, 3 * side :] = spread.astype(jnp.bfloat16)
            return carry

        lax.fori_loop(0, blocks * half // step, some_rows, 0)
        pair_begin(4, wave, slot, blocks, act, act_in, mate)

    def finish(wave, slot, blocks):
        span = slice(slot * half, (slot + blocks) * half)
        pairs[4, wave, slot].wait_recv()
        inner = jnp.sum(
            act[wave, span, 3 * side :].astype(jnp.float32)
            + act_in[wave, span, 3 * side :].astype(jnp.float32),
            axis=1,
            keepdims=True,
        )
        tile = 256
        scale = scales[wave, span, :]
        bent = wide(gains[wave, span, :] * (scale * scale / D) * inner, tile)
        hidden = slice(0, side)
        slopes = slice(side, 3 * side)
        act_all = jnp.concatenate([act[wave, span, hidden], act_in[wave, span, hidden]], axis=1)
        for start in range(0, width, tile):
            cols = slice(start, start + tile)
            weights = jnp.concatenate([w_down[core, :, cols], w_down[1 - core, :, cols]], axis=0)
            out = jnp.dot(act_all, weights, preferred_element_type=jnp.float32)
            parts[wave, span, cols] = out.astype(jnp.bfloat16)
            grad = lax.dot_general(
                act[wave, span, slopes],
                w_up[core, cols, :],
                EXACT,
                preferred_element_type=jnp.float32,
            ) + lax.dot_general(
                act_in[wave, span, slopes],
                w_up[1 - core, cols, :],
                EXACT,
                preferred_element_type=jnp.float32,
            )
            grad = grad - bent * rows[wave, span, cols].astype(jnp.float32)
            parts[wave, span, width + start : width + start + tile] = grad.astype(jnp.bfloat16)

    def arrived(wave, pair, step):
        both = parts.at[wave, pl.ds(0, half)]
        where = scatter_recv.at[wave, lanes[pair][1] + step]
        remote(both, both, 0, where, {"head": mate}).wait_recv()

    def scatter(wave, step, pairs_of=(0, 1)):
        for pair, (steps, first) in enumerate(lanes):
            if step >= steps or pair not in pairs_of:
                continue
            if step > 0:
                arrived(wave, pair, step - 1)
            for way in range(2):
                sub = way if pair == 0 else 1 - way
                sign = 1 if way == 0 else -1
                start = slot_of(sign * (steps - step), count) * half + sub * quarter
                block = parts.at[wave, pl.ds(start, quarter)]
                there = pl.ds(sub * quarter, quarter)
                if step > 0:
                    sum_ref = held.at[wave, way, step - 1, there]
                    sum_ref[...] = (
                        sum_ref[...].astype(jnp.float32) + block[...].astype(jnp.float32)
                    ).astype(jnp.bfloat16)
                    block = sum_ref
                begin(
                    block,
                    held.at[wave, way, step, there],
                    5 + wave,
                    scatter_recv.at[wave, first + step],
                    {"exp": others[way]},
                )

    def settle(wave):
        sides = ((rows, slice(0, width)), (grads, slice(width, 2 * width)))
        arrived(wave, 1, reach - 2)
        for sub in range(2):
            span = slice(sub * quarter, (sub + 1) * quarter)
            for base, cols in sides:
                settled[span, cols] = base[wave, span, :].astype(jnp.float32) + (
                    parts[wave, span, cols].astype(jnp.float32)
                    + held[wave, 1 - sub, reach - 2, span, cols].astype(jnp.float32)
                )
        arrived(wave, 0, reach - 1)
        for sub in range(2):
            span = slice(sub * quarter, (sub + 1) * quarter)
            for index, (base, cols) in enumerate(sides):
                start = index * tokens + wave * half + sub * quarter
                results_ref[start : start + quarter, :] = (
                    settled[span, cols] + held[wave, sub, reach - 1, span, cols].astype(jnp.float32)
                ).astype(jnp.bfloat16)

    def drain():
        others_of = pl.ds(half, (count - 1) * half)
        for kind, sent in enumerate(
            (
                kv_all.at[pl.ds(1, count - 1)],
                grads.at[0, others_of],
                grads.at[1, others_of],
                rows.at[0, others_of],
                rows.at[1, others_of],
                parts.at[0, others_of],
                parts.at[1, others_of],
                tables.at[pl.ds(1, count - 1)],
                squares.at[pl.ds(1, count - 1)],
                near_back,
                near_raw,
                far_back,
                far_raw,
                act,
                head_squares.at[pl.ds(1, 3)],
            )
        ):
            remote(sent, sent, kind, head_recv.at[0], {"head": mate}).wait_send()

    first = (0, 3)
    between = [(2 * step - 1, 2) for step in range(2, reach - 1)]
    last = (2 * reach - 3, 3)
    advance(0)
    advance_wave(0, 0, 0)
    table_copies = broadcast(0, tables)
    split()
    advance(1)
    advance_wave(0, 0, 1)
    back(0, *first)
    advance(2)
    far(0, 0, *first)
    advance_wave(0, 0, 2)
    for step in range(3, reach):
        back(0, *between[step - 3])
        advance(step)
        far(0, 0, *between[step - 3])
        if step == reach - 1:
            attend_most()
        advance_wave(0, 0, step)
    back(0, count - 3, 2)
    advance(reach)
    advance_wave(0, 1, 0, (0,))
    square_total = attention()
    advance_wave(1, 0, 0)
    share_squares(square_total)
    far(0, 0, count - 3, 2)
    advance_wave(0, 0, reach)
    back(0, count - 1, 1)
    advance_wave(0, 1, 1, (0,))
    raw(0, 0, 1)
    far(0, 0, count - 1, 1)
    square_copies = spread_squares()
    far(1, 0, 0, 1)
    advance_wave(1, 0, 1)
    raw(0, 1, 2)
    advance_wave(0, 1, 2, (0,))
    far(1, 0, 1, 2)
    advance_wave(1, 0, 2)
    advance_wave(0, 1, 0, (1,))
    for unit in between[:1]:
        raw(0, *unit)
    for unit in between[:1]:
        far(1, 0, *unit)
    for step in range(3, reach):
        advance_wave(1, 0, step)
        if step == reach - 1:
            advance_wave(1, 1, 0)
        raw(0, 2 * step - 1, 2)
    advance_wave(0, 1, 3, (0,))
    for step in range(3, reach):
        far(1, 0, 2 * step - 1, 2)
    advance_wave(0, 1, 1, (1,))
    advance_wave(1, 0, reach)
    raw(0, count - 1, 1)
    fill_gains(table_copies)
    far(1, 0, count - 1, 1)
    fill_scales(square_copies)
    advance_wave(1, 1, 1)
    activate(0, *first)
    advance_wave(0, 1, 2, (1,))
    back(1, *first)
    advance_wave(1, 1, 2)
    far(0, 1, *first)
    activate(0, *last)
    raw(1, *first)
    for step in range(3, reach):
        advance_wave(0, 1, step, (1,))
    for unit in between:
        activate(0, *unit)
    far(1, 1, *first)
    finish(0, *last)
    for step in range(3, reach):
        advance_wave(1, 1, step)
    scatter(0, 0)
    for unit in between:
        finish(0, *unit)
    advance_wave(0, 1, reach)
    back(1, *last)
    for unit in between:
        back(1, *unit)
    far(0, 1, *last)
    advance_wave(1, 1, reach)
    raw(1, *last)
    scatter(0, 1, (0,))
    far(1, 1, *last)
    finish(0, *first)
    activate(1, *first)
    scatter(0, 1, (1,))
    for unit in between:
        raw(1, *unit)
        far(0, 1, *unit)
    finish(1, *first)
    for unit in between:
        far(1, 1, *unit)
    scatter(0, 2)
    activate(1, *last)
    for step in range(3, reach):
        scatter(0, step)
    finish(1, *last)
    scatter(1, 0)
    for unit in between:
        activate(1, *unit)
        finish(1, *unit)
    settle(0)
    for step in range(1, reach):
        scatter(1, step)
    settle(1)
    drain()


def fused_device(queries, keys, values, w_in, w_out, routes, route_weights, grad_out):
    count = lax.axis_size("exp")
    tokens, width = queries.shape
    cached, kv_width = keys.shape
    hidden = w_in.shape[3]
    side = hidden // 2
    reach = count // 2
    half_rows = tokens // 2
    every = count * half_rows
    experts = w_in.shape[0] * count
    stacked = (kv_width // HEAD_WIDTH, width // kv_width * tokens, HEAD_WIDTH)

    def body(*refs):
        fused_kernel(count, *refs)

    def half(*shape):
        return pltpu.VMEM(shape, jnp.bfloat16)

    def whole(*shape):
        return pltpu.VMEM(shape, jnp.float32)

    dma = pltpu.SemaphoreType.DMA
    vmem = pl.BlockSpec(memory_space=pltpu.VMEM)
    anywhere = pl.BlockSpec(memory_space=pl.ANY)
    both = pl.pallas_call(
        body,
        out_shape=jax.ShapeDtypeStruct((2 * tokens, width), jnp.bfloat16),
        in_specs=[anywhere] * 8,
        out_specs=vmem,
        scratch_shapes=[
            half(tokens, width),
            pltpu.VMEM(routes.shape[::-1], routes.dtype),
            whole(*route_weights.shape[::-1]),
            half(width, 2, hidden),
            half(2, width, hidden),
            half(2, side, width),
            half(count, 2, cached, kv_width),
            half(2, every, width),
            half(2, every, width),
            whole(count, experts, tokens),
            whole(count, 8, tokens),
            whole(4, 8, tokens),
            whole(2, every, LANES),
            whole(2, every, LANES),
            whole(2, every, hidden),
            whole(2, every, side),
            half(2, every, hidden),
            half(2, every, side),
            half(2, every, hidden),
            half(2, every, side),
            half(2, every, hidden),
            half(2, every, side),
            half(2, every, hidden),
            half(2, every, side),
            half(2, every, 3 * side + LANES),
            half(2, every, 3 * side + LANES),
            half(2, every, 2 * width),
            half(2, 2, reach, half_rows, 2 * width),
            whole(half_rows, 2 * width),
            whole(*stacked),
            whole(*stacked),
            whole(*stacked),
            dma((8,)),
            dma((15,)),
            dma((reach,)),
            dma((2, 2, 2 * reach - 1)),
            dma((2, 2 * reach - 1)),
            dma((2,)),
            dma((1,)),
            dma((5 * 2 * (reach - 1) + 6,)),
        ],
        compiler_params=pltpu.CompilerParams(
            collective_id=1, has_side_effects=True, vmem_limit_bytes=60 * 1024 * 1024
        ),
        name="fused",
    )(
        queries,
        keys,
        values,
        w_in,
        w_out[0].reshape(2, side, width),
        routes.T,
        route_weights.T,
        grad_out.reshape(2, half_rows, width),
    )
    return both[:tokens], both[tokens:]


def solution(mesh):
    fused = 2 * TOP >= mesh.shape["exp"] and mesh.shape["exp"] == 8 and mesh.shape["head"] == 4
    in_specs = (
        P("exp", "head"),
        P("exp", "head"),
        P("exp", "head"),
        P("exp", "head", None, None),
        P("exp", None, "head"),
        P("exp", None),
        P("exp", None),
        P("exp", "head"),
    )
    out_specs = (P("exp", "head"), P("exp", "head"))
    return jax.shard_map(
        fused_device if fused else per_device, mesh=mesh, in_specs=in_specs, out_specs=out_specs, check_vma=False
    )
```

```python
import jax
import jax.numpy as jnp
from jax import lax
from jax.experimental import pallas as pl
from jax.experimental.pallas import tpu as pltpu
from jax.sharding import PartitionSpec as P

D = 4096
HEAD_WIDTH = 128
TOP = 6


norm_eps = 1e-05
hidden_logits = -1e30


def block_partial(query_rows, query_pos, rows_of_keys, value_rows, key_pos):
    row_count = query_rows.shape[0]
    count_of_blocks = rows_of_keys.shape[0]
    kv_heads = rows_of_keys.shape[2] // HEAD_WIDTH
    grouping_width = query_rows.shape[1] // HEAD_WIDTH // kv_heads
    heads_of_queries = query_rows.reshape(row_count, kv_heads, grouping_width, HEAD_WIDTH)
    key_heads = rows_of_keys.reshape(count_of_blocks, -1, kv_heads, HEAD_WIDTH)
    value_heads = value_rows.reshape(count_of_blocks, -1, kv_heads, HEAD_WIDTH)
    visible = (key_pos[:, None, :] <= query_pos[None, :, None])[:, :, None, None, :]
    scores = jnp.einsum(
        "tgid,bjgd->btgij", heads_of_queries, key_heads, preferred_element_type=jnp.float32
    ) * HEAD_WIDTH ** (-0.5)
    scores = jnp.where(visible, scores, hidden_logits)
    best_score = jnp.max(scores, axis=-1).astype(jnp.bfloat16)
    weights = jnp.where(visible, jnp.exp(scores - best_score.astype(jnp.float32)[..., None]), 0.0)
    weight_total = jnp.sum(weights, axis=-1).astype(jnp.bfloat16)
    weighted_sum = jnp.einsum(
        "btgij,bjgd->btgid",
        weights.astype(jnp.bfloat16),
        value_heads,
        preferred_element_type=jnp.float32,
    ).astype(jnp.bfloat16)
    head_count = kv_heads * grouping_width
    return (
        best_score.reshape(count_of_blocks, row_count, head_count),
        weight_total.reshape(count_of_blocks, row_count, head_count),
        weighted_sum.reshape(count_of_blocks, row_count, head_count * HEAD_WIDTH),
    )


def fold_partials(running, best_score, weight_total, weighted_sum):
    top_now, total_now, sums_now = running
    best_value = best_score.astype(jnp.float32)
    new_top = jnp.maximum(top_now, jnp.max(best_value, axis=0))
    old_factor = jnp.exp(top_now - new_top)
    block_factor = jnp.exp(best_value - new_top[None])
    total_next = total_now * old_factor + jnp.sum(
        weight_total.astype(jnp.float32) * block_factor, axis=0
    )
    spread_sums = weighted_sum.reshape(
        weighted_sum.shape[0], sums_now.shape[0], sums_now.shape[1], HEAD_WIDTH
    )
    sums_next = sums_now * old_factor[..., None] + jnp.sum(
        spread_sums.astype(jnp.float32) * block_factor[..., None], axis=0
    )
    return (new_top, total_next, sums_next)


def per_device(queries, keys, values, w_in, w_out, routes, route_weights, grad_out):
    exp_count = lax.axis_size("exp")
    exp_index = lax.axis_index("exp")
    head_devices = lax.axis_size("head")
    token_count = queries.shape[0]
    query_width = queries.shape[1]
    head_count = query_width // HEAD_WIDTH
    cache_rows = keys.shape[0]
    window = token_count * exp_count
    offset = cache_rows * exp_count - window
    beginning = (
        jnp.full((token_count, head_count), hidden_logits, jnp.float32),
        jnp.zeros((token_count, head_count), jnp.float32),
        jnp.zeros((token_count, head_count, HEAD_WIDTH), jnp.float32),
    )
    own_pos = offset + exp_index * token_count + jnp.arange(token_count, dtype=jnp.int32)
    key_piece = lax.all_gather(keys, "exp", axis=0, tiled=True)
    value_piece = lax.all_gather(values, "exp", axis=0, tiled=True)
    piece_blocks = key_piece.shape[0] // cache_rows
    key_split = key_piece.reshape(piece_blocks, cache_rows, -1)
    value_split = value_piece.reshape(piece_blocks, cache_rows, -1)
    pos_split = jnp.arange(key_piece.shape[0], dtype=jnp.int32).reshape(piece_blocks, cache_rows)

    def one_block(state, element):
        key_block, value_block, pos_block = element
        block_parts = block_partial(
            queries, own_pos, key_block[None], value_block[None], pos_block[None]
        )
        return (fold_partials(state, block_parts[0], block_parts[1], block_parts[2]), None)

    state, ignored = lax.scan(one_block, beginning, (key_split, value_split, pos_split))
    attended = (
        (state[2] / state[1][..., None]).reshape(token_count, query_width).astype(jnp.bfloat16)
    )
    row_width = attended.shape[1]
    experts_all = w_in.shape[0] * exp_count
    mean_load = TOP * token_count // experts_all
    capacity = mean_load + mean_load // 6
    places = experts_all * capacity
    flat_routes = routes.reshape(-1)
    expert_hits = (
        flat_routes[:, None] == jnp.arange(experts_all, dtype=jnp.int32)[None, :]
    ).astype(jnp.bfloat16)
    before = jnp.tri(flat_routes.shape[0], k=-1, dtype=jnp.bfloat16)
    earlier = jnp.dot(before, expert_hits, preferred_element_type=jnp.float32)
    slot_index = jnp.sum(earlier * expert_hits.astype(jnp.float32), axis=1).astype(jnp.int32)
    place_index = flat_routes * capacity + slot_index
    chosen = (place_index[:, None] == jnp.arange(places, dtype=jnp.int32)[None, :]).astype(
        jnp.bfloat16
    )
    picker = jnp.sum(chosen.reshape(token_count, TOP, places), axis=1)
    contract_rows = (((0,), (0,)), ((), ()))
    send_rows = lax.dot_general(picker, attended, contract_rows, preferred_element_type=jnp.float32)
    send_rows = send_rows.astype(jnp.bfloat16).reshape(experts_all, capacity, row_width)
    send_grads = lax.dot_general(
        picker, grad_out, contract_rows, preferred_element_type=jnp.float32
    )
    send_grads = send_grads.astype(jnp.bfloat16).reshape(experts_all, capacity, row_width)
    w_first = w_in[0]
    w_second = w_out[0]
    rows_in = lax.all_to_all(send_rows, "exp", split_axis=0, concat_axis=0, tiled=True)
    grads_in = lax.all_to_all(send_grads, "exp", split_axis=0, concat_axis=0, tiled=True)
    lead_count, item_count, width_in = rows_in.shape
    row_total = lead_count * item_count
    row_block = rows_in.reshape(row_total, width_in)
    grad_block = grads_in.reshape(row_total, width_in)
    row_float = row_block.astype(jnp.float32)
    raw_sums = jnp.einsum("rd,dkf->rkf", row_block, w_first, preferred_element_type=jnp.float32)
    back_sums = lax.dot_general(
        grad_block, w_second, (((1,), (1,)), ((), ())), preferred_element_type=jnp.float32
    )
    squares = jnp.sum(row_float * row_float, axis=1)
    square_tile = jnp.broadcast_to(squares[:, None, None], (row_total, 1, head_devices))
    raw_part = lax.psum_scatter(raw_sums, "head", scatter_dimension=2, tiled=True)
    back_part = lax.psum_scatter(back_sums[:, None, :], "head", scatter_dimension=2, tiled=True)
    square_part = lax.psum_scatter(square_tile, "head", scatter_dimension=2, tiled=True)
    norm_scale = lax.rsqrt(square_part[:, 0] / D + norm_eps)
    gate_value = raw_part[:, 0] * norm_scale
    up_value = raw_part[:, 1] * norm_scale
    back_value = back_part[:, 0]
    gate_sigmoid = jax.nn.sigmoid(gate_value)
    gate_silu = gate_value * gate_sigmoid
    act_part = (gate_silu * up_value).astype(jnp.bfloat16)
    grad_gate = back_value * up_value * gate_sigmoid * (1.0 + gate_value * (1.0 - gate_sigmoid))
    grad_up = back_value * gate_silu
    grad_part = jnp.stack([grad_gate, grad_up], axis=1).astype(jnp.bfloat16)
    inner_part = jnp.sum(
        grad_part.astype(jnp.float32) * jnp.stack([gate_value, up_value], axis=1), axis=(1, 2)
    )
    act_whole = lax.all_gather(act_part[:, None, :], "head", axis=2, tiled=True)
    grad_hidden = lax.all_gather(grad_part, "head", axis=2, tiled=True)
    hidden_act = act_whole[:, 0]
    inner_sum = lax.psum(inner_part, "head")
    out_rows = jnp.dot(hidden_act, w_second, preferred_element_type=jnp.float32).astype(
        jnp.bfloat16
    )
    grad_normed = jnp.einsum(
        "rkf,dkf->rd", grad_hidden, w_first, preferred_element_type=jnp.float32
    )
    grad_rows = (
        norm_scale * grad_normed - row_float * (norm_scale * norm_scale / D) * inner_sum[:, None]
    )
    expert_out = out_rows.reshape(lead_count, item_count, width_in)
    expert_grad = grad_rows.astype(jnp.bfloat16).reshape(lead_count, item_count, width_in)
    came_out, came_grad = (
        lax.all_to_all(expert_out, "exp", split_axis=0, concat_axis=0, tiled=True),
        lax.all_to_all(expert_grad, "exp", split_axis=0, concat_axis=0, tiled=True),
    )
    picked_out = came_out.reshape(places, row_width)[place_index].reshape(
        token_count, TOP, row_width
    )
    picked_grad = came_grad.reshape(places, row_width)[place_index].reshape(
        token_count, TOP, row_width
    )
    output = attended.astype(jnp.float32) + jnp.sum(
        route_weights[:, :, None] * picked_out.astype(jnp.float32), axis=1
    )
    grad_attended = grad_out.astype(jnp.float32) + jnp.sum(
        route_weights[:, :, None] * picked_grad.astype(jnp.float32), axis=1
    )
    return (output.astype(jnp.bfloat16), grad_attended.astype(jnp.bfloat16))


LANES = 128
EXACT = (((1,), (1,)), ((), ()))


def three_parts(value):
    high = value.astype(jnp.bfloat16)
    rest = value - high.astype(jnp.float32)
    middle = rest.astype(jnp.bfloat16)
    low = (rest - middle.astype(jnp.float32)).astype(jnp.bfloat16)
    return high, middle, low


def ring_place(index, count):
    outer, inner = index // 2, index % 2
    return outer + inner * (count - 1 - 2 * outer)


def ring_index(place, count):
    inner = place // (count // 2)
    return 2 * (place + inner * (count - 1 - 2 * place)) + inner


def ring_lanes(count):
    reach = count // 2
    return ((0, 0, reach), (1, 1, reach), (0, 1, reach - 1), (1, 0, reach - 1))


def slot_of(distance, count):
    if distance == 0:
        return 0
    if abs(distance) == count // 2:
        return count - 1
    return 2 * distance - 1 if distance > 0 else -2 * distance


def wide(value, width):
    return jnp.concatenate([value] * (width // value.shape[1]), axis=1)


def fused_kernel(
    count,
    queries_ref,
    k_ref,
    v_ref,
    w_in_ref,
    w_out_ref,
    routes_in_ref,
    shares_ref,
    grad_ref,
    results_ref,
    q_ref,
    routes_ref,
    share_ref,
    w_pairs,
    w_up,
    w_down,
    kv_all,
    grads,
    rows,
    tables,
    squares,
    head_squares,
    gains,
    scales,
    sum_raw,
    sum_back,
    near_raw,
    near_back,
    near_raw_in,
    near_back_in,
    far_raw,
    far_back,
    far_raw_in,
    far_back_in,
    act,
    act_in,
    parts,
    held,
    settled,
    best_so_far,
    total_so_far,
    mix_so_far,
    load_sem,
    send_sem,
    early_recv,
    wave_recv,
    scatter_recv,
    meta_recv,
    head_recv,
    pair_recv,
):
    reach = count // 2
    tokens, width = q_ref.shape
    cached, kv_width = k_ref.shape
    side = w_down.shape[1]
    experts = tables.shape[1]
    half = tokens // 2
    quarter = half // 2
    me = lax.axis_index("exp")
    place = ring_place(me, count)
    head = lax.axis_index("head")
    core = head % 2
    mate = head + 1 - 2 * core
    across = (head + 2) % 4
    corner = 3 - head
    others = (ring_index((place + 1) % count, count), ring_index((place + count - 1) % count, count))
    distances = [0] + [d for s in range(1, reach) for d in (s, -s)] + [reach]
    lanes = ((reach, 0), (reach - 1, reach))

    def remote(source, target, kind, recv_sem, where):
        return pltpu.make_async_remote_copy(
            src_ref=source,
            dst_ref=target,
            send_sem=send_sem.at[kind],
            recv_sem=recv_sem,
            device_id=where,
            device_id_type=pl.DeviceIdType.MESH,
        )

    def begin(*what):
        copy = remote(*what)
        copy.start()
        return copy

    loads = [
        pltpu.make_async_copy(source, target, load_sem.at[index])
        for index, (source, target) in enumerate(
            (
                (k_ref, kv_all.at[0, 0]),
                (v_ref, kv_all.at[0, 1]),
                (grad_ref, grads.at[:, pl.ds(0, half)]),
                (routes_in_ref, routes_ref),
                (shares_ref, share_ref),
                (w_in_ref.at[0], w_pairs),
                (w_out_ref, w_down),
                (queries_ref, q_ref),
            )
        )
    ]
    for each in loads:
        each.start()

    barrier = pltpu.get_barrier_semaphore()
    for other in (mate, across, corner):
        pl.semaphore_signal(
            barrier, inc=1, device_id={"head": other}, device_id_type=pl.DeviceIdType.MESH
        )
    for distance in distances[1:]:
        other = ring_index((place + distance + count) % count, count)
        pl.semaphore_signal(
            barrier, inc=1, device_id={"exp": other}, device_id_type=pl.DeviceIdType.MESH
        )

    for each in loads[:5]:
        each.wait()
    expert_row = lax.broadcasted_iota(jnp.int32, (experts, tokens), 0)
    table = jnp.zeros((experts, tokens), jnp.float32)
    for k in range(routes_ref.shape[0]):
        table = table + jnp.where(expert_row == routes_ref[k : k + 1, :], share_ref[k : k + 1, :], 0.0)
    tables[0] = table
    pl.semaphore_wait(barrier, 3 + count - 1)

    def advance(step):
        if step >= 1:
            both = kv_all.at[0] if step == reach else kv_all.at[pl.ds(0, 2)]
            remote(both, both, 0, early_recv.at[step - 1], {"head": mate}).wait_recv()
        for way in range(2 if step < reach else 0):
            sign = -1 if way == 0 else 1
            here, there = slot_of(sign * step, count), slot_of(sign * (step + 1), count)
            halved = step == reach - 1
            begin(
                kv_all.at[here, way] if halved else kv_all.at[here],
                kv_all.at[there, way] if halved else kv_all.at[there],
                0,
                early_recv.at[step],
                {"exp": others[way]},
            )

    def advance_wave(kind, wave, step, pairs_of=(0, 1)):
        store = rows if kind else grads
        for pair in pairs_of:
            steps, first = lanes[pair]
            if 1 <= step <= steps:
                both = store.at[wave, pl.ds(0, half)]
                arrived = wave_recv.at[kind, wave, first + step - 1]
                remote(both, both, 0, arrived, {"head": mate}).wait_recv()
            for way in range(2 if step < steps else 0):
                sub = way if pair == 0 else 1 - way
                sign = -1 if way == 0 else 1
                there = slot_of(sign * (step + 1), count) * half + sub * quarter
                here = slot_of(sign * step, count) * half + sub * quarter
                begin(
                    store.at[wave, pl.ds(here, quarter)],
                    store.at[wave, pl.ds(there, quarter)],
                    1 + 2 * kind + wave,
                    wave_recv.at[kind, wave, first + step],
                    {"exp": others[way]},
                )

    def broadcast(kind, store):
        for distance in distances[1:]:
            there = slot_of(-distance, count)
            other = ring_index((place + distance + count) % count, count)
            begin(store.at[0], store.at[there], 7 + kind, meta_recv.at[kind], {"exp": other})
        others_of = store.at[pl.ds(1, count - 1)]
        return remote(others_of, others_of, 7 + kind, meta_recv.at[kind], {"head": mate})

    def split():
        loads[5].wait()
        chunk = LANES
        to = lax.broadcasted_iota(jnp.int32, (2 * chunk, 2 * chunk), 0)
        source = lax.broadcasted_iota(jnp.int32, (2 * chunk, 2 * chunk), 1)
        picks = (source == jnp.where(to < chunk, 2 * to, 2 * to - 2 * chunk + 1)).astype(jnp.bfloat16)

        def split_chunk(index, carry):
            span = pl.ds(pl.multiple_of(index * chunk, chunk), chunk)
            pairs = w_pairs[span].reshape(2 * chunk, 2 * side)
            apart = jnp.dot(picks, pairs, preferred_element_type=jnp.float32).astype(jnp.bfloat16)
            for part in range(2):
                cols = slice(part * side, (part + 1) * side)
                w_up[part, span, :side] = apart[:chunk, cols]
                w_up[part, span, side:] = apart[chunk:, cols]
            return carry

        lax.fori_loop(0, width // chunk, split_chunk, 0)
        loads[6].wait()
        loads[7].wait()

    pairs = {}

    def pair_begin(kind, wave, slot, blocks, source, target, other):
        span = pl.ds(slot * half, blocks * half)
        pairs[kind, wave, slot] = begin(
            source.at[wave, span],
            target.at[wave, span],
            9 + kind,
            pair_recv.at[len(pairs)],
            {"head": other},
        )

    def back(wave, slot, blocks):
        span = slice(slot * half, (slot + blocks) * half)
        weights = jnp.concatenate([w_down[1 - core], w_down[core]], axis=0)
        both = lax.dot_general(
            grads[wave, span, :], weights, EXACT, preferred_element_type=jnp.float32
        )
        near_back[wave, span, :] = both[:, :side].astype(jnp.bfloat16)
        pair_begin(0, wave, slot, blocks, near_back, near_back_in, mate)
        sum_back[wave, span, :] = both[:, side:]

    def raw(wave, slot, blocks):
        span = slice(slot * half, (slot + blocks) * half)
        block = rows[wave, span, :]
        near_raw[wave, span, :] = jnp.dot(
            block, w_up[1 - core], preferred_element_type=jnp.float32
        ).astype(jnp.bfloat16)
        pair_begin(1, wave, slot, blocks, near_raw, near_raw_in, mate)
        sum_raw[wave, span, :] = jnp.dot(block, w_up[core], preferred_element_type=jnp.float32)

    def far(kind, wave, slot, blocks):
        total, near_in = ((sum_back, near_back_in), (sum_raw, near_raw_in))[kind]
        out, target = ((far_back, far_back_in), (far_raw, far_raw_in))[kind]
        span = slice(slot * half, (slot + blocks) * half)
        pairs[kind, wave, slot].wait_recv()
        both = total[wave, span, :] + near_in[wave, span, :].astype(jnp.float32)
        total[wave, span, :] = both
        out[wave, span, :] = both.astype(jnp.bfloat16)
        pair_begin(2 + kind, wave, slot, blocks, out, target, across)

    groups = kv_width // HEAD_WIDTH
    together = width // kv_width

    def visible_in(low, high):
        size = (high - low) * cached
        column = low * cached + lax.broadcasted_iota(jnp.int32, (1, size), 1)
        shift = jnp.zeros((1, size), jnp.int32)
        for slot in range(low, high):
            owner = ring_index((place + distances[slot] + count) % count, count)
            shift = jnp.where(column // cached == slot, (owner - slot) * cached, shift)
        row_pos = (
            count * (cached - tokens)
            + me * tokens
            + lax.broadcasted_iota(jnp.int32, (tokens, size), 0)
        )
        row_pos = jnp.concatenate([row_pos] * together, axis=0)
        return jnp.broadcast_to(shift + column, row_pos.shape) <= row_pos

    def scores_in(group, low, high, visible):
        first_head = group * together
        stacked = jnp.concatenate(
            [
                q_ref[:, one * HEAD_WIDTH : (one + 1) * HEAD_WIDTH]
                for one in range(first_head, first_head + together)
            ],
            axis=0,
        )
        scores = lax.dot_general(
            stacked,
            kv_all[low:high, 0, :, group * HEAD_WIDTH : (group + 1) * HEAD_WIDTH].reshape(
                (high - low) * cached, HEAD_WIDTH
            ),
            EXACT,
            preferred_element_type=jnp.float32,
        ) * HEAD_WIDTH ** (-0.5)
        return jnp.where(visible, scores, hidden_logits)

    def values_in(group, low, high, weights):
        return jnp.dot(
            weights.astype(jnp.bfloat16),
            kv_all[low:high, 1, :, group * HEAD_WIDTH : (group + 1) * HEAD_WIDTH].reshape(
                (high - low) * cached, HEAD_WIDTH
            ),
            preferred_element_type=jnp.float32,
        )

    def attend_most():
        visible = visible_in(0, count - 1)
        for group in range(groups):
            scores = scores_in(group, 0, count - 1, visible)
            best = jnp.max(scores, axis=1, keepdims=True)
            weights = jnp.exp(scores - best)
            total = jnp.sum(weights, axis=1, keepdims=True)
            best_so_far[group] = jnp.broadcast_to(best, (together * tokens, HEAD_WIDTH))
            total_so_far[group] = jnp.broadcast_to(total, (together * tokens, HEAD_WIDTH))
            mix_so_far[group] = values_in(group, 0, count - 1, weights)

    def attention():
        visible = visible_in(count - 1, count)
        squared = jnp.zeros((tokens, LANES), jnp.float32)
        for group in range(groups):
            scores = scores_in(group, count - 1, count, visible)
            before = best_so_far[group]
            best = jnp.maximum(before, jnp.max(scores, axis=1, keepdims=True))
            weights = jnp.exp(scores - best[:, :1])
            factor = jnp.exp(before - best)
            total = total_so_far[group] * factor + jnp.sum(weights, axis=1, keepdims=True)
            mixed = mix_so_far[group] * factor + values_in(group, count - 1, count, weights)
            mixed = (mixed / total).astype(jnp.bfloat16)
            for one in range(together):
                start = (group * together + one) * HEAD_WIDTH
                cols = slice(start, start + HEAD_WIDTH)
                part = mixed[one * tokens : (one + 1) * tokens]
                rows[0, 0:half, cols] = part[:half]
                rows[1, 0:half, cols] = part[half:]
                part = part.astype(jnp.float32)
                squared = squared + part * part
        return squared

    def share_squares(total):
        columns = jnp.broadcast_to(jnp.sum(total, axis=1, keepdims=True), (tokens, LANES))
        head_squares[0] = jnp.transpose(columns)[: head_squares.shape[1]]
        for index, other in enumerate((mate, across, corner)):
            begin(
                head_squares.at[0],
                head_squares.at[index + 1],
                14,
                head_recv.at[0],
                {"head": other},
            )

    def spread_squares():
        others_of = head_squares.at[pl.ds(1, 3)]
        remote(others_of, others_of, 14, head_recv.at[0], {"head": mate}).wait_recv()
        squares[0] = (head_squares[0] + head_squares[1]) + (head_squares[2] + head_squares[3])
        return broadcast(1, squares)

    def fill(store, slot, row):
        columns = jnp.transpose(jnp.broadcast_to(row, (LANES, tokens)))
        for wave in range(2):
            store[wave, slot * half : (slot + 1) * half, :] = columns[wave * half : (wave + 1) * half]

    def fill_gains(copies):
        copies.wait_recv()
        for slot in range(count):
            row = jnp.sum(jnp.where(expert_row == me, tables[slot], 0.0), axis=0, keepdims=True)
            fill(gains, slot, row)

    def fill_scales(copies):
        copies.wait_recv()
        for slot in range(count):
            fill(scales, slot, lax.rsqrt(squares[slot][0:1, :] / D + norm_eps))

    def activate(wave, slot, blocks):
        for kind in (2, 3):
            for one in range(slot, slot + blocks):
                if (kind, wave, one) in pairs:
                    pairs[kind, wave, one].wait_recv()
        step = 32
        lane = lax.broadcasted_iota(jnp.int32, (step, LANES), 1)

        def some_rows(index, carry):
            span = pl.ds(pl.multiple_of(slot * half + index * step, step), step)
            scale = scales[wave, span, :]
            gain = gains[wave, span, :]
            inner = jnp.zeros((step, LANES), jnp.float32)
            for start in range(0, side, LANES):
                cols = slice(start, start + LANES)
                up_cols = slice(side + start, side + start + LANES)
                down_cols = slice(2 * side + start, 2 * side + start + LANES)
                gate = sum_raw[wave, span, cols] + far_raw_in[wave, span, cols].astype(jnp.float32)
                up = sum_raw[wave, span, up_cols] + far_raw_in[wave, span, up_cols].astype(
                    jnp.float32
                )
                gate, up = gate * scale, up * scale
                back_value = sum_back[wave, span, cols] + far_back_in[wave, span, cols].astype(
                    jnp.float32
                )
                sigmoid = jax.nn.sigmoid(gate)
                silu = gate * sigmoid
                grad_gate = back_value * up * sigmoid * (1.0 + gate * (1.0 - sigmoid))
                grad_up = back_value * silu
                inner = inner + (grad_gate * gate + grad_up * up)
                act[wave, span, cols] = (gain * (silu * up)).astype(jnp.bfloat16)
                act[wave, span, up_cols] = (gain * scale * grad_gate).astype(jnp.bfloat16)
                act[wave, span, down_cols] = (gain * scale * grad_up).astype(jnp.bfloat16)
            high, middle, low = three_parts(
                jnp.broadcast_to(jnp.sum(inner, axis=1, keepdims=True), (step, LANES))
            )
            zero = jnp.zeros((step, LANES), jnp.float32)
            spread = jnp.where(lane == 0, high.astype(jnp.float32), zero)
            spread = jnp.where(lane == 1, middle.astype(jnp.float32), spread)
            spread = jnp.where(lane == 2, low.astype(jnp.float32), spread)
            act[wave, span, 3 * side :] = spread.astype(jnp.bfloat16)
            return carry

        lax.fori_loop(0, blocks * half // step, some_rows, 0)
        pair_begin(4, wave, slot, blocks, act, act_in, mate)

    def finish(wave, slot, blocks):
        span = slice(slot * half, (slot + blocks) * half)
        pairs[4, wave, slot].wait_recv()
        inner = jnp.sum(
            act[wave, span, 3 * side :].astype(jnp.float32)
            + act_in[wave, span, 3 * side :].astype(jnp.float32),
            axis=1,
            keepdims=True,
        )
        tile = 256
        scale = scales[wave, span, :]
        bent = wide(gains[wave, span, :] * (scale * scale / D) * inner, tile)
        hidden = slice(0, side)
        slopes = slice(side, 3 * side)
        act_all = jnp.concatenate([act[wave, span, hidden], act_in[wave, span, hidden]], axis=1)
        for start in range(0, width, tile):
            cols = slice(start, start + tile)
            weights = jnp.concatenate([w_down[core, :, cols], w_down[1 - core, :, cols]], axis=0)
            out = jnp.dot(act_all, weights, preferred_element_type=jnp.float32)
            parts[wave, span, cols] = out.astype(jnp.bfloat16)
            grad = lax.dot_general(
                act[wave, span, slopes],
                w_up[core, cols, :],
                EXACT,
                preferred_element_type=jnp.float32,
            ) + lax.dot_general(
                act_in[wave, span, slopes],
                w_up[1 - core, cols, :],
                EXACT,
                preferred_element_type=jnp.float32,
            )
            grad = grad - bent * rows[wave, span, cols].astype(jnp.float32)
            parts[wave, span, width + start : width + start + tile] = grad.astype(jnp.bfloat16)

    def arrived(wave, pair, step):
        both = parts.at[wave, pl.ds(0, half)]
        where = scatter_recv.at[wave, lanes[pair][1] + step]
        remote(both, both, 0, where, {"head": mate}).wait_recv()

    def scatter(wave, step, pairs_of=(0, 1)):
        for pair, (steps, first) in enumerate(lanes):
            if step >= steps or pair not in pairs_of:
                continue
            if step > 0:
                arrived(wave, pair, step - 1)
            for way in range(2):
                sub = way if pair == 0 else 1 - way
                sign = 1 if way == 0 else -1
                start = slot_of(sign * (steps - step), count) * half + sub * quarter
                block = parts.at[wave, pl.ds(start, quarter)]
                there = pl.ds(sub * quarter, quarter)
                if step > 0:
                    sum_ref = held.at[wave, way, step - 1, there]
                    sum_ref[...] = (
                        sum_ref[...].astype(jnp.float32) + block[...].astype(jnp.float32)
                    ).astype(jnp.bfloat16)
                    block = sum_ref
                begin(
                    block,
                    held.at[wave, way, step, there],
                    5 + wave,
                    scatter_recv.at[wave, first + step],
                    {"exp": others[way]},
                )

    def settle(wave):
        sides = ((rows, slice(0, width)), (grads, slice(width, 2 * width)))
        arrived(wave, 1, reach - 2)
        for sub in range(2):
            span = slice(sub * quarter, (sub + 1) * quarter)
            for base, cols in sides:
                settled[span, cols] = base[wave, span, :].astype(jnp.float32) + (
                    parts[wave, span, cols].astype(jnp.float32)
                    + held[wave, 1 - sub, reach - 2, span, cols].astype(jnp.float32)
                )
        arrived(wave, 0, reach - 1)
        for sub in range(2):
            span = slice(sub * quarter, (sub + 1) * quarter)
            for index, (base, cols) in enumerate(sides):
                start = index * tokens + wave * half + sub * quarter
                results_ref[start : start + quarter, :] = (
                    settled[span, cols] + held[wave, sub, reach - 1, span, cols].astype(jnp.float32)
                ).astype(jnp.bfloat16)

    def drain():
        others_of = pl.ds(half, (count - 1) * half)
        for kind, sent in enumerate(
            (
                kv_all.at[pl.ds(1, count - 1)],
                grads.at[0, others_of],
                grads.at[1, others_of],
                rows.at[0, others_of],
                rows.at[1, others_of],
                parts.at[0, others_of],
                parts.at[1, others_of],
                tables.at[pl.ds(1, count - 1)],
                squares.at[pl.ds(1, count - 1)],
                near_back,
                near_raw,
                far_back,
                far_raw,
                act,
                head_squares.at[pl.ds(1, 3)],
            )
        ):
            remote(sent, sent, kind, head_recv.at[0], {"head": mate}).wait_send()

    first = (0, 3)
    between = [(2 * step - 1, 2) for step in range(2, reach - 1)]
    last = (2 * reach - 3, 3)
    advance(0)
    advance_wave(0, 0, 0)
    table_copies = broadcast(0, tables)
    split()
    advance(1)
    advance_wave(0, 0, 1)
    back(0, *first)
    advance(2)
    far(0, 0, *first)
    advance_wave(0, 0, 2)
    for step in range(3, reach):
        back(0, *between[step - 3])
        advance(step)
        far(0, 0, *between[step - 3])
        if step == reach - 1:
            attend_most()
        advance_wave(0, 0, step)
    back(0, count - 3, 2)
    advance(reach)
    advance_wave(0, 1, 0, (0,))
    square_total = attention()
    advance_wave(1, 0, 0)
    share_squares(square_total)
    far(0, 0, count - 3, 2)
    advance_wave(0, 0, reach)
    back(0, count - 1, 1)
    advance_wave(0, 1, 1, (0,))
    raw(0, 0, 1)
    far(0, 0, count - 1, 1)
    square_copies = spread_squares()
    far(1, 0, 0, 1)
    advance_wave(1, 0, 1)
    raw(0, 1, 2)
    advance_wave(0, 1, 2, (0,))
    far(1, 0, 1, 2)
    advance_wave(1, 0, 2)
    advance_wave(0, 1, 0, (1,))
    for unit in between[:1]:
        raw(0, *unit)
    for unit in between[:1]:
        far(1, 0, *unit)
    for step in range(3, reach):
        advance_wave(1, 0, step)
        if step == reach - 1:
            advance_wave(1, 1, 0)
        raw(0, 2 * step - 1, 2)
    advance_wave(0, 1, 3, (0,))
    for step in range(3, reach):
        far(1, 0, 2 * step - 1, 2)
    advance_wave(0, 1, 1, (1,))
    advance_wave(1, 0, reach)
    raw(0, count - 1, 1)
    fill_gains(table_copies)
    far(1, 0, count - 1, 1)
    fill_scales(square_copies)
    advance_wave(1, 1, 1)
    raw(1, *first)
    activate(0, *first)
    far(1, 1, *first)
    advance_wave(0, 1, 2, (1,))
    back(1, *first)
    activate(0, *last)
    advance_wave(1, 1, 2)
    far(0, 1, *first)
    for unit in between:
        activate(0, *unit)
    finish(0, *last)
    for step in range(3, reach):
        advance_wave(0, 1, step, (1,))
    for step in range(3, reach):
        advance_wave(1, 1, step)
    scatter(0, 0)
    for unit in between:
        finish(0, *unit)
    advance_wave(0, 1, reach)
    back(1, *last)
    for unit in between:
        back(1, *unit)
    far(0, 1, *last)
    advance_wave(1, 1, reach)
    raw(1, *last)
    scatter(0, 1, (0,))
    far(1, 1, *last)
    finish(0, *first)
    activate(1, *first)
    scatter(0, 1, (1,))
    for unit in between:
        raw(1, *unit)
        far(0, 1, *unit)
    finish(1, *first)
    for unit in between:
        far(1, 1, *unit)
    scatter(0, 2)
    activate(1, *last)
    for step in range(3, reach):
        scatter(0, step)
    finish(1, *last)
    scatter(1, 0)
    for unit in between:
        activate(1, *unit)
        finish(1, *unit)
    settle(0)
    for step in range(1, reach):
        scatter(1, step)
    settle(1)
    drain()


def fused_device(queries, keys, values, w_in, w_out, routes, route_weights, grad_out):
    count = lax.axis_size("exp")
    tokens, width = queries.shape
    cached, kv_width = keys.shape
    hidden = w_in.shape[3]
    side = hidden // 2
    reach = count // 2
    half_rows = tokens // 2
    every = count * half_rows
    experts = w_in.shape[0] * count
    stacked = (kv_width // HEAD_WIDTH, width // kv_width * tokens, HEAD_WIDTH)

    def body(*refs):
        fused_kernel(count, *refs)

    def half(*shape):
        return pltpu.VMEM(shape, jnp.bfloat16)

    def whole(*shape):
        return pltpu.VMEM(shape, jnp.float32)

    dma = pltpu.SemaphoreType.DMA
    vmem = pl.BlockSpec(memory_space=pltpu.VMEM)
    anywhere = pl.BlockSpec(memory_space=pl.ANY)
    both = pl.pallas_call(
        body,
        out_shape=jax.ShapeDtypeStruct((2 * tokens, width), jnp.bfloat16),
        in_specs=[anywhere] * 8,
        out_specs=vmem,
        scratch_shapes=[
            half(tokens, width),
            pltpu.VMEM(routes.shape[::-1], routes.dtype),
            whole(*route_weights.shape[::-1]),
            half(width, 2, hidden),
            half(2, width, hidden),
            half(2, side, width),
            half(count, 2, cached, kv_width),
            half(2, every, width),
            half(2, every, width),
            whole(count, experts, tokens),
            whole(count, 8, tokens),
            whole(4, 8, tokens),
            whole(2, every, LANES),
            whole(2, every, LANES),
            whole(2, every, hidden),
            whole(2, every, side),
            half(2, every, hidden),
            half(2, every, side),
            half(2, every, hidden),
            half(2, every, side),
            half(2, every, hidden),
            half(2, every, side),
            half(2, every, hidden),
            half(2, every, side),
            half(2, every, 3 * side + LANES),
            half(2, every, 3 * side + LANES),
            half(2, every, 2 * width),
            half(2, 2, reach, half_rows, 2 * width),
            whole(half_rows, 2 * width),
            whole(*stacked),
            whole(*stacked),
            whole(*stacked),
            dma((8,)),
            dma((15,)),
            dma((reach,)),
            dma((2, 2, 2 * reach - 1)),
            dma((2, 2 * reach - 1)),
            dma((2,)),
            dma((1,)),
            dma((5 * 2 * (reach - 1) + 6,)),
        ],
        compiler_params=pltpu.CompilerParams(
            collective_id=1, has_side_effects=True, vmem_limit_bytes=60 * 1024 * 1024
        ),
        name="fused",
    )(
        queries,
        keys,
        values,
        w_in,
        w_out[0].reshape(2, side, width),
        routes.T,
        route_weights.T,
        grad_out.reshape(2, half_rows, width),
    )
    return both[:tokens], both[tokens:]


def solution(mesh):
    fused = 2 * TOP >= mesh.shape["exp"] and mesh.shape["exp"] == 8 and mesh.shape["head"] == 4
    in_specs = (
        P("exp", "head"),
        P("exp", "head"),
        P("exp", "head"),
        P("exp", "head", None, None),
        P("exp", None, "head"),
        P("exp", None),
        P("exp", None),
        P("exp", "head"),
    )
    out_specs = (P("exp", "head"), P("exp", "head"))
    return jax.shard_map(
        fused_device if fused else per_device, mesh=mesh, in_specs=in_specs, out_specs=out_specs, check_vma=False
    )
```

```python
import jax
import jax.numpy as jnp
from jax import lax
from jax.experimental import pallas as pl
from jax.experimental.pallas import tpu as pltpu
from jax.sharding import PartitionSpec as P

D = 4096
HEAD_WIDTH = 128
TOP = 6


norm_eps = 1e-05
hidden_logits = -1e30


def block_partial(query_rows, query_pos, rows_of_keys, value_rows, key_pos):
    row_count = query_rows.shape[0]
    count_of_blocks = rows_of_keys.shape[0]
    kv_heads = rows_of_keys.shape[2] // HEAD_WIDTH
    grouping_width = query_rows.shape[1] // HEAD_WIDTH // kv_heads
    heads_of_queries = query_rows.reshape(row_count, kv_heads, grouping_width, HEAD_WIDTH)
    key_heads = rows_of_keys.reshape(count_of_blocks, -1, kv_heads, HEAD_WIDTH)
    value_heads = value_rows.reshape(count_of_blocks, -1, kv_heads, HEAD_WIDTH)
    visible = (key_pos[:, None, :] <= query_pos[None, :, None])[:, :, None, None, :]
    scores = jnp.einsum(
        "tgid,bjgd->btgij", heads_of_queries, key_heads, preferred_element_type=jnp.float32
    ) * HEAD_WIDTH ** (-0.5)
    scores = jnp.where(visible, scores, hidden_logits)
    best_score = jnp.max(scores, axis=-1).astype(jnp.bfloat16)
    weights = jnp.where(visible, jnp.exp(scores - best_score.astype(jnp.float32)[..., None]), 0.0)
    weight_total = jnp.sum(weights, axis=-1).astype(jnp.bfloat16)
    weighted_sum = jnp.einsum(
        "btgij,bjgd->btgid",
        weights.astype(jnp.bfloat16),
        value_heads,
        preferred_element_type=jnp.float32,
    ).astype(jnp.bfloat16)
    head_count = kv_heads * grouping_width
    return (
        best_score.reshape(count_of_blocks, row_count, head_count),
        weight_total.reshape(count_of_blocks, row_count, head_count),
        weighted_sum.reshape(count_of_blocks, row_count, head_count * HEAD_WIDTH),
    )


def fold_partials(running, best_score, weight_total, weighted_sum):
    top_now, total_now, sums_now = running
    best_value = best_score.astype(jnp.float32)
    new_top = jnp.maximum(top_now, jnp.max(best_value, axis=0))
    old_factor = jnp.exp(top_now - new_top)
    block_factor = jnp.exp(best_value - new_top[None])
    total_next = total_now * old_factor + jnp.sum(
        weight_total.astype(jnp.float32) * block_factor, axis=0
    )
    spread_sums = weighted_sum.reshape(
        weighted_sum.shape[0], sums_now.shape[0], sums_now.shape[1], HEAD_WIDTH
    )
    sums_next = sums_now * old_factor[..., None] + jnp.sum(
        spread_sums.astype(jnp.float32) * block_factor[..., None], axis=0
    )
    return (new_top, total_next, sums_next)


def per_device(queries, keys, values, w_in, w_out, routes, route_weights, grad_out):
    exp_count = lax.axis_size("exp")
    exp_index = lax.axis_index("exp")
    head_devices = lax.axis_size("head")
    token_count = queries.shape[0]
    query_width = queries.shape[1]
    head_count = query_width // HEAD_WIDTH
    cache_rows = keys.shape[0]
    window = token_count * exp_count
    offset = cache_rows * exp_count - window
    beginning = (
        jnp.full((token_count, head_count), hidden_logits, jnp.float32),
        jnp.zeros((token_count, head_count), jnp.float32),
        jnp.zeros((token_count, head_count, HEAD_WIDTH), jnp.float32),
    )
    own_pos = offset + exp_index * token_count + jnp.arange(token_count, dtype=jnp.int32)
    key_piece = lax.all_gather(keys, "exp", axis=0, tiled=True)
    value_piece = lax.all_gather(values, "exp", axis=0, tiled=True)
    piece_blocks = key_piece.shape[0] // cache_rows
    key_split = key_piece.reshape(piece_blocks, cache_rows, -1)
    value_split = value_piece.reshape(piece_blocks, cache_rows, -1)
    pos_split = jnp.arange(key_piece.shape[0], dtype=jnp.int32).reshape(piece_blocks, cache_rows)

    def one_block(state, element):
        key_block, value_block, pos_block = element
        block_parts = block_partial(
            queries, own_pos, key_block[None], value_block[None], pos_block[None]
        )
        return (fold_partials(state, block_parts[0], block_parts[1], block_parts[2]), None)

    state, ignored = lax.scan(one_block, beginning, (key_split, value_split, pos_split))
    attended = (
        (state[2] / state[1][..., None]).reshape(token_count, query_width).astype(jnp.bfloat16)
    )
    row_width = attended.shape[1]
    experts_all = w_in.shape[0] * exp_count
    mean_load = TOP * token_count // experts_all
    capacity = mean_load + mean_load // 6
    places = experts_all * capacity
    flat_routes = routes.reshape(-1)
    expert_hits = (
        flat_routes[:, None] == jnp.arange(experts_all, dtype=jnp.int32)[None, :]
    ).astype(jnp.bfloat16)
    before = jnp.tri(flat_routes.shape[0], k=-1, dtype=jnp.bfloat16)
    earlier = jnp.dot(before, expert_hits, preferred_element_type=jnp.float32)
    slot_index = jnp.sum(earlier * expert_hits.astype(jnp.float32), axis=1).astype(jnp.int32)
    place_index = flat_routes * capacity + slot_index
    chosen = (place_index[:, None] == jnp.arange(places, dtype=jnp.int32)[None, :]).astype(
        jnp.bfloat16
    )
    picker = jnp.sum(chosen.reshape(token_count, TOP, places), axis=1)
    contract_rows = (((0,), (0,)), ((), ()))
    send_rows = lax.dot_general(picker, attended, contract_rows, preferred_element_type=jnp.float32)
    send_rows = send_rows.astype(jnp.bfloat16).reshape(experts_all, capacity, row_width)
    send_grads = lax.dot_general(
        picker, grad_out, contract_rows, preferred_element_type=jnp.float32
    )
    send_grads = send_grads.astype(jnp.bfloat16).reshape(experts_all, capacity, row_width)
    w_first = w_in[0]
    w_second = w_out[0]
    rows_in = lax.all_to_all(send_rows, "exp", split_axis=0, concat_axis=0, tiled=True)
    grads_in = lax.all_to_all(send_grads, "exp", split_axis=0, concat_axis=0, tiled=True)
    lead_count, item_count, width_in = rows_in.shape
    row_total = lead_count * item_count
    row_block = rows_in.reshape(row_total, width_in)
    grad_block = grads_in.reshape(row_total, width_in)
    row_float = row_block.astype(jnp.float32)
    raw_sums = jnp.einsum("rd,dkf->rkf", row_block, w_first, preferred_element_type=jnp.float32)
    back_sums = lax.dot_general(
        grad_block, w_second, (((1,), (1,)), ((), ())), preferred_element_type=jnp.float32
    )
    squares = jnp.sum(row_float * row_float, axis=1)
    square_tile = jnp.broadcast_to(squares[:, None, None], (row_total, 1, head_devices))
    raw_part = lax.psum_scatter(raw_sums, "head", scatter_dimension=2, tiled=True)
    back_part = lax.psum_scatter(back_sums[:, None, :], "head", scatter_dimension=2, tiled=True)
    square_part = lax.psum_scatter(square_tile, "head", scatter_dimension=2, tiled=True)
    norm_scale = lax.rsqrt(square_part[:, 0] / D + norm_eps)
    gate_value = raw_part[:, 0] * norm_scale
    up_value = raw_part[:, 1] * norm_scale
    back_value = back_part[:, 0]
    gate_sigmoid = jax.nn.sigmoid(gate_value)
    gate_silu = gate_value * gate_sigmoid
    act_part = (gate_silu * up_value).astype(jnp.bfloat16)
    grad_gate = back_value * up_value * gate_sigmoid * (1.0 + gate_value * (1.0 - gate_sigmoid))
    grad_up = back_value * gate_silu
    grad_part = jnp.stack([grad_gate, grad_up], axis=1).astype(jnp.bfloat16)
    inner_part = jnp.sum(
        grad_part.astype(jnp.float32) * jnp.stack([gate_value, up_value], axis=1), axis=(1, 2)
    )
    act_whole = lax.all_gather(act_part[:, None, :], "head", axis=2, tiled=True)
    grad_hidden = lax.all_gather(grad_part, "head", axis=2, tiled=True)
    hidden_act = act_whole[:, 0]
    inner_sum = lax.psum(inner_part, "head")
    out_rows = jnp.dot(hidden_act, w_second, preferred_element_type=jnp.float32).astype(
        jnp.bfloat16
    )
    grad_normed = jnp.einsum(
        "rkf,dkf->rd", grad_hidden, w_first, preferred_element_type=jnp.float32
    )
    grad_rows = (
        norm_scale * grad_normed - row_float * (norm_scale * norm_scale / D) * inner_sum[:, None]
    )
    expert_out = out_rows.reshape(lead_count, item_count, width_in)
    expert_grad = grad_rows.astype(jnp.bfloat16).reshape(lead_count, item_count, width_in)
    came_out, came_grad = (
        lax.all_to_all(expert_out, "exp", split_axis=0, concat_axis=0, tiled=True),
        lax.all_to_all(expert_grad, "exp", split_axis=0, concat_axis=0, tiled=True),
    )
    picked_out = came_out.reshape(places, row_width)[place_index].reshape(
        token_count, TOP, row_width
    )
    picked_grad = came_grad.reshape(places, row_width)[place_index].reshape(
        token_count, TOP, row_width
    )
    output = attended.astype(jnp.float32) + jnp.sum(
        route_weights[:, :, None] * picked_out.astype(jnp.float32), axis=1
    )
    grad_attended = grad_out.astype(jnp.float32) + jnp.sum(
        route_weights[:, :, None] * picked_grad.astype(jnp.float32), axis=1
    )
    return (output.astype(jnp.bfloat16), grad_attended.astype(jnp.bfloat16))


LANES = 128
EXACT = (((1,), (1,)), ((), ()))


def three_parts(value):
    high = value.astype(jnp.bfloat16)
    rest = value - high.astype(jnp.float32)
    middle = rest.astype(jnp.bfloat16)
    low = (rest - middle.astype(jnp.float32)).astype(jnp.bfloat16)
    return high, middle, low


def ring_place(index, count):
    outer, inner = index // 2, index % 2
    return outer + inner * (count - 1 - 2 * outer)


def ring_index(place, count):
    inner = place // (count // 2)
    return 2 * (place + inner * (count - 1 - 2 * place)) + inner


def ring_lanes(count):
    reach = count // 2
    return ((0, 0, reach), (1, 1, reach), (0, 1, reach - 1), (1, 0, reach - 1))


def slot_of(distance, count):
    if distance == 0:
        return 0
    if abs(distance) == count // 2:
        return count - 1
    return 2 * distance - 1 if distance > 0 else -2 * distance


def wide(value, width):
    return jnp.concatenate([value] * (width // value.shape[1]), axis=1)


def fused_kernel(
    count,
    queries_ref,
    k_ref,
    v_ref,
    w_in_ref,
    w_out_ref,
    routes_in_ref,
    shares_ref,
    grad_ref,
    results_ref,
    q_ref,
    routes_ref,
    share_ref,
    w_pairs,
    w_up,
    w_down,
    kv_all,
    grads,
    rows,
    tables,
    squares,
    head_squares,
    gains,
    scales,
    sum_raw,
    sum_back,
    near_raw,
    near_back,
    near_raw_in,
    near_back_in,
    far_raw,
    far_back,
    far_raw_in,
    far_back_in,
    act,
    act_in,
    parts,
    held,
    settled,
    best_so_far,
    total_so_far,
    mix_so_far,
    load_sem,
    send_sem,
    early_recv,
    wave_recv,
    scatter_recv,
    meta_recv,
    head_recv,
    pair_recv,
):
    reach = count // 2
    tokens, width = q_ref.shape
    cached, kv_width = k_ref.shape
    side = w_down.shape[1]
    experts = tables.shape[1]
    half = tokens // 2
    quarter = half // 2
    me = lax.axis_index("exp")
    place = ring_place(me, count)
    head = lax.axis_index("head")
    core = head % 2
    mate = head + 1 - 2 * core
    across = (head + 2) % 4
    corner = 3 - head
    others = (ring_index((place + 1) % count, count), ring_index((place + count - 1) % count, count))
    distances = [0] + [d for s in range(1, reach) for d in (s, -s)] + [reach]
    lanes = ((reach, 0), (reach - 1, reach))

    def remote(source, target, kind, recv_sem, where):
        return pltpu.make_async_remote_copy(
            src_ref=source,
            dst_ref=target,
            send_sem=send_sem.at[kind],
            recv_sem=recv_sem,
            device_id=where,
            device_id_type=pl.DeviceIdType.MESH,
        )

    def begin(*what):
        copy = remote(*what)
        copy.start()
        return copy

    loads = [
        pltpu.make_async_copy(source, target, load_sem.at[index])
        for index, (source, target) in enumerate(
            (
                (k_ref, kv_all.at[0, 0]),
                (v_ref, kv_all.at[0, 1]),
                (grad_ref, grads.at[:, pl.ds(0, half)]),
                (routes_in_ref, routes_ref),
                (shares_ref, share_ref),
                (w_in_ref.at[0], w_pairs),
                (w_out_ref, w_down),
                (queries_ref, q_ref),
            )
        )
    ]
    for each in loads:
        each.start()

    barrier = pltpu.get_barrier_semaphore()
    for other in (mate, across, corner):
        pl.semaphore_signal(
            barrier, inc=1, device_id={"head": other}, device_id_type=pl.DeviceIdType.MESH
        )
    for distance in distances[1:]:
        other = ring_index((place + distance + count) % count, count)
        pl.semaphore_signal(
            barrier, inc=1, device_id={"exp": other}, device_id_type=pl.DeviceIdType.MESH
        )

    for each in loads[:5]:
        each.wait()
    expert_row = lax.broadcasted_iota(jnp.int32, (experts, tokens), 0)
    table = jnp.zeros((experts, tokens), jnp.float32)
    for k in range(routes_ref.shape[0]):
        table = table + jnp.where(expert_row == routes_ref[k : k + 1, :], share_ref[k : k + 1, :], 0.0)
    tables[0] = table
    pl.semaphore_wait(barrier, 3 + count - 1)

    def advance(step):
        if step >= 1:
            both = kv_all.at[0] if step == reach else kv_all.at[pl.ds(0, 2)]
            remote(both, both, 0, early_recv.at[step - 1], {"head": mate}).wait_recv()
        for way in range(2 if step < reach else 0):
            sign = -1 if way == 0 else 1
            here, there = slot_of(sign * step, count), slot_of(sign * (step + 1), count)
            halved = step == reach - 1
            begin(
                kv_all.at[here, way] if halved else kv_all.at[here],
                kv_all.at[there, way] if halved else kv_all.at[there],
                0,
                early_recv.at[step],
                {"exp": others[way]},
            )

    def advance_wave(kind, wave, step, pairs_of=(0, 1)):
        store = rows if kind else grads
        for pair in pairs_of:
            steps, first = lanes[pair]
            if 1 <= step <= steps:
                both = store.at[wave, pl.ds(0, half)]
                arrived = wave_recv.at[kind, wave, first + step - 1]
                remote(both, both, 0, arrived, {"head": mate}).wait_recv()
            for way in range(2 if step < steps else 0):
                sub = way if pair == 0 else 1 - way
                sign = -1 if way == 0 else 1
                there = slot_of(sign * (step + 1), count) * half + sub * quarter
                here = slot_of(sign * step, count) * half + sub * quarter
                begin(
                    store.at[wave, pl.ds(here, quarter)],
                    store.at[wave, pl.ds(there, quarter)],
                    1 + 2 * kind + wave,
                    wave_recv.at[kind, wave, first + step],
                    {"exp": others[way]},
                )

    def broadcast(kind, store):
        for distance in distances[1:]:
            there = slot_of(-distance, count)
            other = ring_index((place + distance + count) % count, count)
            begin(store.at[0], store.at[there], 7 + kind, meta_recv.at[kind], {"exp": other})
        others_of = store.at[pl.ds(1, count - 1)]
        return remote(others_of, others_of, 7 + kind, meta_recv.at[kind], {"head": mate})

    def split():
        loads[5].wait()
        chunk = LANES
        to = lax.broadcasted_iota(jnp.int32, (2 * chunk, 2 * chunk), 0)
        source = lax.broadcasted_iota(jnp.int32, (2 * chunk, 2 * chunk), 1)
        picks = (source == jnp.where(to < chunk, 2 * to, 2 * to - 2 * chunk + 1)).astype(jnp.bfloat16)

        def split_chunk(index, carry):
            span = pl.ds(pl.multiple_of(index * chunk, chunk), chunk)
            pairs = w_pairs[span].reshape(2 * chunk, 2 * side)
            apart = jnp.dot(picks, pairs, preferred_element_type=jnp.float32).astype(jnp.bfloat16)
            for part in range(2):
                cols = slice(part * side, (part + 1) * side)
                w_up[part, span, :side] = apart[:chunk, cols]
                w_up[part, span, side:] = apart[chunk:, cols]
            return carry

        lax.fori_loop(0, width // chunk, split_chunk, 0)
        loads[6].wait()
        loads[7].wait()

    pairs = {}

    def pair_begin(kind, wave, slot, blocks, source, target, other):
        span = pl.ds(slot * half, blocks * half)
        pairs[kind, wave, slot] = begin(
            source.at[wave, span],
            target.at[wave, span],
            9 + kind,
            pair_recv.at[len(pairs)],
            {"head": other},
        )

    def back(wave, slot, blocks):
        span = slice(slot * half, (slot + blocks) * half)
        weights = jnp.concatenate([w_down[1 - core], w_down[core]], axis=0)
        both = lax.dot_general(
            grads[wave, span, :], weights, EXACT, preferred_element_type=jnp.float32
        )
        near_back[wave, span, :] = both[:, :side].astype(jnp.bfloat16)
        pair_begin(0, wave, slot, blocks, near_back, near_back_in, mate)
        sum_back[wave, span, :] = both[:, side:]

    def raw(wave, slot, blocks):
        span = slice(slot * half, (slot + blocks) * half)
        block = rows[wave, span, :]
        near_raw[wave, span, :] = jnp.dot(
            block, w_up[1 - core], preferred_element_type=jnp.float32
        ).astype(jnp.bfloat16)
        pair_begin(1, wave, slot, blocks, near_raw, near_raw_in, mate)
        sum_raw[wave, span, :] = jnp.dot(block, w_up[core], preferred_element_type=jnp.float32)

    def far(kind, wave, slot, blocks):
        total, near_in = ((sum_back, near_back_in), (sum_raw, near_raw_in))[kind]
        out, target = ((far_back, far_back_in), (far_raw, far_raw_in))[kind]
        span = slice(slot * half, (slot + blocks) * half)
        pairs[kind, wave, slot].wait_recv()
        both = total[wave, span, :] + near_in[wave, span, :].astype(jnp.float32)
        total[wave, span, :] = both
        out[wave, span, :] = both.astype(jnp.bfloat16)
        pair_begin(2 + kind, wave, slot, blocks, out, target, across)

    groups = kv_width // HEAD_WIDTH
    together = width // kv_width

    def visible_in(low, high):
        size = (high - low) * cached
        column = low * cached + lax.broadcasted_iota(jnp.int32, (1, size), 1)
        shift = jnp.zeros((1, size), jnp.int32)
        for slot in range(low, high):
            owner = ring_index((place + distances[slot] + count) % count, count)
            shift = jnp.where(column // cached == slot, (owner - slot) * cached, shift)
        row_pos = (
            count * (cached - tokens)
            + me * tokens
            + lax.broadcasted_iota(jnp.int32, (tokens, size), 0)
        )
        row_pos = jnp.concatenate([row_pos] * together, axis=0)
        return jnp.broadcast_to(shift + column, row_pos.shape) <= row_pos

    def scores_in(group, low, high, visible):
        first_head = group * together
        stacked = jnp.concatenate(
            [
                q_ref[:, one * HEAD_WIDTH : (one + 1) * HEAD_WIDTH]
                for one in range(first_head, first_head + together)
            ],
            axis=0,
        )
        scores = lax.dot_general(
            stacked,
            kv_all[low:high, 0, :, group * HEAD_WIDTH : (group + 1) * HEAD_WIDTH].reshape(
                (high - low) * cached, HEAD_WIDTH
            ),
            EXACT,
            preferred_element_type=jnp.float32,
        ) * HEAD_WIDTH ** (-0.5)
        return jnp.where(visible, scores, hidden_logits)

    def values_in(group, low, high, weights):
        return jnp.dot(
            weights.astype(jnp.bfloat16),
            kv_all[low:high, 1, :, group * HEAD_WIDTH : (group + 1) * HEAD_WIDTH].reshape(
                (high - low) * cached, HEAD_WIDTH
            ),
            preferred_element_type=jnp.float32,
        )

    def attend_most():
        visible = visible_in(0, count - 1)
        for group in range(groups):
            scores = scores_in(group, 0, count - 1, visible)
            best = jnp.max(scores, axis=1, keepdims=True)
            weights = jnp.exp(scores - best)
            total = jnp.sum(weights, axis=1, keepdims=True)
            best_so_far[group] = jnp.broadcast_to(best, (together * tokens, HEAD_WIDTH))
            total_so_far[group] = jnp.broadcast_to(total, (together * tokens, HEAD_WIDTH))
            mix_so_far[group] = values_in(group, 0, count - 1, weights)

    def attention():
        visible = visible_in(count - 1, count)
        squared = jnp.zeros((tokens, LANES), jnp.float32)
        for group in range(groups):
            scores = scores_in(group, count - 1, count, visible)
            before = best_so_far[group]
            best = jnp.maximum(before, jnp.max(scores, axis=1, keepdims=True))
            weights = jnp.exp(scores - best[:, :1])
            factor = jnp.exp(before - best)
            total = total_so_far[group] * factor + jnp.sum(weights, axis=1, keepdims=True)
            mixed = mix_so_far[group] * factor + values_in(group, count - 1, count, weights)
            mixed = (mixed / total).astype(jnp.bfloat16)
            for one in range(together):
                start = (group * together + one) * HEAD_WIDTH
                cols = slice(start, start + HEAD_WIDTH)
                part = mixed[one * tokens : (one + 1) * tokens]
                rows[0, 0:half, cols] = part[:half]
                rows[1, 0:half, cols] = part[half:]
                part = part.astype(jnp.float32)
                squared = squared + part * part
        return squared

    def share_squares(total):
        columns = jnp.broadcast_to(jnp.sum(total, axis=1, keepdims=True), (tokens, LANES))
        head_squares[0] = jnp.transpose(columns)[: head_squares.shape[1]]
        for index, other in enumerate((mate, across, corner)):
            begin(
                head_squares.at[0],
                head_squares.at[index + 1],
                14,
                head_recv.at[0],
                {"head": other},
            )

    def spread_squares():
        others_of = head_squares.at[pl.ds(1, 3)]
        remote(others_of, others_of, 14, head_recv.at[0], {"head": mate}).wait_recv()
        squares[0] = (head_squares[0] + head_squares[1]) + (head_squares[2] + head_squares[3])
        return broadcast(1, squares)

    def fill(store, slot, row):
        columns = jnp.transpose(jnp.broadcast_to(row, (LANES, tokens)))
        for wave in range(2):
            store[wave, slot * half : (slot + 1) * half, :] = columns[wave * half : (wave + 1) * half]

    def fill_gains(copies):
        copies.wait_recv()
        for slot in range(count):
            row = jnp.sum(jnp.where(expert_row == me, tables[slot], 0.0), axis=0, keepdims=True)
            fill(gains, slot, row)

    def fill_scales(copies):
        copies.wait_recv()
        for slot in range(count):
            fill(scales, slot, lax.rsqrt(squares[slot][0:1, :] / D + norm_eps))

    def activate(wave, slot, blocks):
        for kind in (2, 3):
            for one in range(slot, slot + blocks):
                if (kind, wave, one) in pairs:
                    pairs[kind, wave, one].wait_recv()
        step = 32
        lane = lax.broadcasted_iota(jnp.int32, (step, LANES), 1)

        def some_rows(index, carry):
            span = pl.ds(pl.multiple_of(slot * half + index * step, step), step)
            scale = scales[wave, span, :]
            gain = gains[wave, span, :]
            inner = jnp.zeros((step, LANES), jnp.float32)
            for start in range(0, side, LANES):
                cols = slice(start, start + LANES)
                up_cols = slice(side + start, side + start + LANES)
                down_cols = slice(2 * side + start, 2 * side + start + LANES)
                gate = sum_raw[wave, span, cols] + far_raw_in[wave, span, cols].astype(jnp.float32)
                up = sum_raw[wave, span, up_cols] + far_raw_in[wave, span, up_cols].astype(
                    jnp.float32
                )
                gate, up = gate * scale, up * scale
                back_value = sum_back[wave, span, cols] + far_back_in[wave, span, cols].astype(
                    jnp.float32
                )
                sigmoid = jax.nn.sigmoid(gate)
                silu = gate * sigmoid
                grad_gate = back_value * up * sigmoid * (1.0 + gate * (1.0 - sigmoid))
                grad_up = back_value * silu
                inner = inner + (grad_gate * gate + grad_up * up)
                act[wave, span, cols] = (gain * (silu * up)).astype(jnp.bfloat16)
                act[wave, span, up_cols] = (gain * scale * grad_gate).astype(jnp.bfloat16)
                act[wave, span, down_cols] = (gain * scale * grad_up).astype(jnp.bfloat16)
            high, middle, low = three_parts(
                jnp.broadcast_to(jnp.sum(inner, axis=1, keepdims=True), (step, LANES))
            )
            zero = jnp.zeros((step, LANES), jnp.float32)
            spread = jnp.where(lane == 0, high.astype(jnp.float32), zero)
            spread = jnp.where(lane == 1, middle.astype(jnp.float32), spread)
            spread = jnp.where(lane == 2, low.astype(jnp.float32), spread)
            act[wave, span, 3 * side :] = spread.astype(jnp.bfloat16)
            return carry

        lax.fori_loop(0, blocks * half // step, some_rows, 0)
        pair_begin(4, wave, slot, blocks, act, act_in, mate)

    def finish(wave, slot, blocks):
        span = slice(slot * half, (slot + blocks) * half)
        pairs[4, wave, slot].wait_recv()
        inner = jnp.sum(
            act[wave, span, 3 * side :].astype(jnp.float32)
            + act_in[wave, span, 3 * side :].astype(jnp.float32),
            axis=1,
            keepdims=True,
        )
        tile = 256
        scale = scales[wave, span, :]
        bent = wide(gains[wave, span, :] * (scale * scale / D) * inner, tile)
        hidden = slice(0, side)
        slopes = slice(side, 3 * side)
        act_all = jnp.concatenate([act[wave, span, hidden], act_in[wave, span, hidden]], axis=1)
        for start in range(0, width, tile):
            cols = slice(start, start + tile)
            weights = jnp.concatenate([w_down[core, :, cols], w_down[1 - core, :, cols]], axis=0)
            out = jnp.dot(act_all, weights, preferred_element_type=jnp.float32)
            parts[wave, span, cols] = out.astype(jnp.bfloat16)
            grad = lax.dot_general(
                act[wave, span, slopes],
                w_up[core, cols, :],
                EXACT,
                preferred_element_type=jnp.float32,
            ) + lax.dot_general(
                act_in[wave, span, slopes],
                w_up[1 - core, cols, :],
                EXACT,
                preferred_element_type=jnp.float32,
            )
            grad = grad - bent * rows[wave, span, cols].astype(jnp.float32)
            parts[wave, span, width + start : width + start + tile] = grad.astype(jnp.bfloat16)

    def arrived(wave, pair, step):
        both = parts.at[wave, pl.ds(0, half)]
        where = scatter_recv.at[wave, lanes[pair][1] + step]
        remote(both, both, 0, where, {"head": mate}).wait_recv()

    def scatter(wave, step, pairs_of=(0, 1)):
        for pair, (steps, first) in enumerate(lanes):
            if step >= steps or pair not in pairs_of:
                continue
            if step > 0:
                arrived(wave, pair, step - 1)
            for way in range(2):
                sub = way if pair == 0 else 1 - way
                sign = 1 if way == 0 else -1
                start = slot_of(sign * (steps - step), count) * half + sub * quarter
                block = parts.at[wave, pl.ds(start, quarter)]
                there = pl.ds(sub * quarter, quarter)
                if step > 0:
                    sum_ref = held.at[wave, way, step - 1, there]
                    sum_ref[...] = (
                        sum_ref[...].astype(jnp.float32) + block[...].astype(jnp.float32)
                    ).astype(jnp.bfloat16)
                    block = sum_ref
                begin(
                    block,
                    held.at[wave, way, step, there],
                    5 + wave,
                    scatter_recv.at[wave, first + step],
                    {"exp": others[way]},
                )

    def settle(wave):
        sides = ((rows, slice(0, width)), (grads, slice(width, 2 * width)))
        arrived(wave, 1, reach - 2)
        for sub in range(2):
            span = slice(sub * quarter, (sub + 1) * quarter)
            for base, cols in sides:
                settled[span, cols] = base[wave, span, :].astype(jnp.float32) + (
                    parts[wave, span, cols].astype(jnp.float32)
                    + held[wave, 1 - sub, reach - 2, span, cols].astype(jnp.float32)
                )
        arrived(wave, 0, reach - 1)
        for sub in range(2):
            span = slice(sub * quarter, (sub + 1) * quarter)
            for index, (base, cols) in enumerate(sides):
                start = index * tokens + wave * half + sub * quarter
                results_ref[start : start + quarter, :] = (
                    settled[span, cols] + held[wave, sub, reach - 1, span, cols].astype(jnp.float32)
                ).astype(jnp.bfloat16)

    def drain():
        others_of = pl.ds(half, (count - 1) * half)
        for kind, sent in enumerate(
            (
                kv_all.at[pl.ds(1, count - 1)],
                grads.at[0, others_of],
                grads.at[1, others_of],
                rows.at[0, others_of],
                rows.at[1, others_of],
                parts.at[0, others_of],
                parts.at[1, others_of],
                tables.at[pl.ds(1, count - 1)],
                squares.at[pl.ds(1, count - 1)],
                near_back,
                near_raw,
                far_back,
                far_raw,
                act,
                head_squares.at[pl.ds(1, 3)],
            )
        ):
            remote(sent, sent, kind, head_recv.at[0], {"head": mate}).wait_send()

    first = (0, 3)
    between = [(2 * step - 1, 2) for step in range(2, reach - 1)]
    last = (2 * reach - 3, 3)
    advance(0)
    advance_wave(0, 0, 0)
    table_copies = broadcast(0, tables)
    split()
    advance(1)
    advance_wave(0, 0, 1)
    back(0, *first)
    advance(2)
    far(0, 0, *first)
    advance_wave(0, 0, 2)
    for step in range(3, reach):
        back(0, *between[step - 3])
        advance(step)
        far(0, 0, *between[step - 3])
        if step == reach - 1:
            attend_most()
        advance_wave(0, 0, step)
    back(0, count - 3, 2)
    advance(reach)
    advance_wave(0, 1, 0, (0,))
    square_total = attention()
    advance_wave(1, 0, 0)
    share_squares(square_total)
    far(0, 0, count - 3, 2)
    advance_wave(0, 0, reach)
    back(0, count - 1, 1)
    advance_wave(0, 1, 1, (0,))
    raw(0, 0, 1)
    far(0, 0, count - 1, 1)
    square_copies = spread_squares()
    far(1, 0, 0, 1)
    advance_wave(1, 0, 1)
    raw(0, 1, 2)
    advance_wave(0, 1, 2, (0,))
    far(1, 0, 1, 2)
    advance_wave(1, 0, 2)
    advance_wave(0, 1, 0, (1,))
    for unit in between[:1]:
        raw(0, *unit)
    for unit in between[:1]:
        far(1, 0, *unit)
    for step in range(3, reach):
        advance_wave(1, 0, step)
        if step == reach - 1:
            advance_wave(1, 1, 0)
        raw(0, 2 * step - 1, 2)
    for step in range(3, reach):
        far(1, 0, 2 * step - 1, 2)
    advance_wave(0, 1, 1, (1,))
    advance_wave(1, 0, reach)
    raw(0, count - 1, 1)
    fill_gains(table_copies)
    far(1, 0, count - 1, 1)
    fill_scales(square_copies)
    advance_wave(1, 1, 1)
    advance_wave(0, 1, 3, (0,))
    raw(1, *first)
    activate(0, *first)
    far(1, 1, *first)
    advance_wave(0, 1, 2, (1,))
    back(1, *first)
    advance_wave(1, 1, 2)
    far(0, 1, *first)
    activate(0, *last)
    for unit in between:
        activate(0, *unit)
    finish(0, *last)
    for step in range(3, reach):
        advance_wave(0, 1, step, (1,))
    for step in range(3, reach):
        advance_wave(1, 1, step)
    scatter(0, 0)
    for unit in between:
        finish(0, *unit)
    advance_wave(0, 1, reach)
    back(1, *last)
    for unit in between:
        back(1, *unit)
    far(0, 1, *last)
    advance_wave(1, 1, reach)
    raw(1, *last)
    scatter(0, 1, (0,))
    far(1, 1, *last)
    finish(0, *first)
    activate(1, *first)
    scatter(0, 1, (1,))
    for unit in between:
        raw(1, *unit)
        far(0, 1, *unit)
    finish(1, *first)
    for unit in between:
        far(1, 1, *unit)
    scatter(0, 2)
    activate(1, *last)
    for step in range(3, reach):
        scatter(0, step)
    finish(1, *last)
    scatter(1, 0)
    for unit in between:
        activate(1, *unit)
        finish(1, *unit)
    settle(0)
    for step in range(1, reach):
        scatter(1, step)
    settle(1)
    drain()


def fused_device(queries, keys, values, w_in, w_out, routes, route_weights, grad_out):
    count = lax.axis_size("exp")
    tokens, width = queries.shape
    cached, kv_width = keys.shape
    hidden = w_in.shape[3]
    side = hidden // 2
    reach = count // 2
    half_rows = tokens // 2
    every = count * half_rows
    experts = w_in.shape[0] * count
    stacked = (kv_width // HEAD_WIDTH, width // kv_width * tokens, HEAD_WIDTH)

    def body(*refs):
        fused_kernel(count, *refs)

    def half(*shape):
        return pltpu.VMEM(shape, jnp.bfloat16)

    def whole(*shape):
        return pltpu.VMEM(shape, jnp.float32)

    dma = pltpu.SemaphoreType.DMA
    vmem = pl.BlockSpec(memory_space=pltpu.VMEM)
    anywhere = pl.BlockSpec(memory_space=pl.ANY)
    both = pl.pallas_call(
        body,
        out_shape=jax.ShapeDtypeStruct((2 * tokens, width), jnp.bfloat16),
        in_specs=[anywhere] * 8,
        out_specs=vmem,
        scratch_shapes=[
            half(tokens, width),
            pltpu.VMEM(routes.shape[::-1], routes.dtype),
            whole(*route_weights.shape[::-1]),
            half(width, 2, hidden),
            half(2, width, hidden),
            half(2, side, width),
            half(count, 2, cached, kv_width),
            half(2, every, width),
            half(2, every, width),
            whole(count, experts, tokens),
            whole(count, 8, tokens),
            whole(4, 8, tokens),
            whole(2, every, LANES),
            whole(2, every, LANES),
            whole(2, every, hidden),
            whole(2, every, side),
            half(2, every, hidden),
            half(2, every, side),
            half(2, every, hidden),
            half(2, every, side),
            half(2, every, hidden),
            half(2, every, side),
            half(2, every, hidden),
            half(2, every, side),
            half(2, every, 3 * side + LANES),
            half(2, every, 3 * side + LANES),
            half(2, every, 2 * width),
            half(2, 2, reach, half_rows, 2 * width),
            whole(half_rows, 2 * width),
            whole(*stacked),
            whole(*stacked),
            whole(*stacked),
            dma((8,)),
            dma((15,)),
            dma((reach,)),
            dma((2, 2, 2 * reach - 1)),
            dma((2, 2 * reach - 1)),
            dma((2,)),
            dma((1,)),
            dma((5 * 2 * (reach - 1) + 6,)),
        ],
        compiler_params=pltpu.CompilerParams(
            collective_id=1, has_side_effects=True, vmem_limit_bytes=60 * 1024 * 1024
        ),
        name="fused",
    )(
        queries,
        keys,
        values,
        w_in,
        w_out[0].reshape(2, side, width),
        routes.T,
        route_weights.T,
        grad_out.reshape(2, half_rows, width),
    )
    return both[:tokens], both[tokens:]


def solution(mesh):
    fused = 2 * TOP >= mesh.shape["exp"] and mesh.shape["exp"] == 8 and mesh.shape["head"] == 4
    in_specs = (
        P("exp", "head"),
        P("exp", "head"),
        P("exp", "head"),
        P("exp", "head", None, None),
        P("exp", None, "head"),
        P("exp", None),
        P("exp", None),
        P("exp", "head"),
    )
    out_specs = (P("exp", "head"), P("exp", "head"))
    return jax.shard_map(
        fused_device if fused else per_device, mesh=mesh, in_specs=in_specs, out_specs=out_specs, check_vma=False
    )
```
